256 devices in a mesh: row: 8 (over y, core), col: 32 (over z, x).
Axes of the slice: x: 4, y: 4, z: 8, core: 2. Of those that a mesh axis runs over, the one named last changes fastest.
Arguments:
- fields: float32 [4096, 5, 4096], P(('row', 'col')), as said below
- counts: int32 [8, 32], P('row', 'col'), may hold values from 1 to 16, 256 in all within a row
Outputs:
- fields_out: float32 [4096, 5, 4096], P(('row', 'col'))
The draws below stay inside these ranges and needn't reach their ends.
Inputs may be any that keep to these rules, and one draw needn't show every extreme that they name: `fields`: in every slot, also those that hold no patch, density lies in 0.5 to 3, pressure 0.4 (E - |m|^2 / (2 rho)) in 0.5 to 2 and each velocity component in -0.5 to 0.5. Each index of row holds 256 patches in all: the entries of counts[r] sum to 256, and some device of each index of row holds 16.
All inputs are finite; a program needn't handle non-finite values.
Results may differ from the reference program's by a relative error of at most 0.0003.
Values sent between devices are 32-bit elements; how exact they have to be, the bound alone decides.
No kernel may reach another device: no remote copies, remote signals or barrier semaphores. Data moves between devices by JAX's collectives and lax.ppermute only.
A program may use at most 128 MiB of HBM per device.

```python
import math
import jax
import jax.numpy as jnp
import numpy as np
from jax import lax

PE = 16
GX = 256
GY = 256
GZ = 128
LXR = 2
LY = 16
LZ = 8
PPR = 256
CAP = 16
SLOTS = 4096
CELLS = 4096
N_ROW = 8
N_COL = 32


def draw_fields(key, part):
    subkeys = jax.random.split(key, 3)
    slot_shape = (SLOTS, CELLS)
    density = jnp.exp(jax.random.uniform(subkeys[0], slot_shape, minval=math.log(0.5), maxval=math.log(2.0)))
    velocity = jax.random.uniform(subkeys[1], (3,) + slot_shape, minval=-0.5, maxval=0.5)
    pressure = jnp.exp(jax.random.uniform(subkeys[2], slot_shape, minval=math.log(0.5), maxval=math.log(2.0)))
    momenta = density[None] * velocity
    speed_sq = velocity[0] * velocity[0] + velocity[1] * velocity[1] + velocity[2] * velocity[2]
    energy = pressure / 0.4 + 0.5 * density * speed_sq
    return jnp.stack([density, momenta[0], momenta[1], momenta[2], energy], axis=1).astype(jnp.float32)


def split_up(count, total, reach, slope):
    weights = [(1 << 20) // math.isqrt(grade ** slope) + 1 for grade in range(2, count + 1)]
    spare, holding = total - reach - (count - 1), [1] * (count - 1)
    while spare > 0:
        movable = [i for i in range(count - 1) if holding[i] < reach]
        mass, remaining = sum([weights[i] for i in movable]), spare
        for i in movable:
            more = min(reach - holding[i], max(1, remaining * weights[i] // mass), spare)
            holding[i] = holding[i] + more
            spare = spare - more
    return np.array([reach] + holding)


def uneven_parts(key, number_of, total, most, slope):
    if number_of == 2:
        one = jax.random.randint(key, (), max(1, total - most), min(most, total - 1) + 1)
        return jnp.stack([one, total - one])
    sizes = jnp.asarray(split_up(number_of, total, most, slope), jnp.int32)
    twos = (number_of - 1) // 2
    source_of, receiver = sizes[1:1 + 2 * twos:2], sizes[2:2 + 2 * twos:2]
    slack = jnp.minimum(source_of - 1, most - receiver)
    shifted = jax.random.randint(jax.random.fold_in(key, 1), (twos,), 0, 1 << 20) % (slack + 1)
    sizes = sizes.at[1:1 + 2 * twos:2].set(source_of - shifted).at[2:2 + 2 * twos:2].set(receiver + shifted)
    return sizes[jax.random.permutation(jax.random.fold_in(key, 2), number_of)]


def setup_inputs(seed: int = 0) -> dict:
    seeds = jax.random.split(jax.random.key(seed), 3)
    return {
        "fields": draw_fields(jax.random.fold_in(seeds[2], 71), 0),
        "counts": jax.vmap(lambda own: uneven_parts(own, N_COL, PPR, CAP, 2))(jax.random.split(seeds[1], N_ROW)).reshape((N_ROW, N_COL)).astype(jnp.int32),
    }


gamma_gas = 1.4
speed_bound = 4.0
time_step = 0.03
four_pi_g = 10.0


def minmod_slope(lower_gap, upper_gap):
    return 0.5 * (jnp.sign(lower_gap) + jnp.sign(upper_gap)) * jnp.minimum(jnp.abs(lower_gap), jnp.abs(upper_gap))


def normal_flux(states, direction):
    density = states[0]
    momenta = states[1:4]
    energy = states[4]
    velocity = momenta[direction] / density
    kinetic = 0.5 * (momenta[0] * momenta[0] + momenta[1] * momenta[1] + momenta[2] * momenta[2]) / density
    pressure = (gamma_gas - 1.0) * (energy - kinetic)
    pieces = [momenta[direction]]
    for component in range(3):
        flux_term = momenta[component] * velocity
        if component == direction:
            flux_term = flux_term + pressure
        pieces.append(flux_term)
    pieces.append((energy + pressure) * velocity)
    return jnp.stack(pieces)


def cut_range(array, dim_index, first_cell, count_cells):
    return lax.slice_in_dim(array, first_cell, first_cell + count_cells, axis=dim_index)


def face_rates(states):
    total_rate = None
    for direction in range(3):
        dim_index = direction + 1
        trimmed = states
        for other_dim in range(1, 4):
            if other_dim != dim_index:
                trimmed = cut_range(trimmed, other_dim, 2, trimmed.shape[other_dim] - 4)
        length = trimmed.shape[dim_index]
        lower_cell = cut_range(trimmed, dim_index, 0, length - 3)
        centre = cut_range(trimmed, dim_index, 1, length - 3)
        upper_cell = cut_range(trimmed, dim_index, 2, length - 3)
        far_cell = cut_range(trimmed, dim_index, 3, length - 3)
        left_state = centre + 0.5 * minmod_slope(centre - lower_cell, upper_cell - centre)
        right_state = upper_cell - 0.5 * minmod_slope(upper_cell - centre, far_cell - upper_cell)
        face_flux = 0.5 * (normal_flux(left_state, direction) + normal_flux(right_state, direction)) - 0.5 * speed_bound * (right_state - left_state)
        change = cut_range(face_flux, dim_index, 1, length - 4) - cut_range(face_flux, dim_index, 0, length - 4)
        total_rate = change if total_rate is None else total_rate + change
    return -total_rate


def crop_all(array, margin):
    return array[:, margin:array.shape[1] - margin, margin:array.shape[2] - margin, margin:array.shape[3] - margin]


def advance(extended):
    first = crop_all(extended, 2) + time_step * face_rates(extended)
    second = crop_all(first, 2) + time_step * face_rates(first)
    return 0.5 * crop_all(extended, 4) + 0.5 * second


def lap_eigen(wave, length):
    return 2.0 * jnp.cos((2.0 * math.pi / length) * wave) - 2.0


def apply_kick(stepped, gradient):
    density = stepped[0]
    momenta = stepped[1:4]
    new_momenta = momenta - time_step * density[None] * gradient
    work_done = momenta[0] * gradient[0] + momenta[1] * gradient[1] + momenta[2] * gradient[2]
    new_energy = stepped[4] - time_step * work_done
    return jnp.concatenate([stepped[0:1], new_momenta, new_energy[None]], axis=0)


def reference(fields, counts):
    counts = counts.astype(jnp.int32)
    starts = (jnp.cumsum(counts, axis=1) - counts).astype(jnp.int32)
    positions = jnp.arange(PPR, dtype=jnp.int32)
    owners = (jnp.sum((starts[:, None, :] <= positions[None, :, None]).astype(jnp.int32), axis=2) - 1).astype(jnp.int32)
    owner_start = jnp.take_along_axis(starts, owners, axis=1).astype(jnp.int32)
    row_ids = jnp.arange(N_ROW, dtype=jnp.int32)
    slot_rows = ((row_ids[:, None] * N_COL + owners) * CAP + positions[None, :] - owner_start).astype(jnp.int32)
    patches = jnp.take(fields, slot_rows.reshape(-1), axis=0)
    state = patches.reshape(N_ROW, LXR, LZ, LY, 5, PE, PE, PE).transpose(4, 0, 1, 5, 3, 6, 2, 7).reshape(5, GX, GY, GZ)

    padded = jnp.pad(state, ((0, 0), (4, 4), (4, 4), (4, 4)), mode="wrap")
    slab_width = GX // N_ROW

    def one_slab(slab_index):
        slab_piece = lax.dynamic_slice_in_dim(padded, slab_index * slab_width, slab_width + 8, axis=1)
        return advance(slab_piece)

    slab_results = lax.map(one_slab, jnp.arange(N_ROW, dtype=jnp.int32))
    stepped = jnp.moveaxis(slab_results, 0, 1).reshape(5, GX, GY, GZ)

    spectrum = jnp.fft.fftn(stepped[0])
    wave_x = jnp.arange(GX, dtype=jnp.float32)
    wave_y = jnp.arange(GY, dtype=jnp.float32)
    wave_z = jnp.arange(GZ, dtype=jnp.float32)
    eigen = (lap_eigen(wave_x, GX)[:, None, None] + lap_eigen(wave_y, GY)[None, :, None]) + lap_eigen(wave_z, GZ)[None, None, :]
    zero_mode = (wave_x == 0.0)[:, None, None] & (wave_y == 0.0)[None, :, None] & (wave_z == 0.0)[None, None, :]
    green = jnp.where(zero_mode, 0.0, four_pi_g / jnp.where(zero_mode, -1.0, eigen))
    potential = jnp.real(jnp.fft.ifftn(spectrum * green))
    gradient = jnp.stack([0.5 * (jnp.roll(potential, -1, direction) - jnp.roll(potential, 1, direction)) for direction in range(3)])
    kicked = apply_kick(stepped, gradient)

    out_patches = kicked.reshape(5, N_ROW, LXR, PE, LY, PE, LZ, PE).transpose(1, 2, 6, 4, 0, 3, 5, 7).reshape(N_ROW * PPR, 5, CELLS)
    slot_ids = jnp.arange(SLOTS, dtype=jnp.int32)
    row_of = (slot_ids // (N_COL * CAP)).astype(jnp.int32)
    col_of = ((slot_ids // CAP) % N_COL).astype(jnp.int32)
    within = (slot_ids % CAP).astype(jnp.int32)
    slot_counts = counts[row_of, col_of]
    slot_starts = starts[row_of, col_of]
    live = within < slot_counts
    source = (row_of * PPR + jnp.where(live, slot_starts + within, 0)).astype(jnp.int32)
    return jnp.where(live[:, None, None], jnp.take(out_patches, source, axis=0), 0.0)
```

```python
import math

import jax
import jax.numpy as jnp
from jax import lax
from jax.sharding import PartitionSpec as P

PE = 16
GX = 256
GY = 256
GZ = 128


gamma_gas = 1.4
speed_bound = 4.0
time_step = 0.03
four_pi_g = 10.0


def padded(block, sides, width):
    for axis, dim in sides:
        count = lax.axis_size(axis)
        forward = [(i, i + 1) for i in range(count - 1)]
        forward.append((count - 1, 0))
        backward = [(target, source) for source, target in forward]
        low = lax.ppermute(
            lax.slice_in_dim(block, block.shape[dim] - width, None, axis=dim), axis, forward
        )
        high = lax.ppermute(lax.slice_in_dim(block, 0, width, axis=dim), axis, backward)
        block = jnp.concatenate([low, block, high], axis=dim)
    return block


def minmod_slope(lower_gap, upper_gap):
    return (
        0.5
        * (jnp.sign(lower_gap) + jnp.sign(upper_gap))
        * jnp.minimum(jnp.abs(lower_gap), jnp.abs(upper_gap))
    )


def normal_flux(states, direction):
    density = states[0]
    momenta = states[1:4]
    energy = states[4]
    velocity = momenta[direction] / density
    kinetic = (
        0.5
        * (momenta[0] * momenta[0] + momenta[1] * momenta[1] + momenta[2] * momenta[2])
        / density
    )
    pressure = (gamma_gas - 1.0) * (energy - kinetic)
    pieces = [momenta[direction]]
    for component in range(3):
        flux_term = momenta[component] * velocity
        if component == direction:
            flux_term = flux_term + pressure
        pieces.append(flux_term)
    pieces.append((energy + pressure) * velocity)
    return jnp.stack(pieces)


def cut_range(array, dim_index, first_cell, count_cells):
    return lax.slice_in_dim(array, first_cell, first_cell + count_cells, axis=dim_index)


def face_rates(states):
    total_rate = None
    for direction in range(3):
        dim_index = direction + 1
        trimmed = states
        for other_dim in (1, 2):
            if other_dim != dim_index:
                trimmed = cut_range(trimmed, other_dim, 2, trimmed.shape[other_dim] - 4)
        if direction < 2:
            length = trimmed.shape[dim_index]
            lower_cell = cut_range(trimmed, dim_index, 0, length - 3)
            centre = cut_range(trimmed, dim_index, 1, length - 3)
            upper_cell = cut_range(trimmed, dim_index, 2, length - 3)
            far_cell = cut_range(trimmed, dim_index, 3, length - 3)
        else:
            lower_cell = jnp.roll(trimmed, 1, 3)
            centre = trimmed
            upper_cell = jnp.roll(trimmed, -1, 3)
            far_cell = jnp.roll(trimmed, -2, 3)
        left_state = centre + 0.5 * minmod_slope(centre - lower_cell, upper_cell - centre)
        right_state = upper_cell - 0.5 * minmod_slope(upper_cell - centre, far_cell - upper_cell)
        face_flux = 0.5 * (
            normal_flux(left_state, direction) + normal_flux(right_state, direction)
        ) - 0.5 * speed_bound * (right_state - left_state)
        if direction < 2:
            change = cut_range(face_flux, dim_index, 1, length - 4) - cut_range(
                face_flux, dim_index, 0, length - 4
            )
        else:
            change = face_flux - jnp.roll(face_flux, 1, 3)
        total_rate = change if total_rate is None else total_rate + change
    return -total_rate


def crop_plane(array, margin):
    return array[:, margin : array.shape[1] - margin, margin : array.shape[2] - margin, :]


def advance(extended):
    first = crop_plane(extended, 2) + time_step * face_rates(extended)
    second = crop_plane(first, 2) + time_step * face_rates(first)
    return 0.5 * crop_plane(extended, 4) + 0.5 * second


def lap_eigen(wave, length):
    return 2.0 * jnp.cos(2.0 * math.pi / length * wave) - 2.0


def apply_kick(stepped, gradient):
    density = stepped[0]
    momenta = stepped[1:4]
    new_momenta = momenta - time_step * density[None] * gradient
    work_done = momenta[0] * gradient[0] + momenta[1] * gradient[1] + momenta[2] * gradient[2]
    new_energy = stepped[4] - time_step * work_done
    return jnp.concatenate([stepped[0:1], new_momenta, new_energy[None]], axis=0)


def dft_tables(length):
    indices = jnp.arange(length, dtype=jnp.int32)
    wrapped = indices[:, None] * indices[None, :] % length
    angles = 2.0 * math.pi / length * wrapped.astype(jnp.float32)
    return (jnp.cos(angles), jnp.sin(angles))


def right_mul(values, matrix):
    return jnp.matmul(values, matrix, precision=lax.Precision.HIGHEST)


def left_mul(matrix, values):
    return jnp.einsum("yk,...km->...ym", matrix, values, precision=lax.Precision.HIGHEST)


def on_device(fields, counts):
    rows_count = lax.axis_size("row")
    cols_count = lax.axis_size("col")
    my_row = lax.axis_index("row")
    my_column = lax.axis_index("col")
    capacity = fields.shape[0]
    block_x = GX // rows_count
    block_y = GY // cols_count
    lat_x = block_x // PE
    lat_y = GY // PE
    lat_z = GZ // PE
    brick_y = min(PE, block_y)
    per_patch = PE // brick_y
    per_pencil_y = block_y // brick_y
    repeat_y = max(1, block_y // PE)
    per_peer = (capacity + lat_y - 1) // lat_y * repeat_y
    brick_cells = 5 * PE * brick_y * PE
    buffer_rows = cols_count * per_peer
    row_counts = lax.all_gather(counts, "col", axis=1, tiled=True).reshape(cols_count)
    column_ids = jnp.arange(cols_count, dtype=jnp.int32)
    starts = jnp.sum(
        jnp.where(column_ids[None, :] < column_ids[:, None], row_counts[None, :], 0), axis=1
    )
    own_start = jnp.sum(jnp.where(column_ids == my_column, starts, 0))
    own_count = counts[0, 0]
    slot_ids = jnp.arange(capacity, dtype=jnp.int32)
    brick_ids = jnp.arange(per_patch, dtype=jnp.int32)
    y_patch = (own_start + slot_ids) % lat_y
    global_y = y_patch[:, None] * PE + brick_ids[None, :] * brick_y
    slot_inner = (slot_ids // lat_y * repeat_y + y_patch % repeat_y)[:, None]
    dest_index = (global_y // block_y * per_peer + slot_inner).reshape(-1)
    live_slots = jnp.broadcast_to((slot_ids < own_count)[:, None], (capacity, per_patch)).reshape(
        -1
    )
    buffer_ids = jnp.arange(buffer_rows, dtype=jnp.int32)
    send_select = ((buffer_ids[:, None] == dest_index[None, :]) & live_slots[None, :]).astype(
        jnp.float32
    )
    grid_xl = jnp.arange(lat_x, dtype=jnp.int32)[:, None, None]
    grid_w = jnp.arange(per_pencil_y, dtype=jnp.int32)[None, :, None]
    grid_zl = jnp.arange(lat_z, dtype=jnp.int32)[None, None, :]
    pencil_y = (my_column * block_y + grid_w * brick_y) // PE
    curve_pos = (grid_xl * lat_z + grid_zl) * lat_y + pencil_y
    curve_pos = curve_pos.reshape(-1)
    y_flat = jnp.broadcast_to(pencil_y, (lat_x, per_pencil_y, lat_z)).reshape(-1)
    owner = jnp.sum((starts[None, :] <= curve_pos[:, None]).astype(jnp.int32), axis=1) - 1
    owner_start = jnp.sum(
        jnp.where(column_ids[None, :] == owner[:, None], starts[None, :], 0), axis=1
    )
    source_index = (
        owner * per_peer + (curve_pos - owner_start) // lat_y * repeat_y + y_flat % repeat_y
    )
    recv_select = (buffer_ids[None, :] == source_index[:, None]).astype(jnp.float32)
    patch_bricks = (
        fields.reshape(capacity, 5, PE, per_patch, brick_y, PE)
        .transpose(0, 3, 1, 2, 4, 5)
        .reshape(capacity * per_patch, brick_cells)
    )
    send_buffer = jnp.matmul(send_select, patch_bricks, precision=lax.Precision.HIGHEST)
    arrived = lax.all_to_all(send_buffer, "col", split_axis=0, concat_axis=0, tiled=True)
    pencil_bricks = jnp.matmul(recv_select, arrived, precision=lax.Precision.HIGHEST)
    pencil = (
        pencil_bricks.reshape(lat_x, per_pencil_y, lat_z, 5, PE, brick_y, PE)
        .transpose(3, 0, 4, 1, 5, 2, 6)
        .reshape(5, block_x, block_y, GZ)
    )
    extended = padded(pencil, (("row", 1), ("col", 2)), 4)
    stepped = advance(extended)
    rows_y = GY // rows_count
    cols_z = GZ // cols_count
    cos_x, sin_x = dft_tables(GX)
    cos_y, sin_y = dft_tables(GY)
    cos_z, sin_z = dft_tables(GZ)
    density = stepped[0]
    along_re = right_mul(density, cos_z)
    along_im = -right_mul(density, sin_z)
    packed = (
        jnp.stack([along_re, along_im])
        .reshape(2, block_x, block_y, cols_count, cols_z)
        .transpose(3, 2, 0, 4, 1)
    )
    paired = lax.all_to_all(packed, "col", split_axis=0, concat_axis=0, tiled=True)
    paired = paired.reshape(GY, 2, cols_z * block_x)
    mid_re = paired[:, 0]
    mid_im = paired[:, 1]
    spec_re = left_mul(cos_y, mid_re) + left_mul(sin_y, mid_im)
    spec_im = left_mul(cos_y, mid_im) - left_mul(sin_y, mid_re)
    packed = (
        jnp.stack([spec_re, spec_im])
        .reshape(2, rows_count, rows_y, cols_z * block_x)
        .transpose(1, 0, 2, 3)
    )
    paired = lax.all_to_all(packed, "row", split_axis=0, concat_axis=0, tiled=True)
    paired = (
        paired.reshape(rows_count, 2, rows_y, cols_z, block_x)
        .transpose(1, 2, 3, 0, 4)
        .reshape(2, rows_y * cols_z, GX)
    )
    spec_re = right_mul(paired[0], cos_x) + right_mul(paired[1], sin_x)
    spec_im = right_mul(paired[1], cos_x) - right_mul(paired[0], sin_x)
    index_x = jnp.arange(GX, dtype=jnp.int32)
    index_y = my_row * rows_y + jnp.arange(rows_y, dtype=jnp.int32)
    index_z = my_column * cols_z + jnp.arange(cols_z, dtype=jnp.int32)
    wave_x = index_x.astype(jnp.float32)
    wave_y = index_y.astype(jnp.float32)
    wave_z = index_z.astype(jnp.float32)
    eigen = (
        lap_eigen(wave_x, GX)[None, None, :]
        + lap_eigen(wave_y, GY)[:, None, None]
        + lap_eigen(wave_z, GZ)[None, :, None]
    )
    zero_mode = (
        (index_x == 0)[None, None, :]
        & (index_y == 0)[:, None, None]
        & (index_z == 0)[None, :, None]
    )
    green = jnp.where(zero_mode, 0.0, four_pi_g / jnp.where(zero_mode, -1.0, eigen)).reshape(
        rows_y * cols_z, GX
    )
    pot_re = spec_re * green
    pot_im = spec_im * green
    scale = 1.0 / (GX * GY * GZ)
    sine_x = jnp.sin(2.0 * math.pi / GX * wave_x)[None, :]
    sine_y = jnp.broadcast_to(
        jnp.sin(2.0 * math.pi / GY * wave_y)[:, None], (rows_y, cols_z)
    ).reshape(rows_y * cols_z, 1)
    sine_z = jnp.broadcast_to(
        jnp.sin(2.0 * math.pi / GZ * wave_z)[None, :], (rows_y, cols_z)
    ).reshape(rows_y * cols_z, 1)
    grad_re = jnp.stack([-(sine_x * pot_im), -(sine_y * pot_im), -(sine_z * pot_im)])
    grad_im = jnp.stack([sine_x * pot_re, sine_y * pot_re, sine_z * pot_re])
    back_re = right_mul(grad_re, cos_x) - right_mul(grad_im, sin_x)
    back_im = right_mul(grad_im, cos_x) + right_mul(grad_re, sin_x)
    packed = (
        jnp.stack([back_re, back_im], axis=1)
        .reshape(3, 2, rows_y, cols_z, rows_count, block_x)
        .transpose(4, 0, 1, 2, 3, 5)
    )
    returned = lax.all_to_all(packed, "row", split_axis=0, concat_axis=0, tiled=True)
    returned = returned.transpose(1, 2, 0, 3, 4, 5).reshape(3, 2, GY, cols_z * block_x)
    mid_re = left_mul(cos_y, returned[:, 0]) - left_mul(sin_y, returned[:, 1])
    mid_im = left_mul(cos_y, returned[:, 1]) + left_mul(sin_y, returned[:, 0])
    packed = (
        jnp.stack([mid_re, mid_im], axis=1)
        .reshape(3, 2, cols_count, block_y, cols_z * block_x)
        .transpose(2, 0, 1, 3, 4)
    )
    returned = lax.all_to_all(packed, "col", split_axis=0, concat_axis=0, tiled=True)
    returned = (
        returned.reshape(cols_count, 3, 2, block_y, cols_z, block_x)
        .transpose(1, 2, 5, 3, 0, 4)
        .reshape(3, 2, block_x, block_y, GZ)
    )
    gradient = (right_mul(returned[:, 0], cos_z) - right_mul(returned[:, 1], sin_z)) * scale
    kicked = apply_kick(stepped, gradient)
    back_bricks = (
        kicked.reshape(5, lat_x, PE, per_pencil_y, brick_y, lat_z, PE)
        .transpose(1, 3, 5, 0, 2, 4, 6)
        .reshape(lat_x * per_pencil_y * lat_z, brick_cells)
    )
    return_buffer = jnp.matmul(recv_select.T, back_bricks, precision=lax.Precision.HIGHEST)
    came_back = lax.all_to_all(return_buffer, "col", split_axis=0, concat_axis=0, tiled=True)
    slot_bricks = jnp.matmul(send_select.T, came_back, precision=lax.Precision.HIGHEST)
    return (
        slot_bricks.reshape(capacity, per_patch, 5, PE, brick_y, PE)
        .transpose(0, 2, 3, 1, 4, 5)
        .reshape(capacity, 5, PE * PE * PE)
    )


def solution(mesh):
    return jax.shard_map(
        on_device,
        mesh=mesh,
        in_specs=(P(("row", "col"), None, None), P("row", "col")),
        out_specs=P(("row", "col"), None, None),
        check_vma=False,
    )
```

```python
import math

import jax
import jax.numpy as jnp
import numpy as np
from jax import lax
from jax.experimental import pallas as pl
from jax.experimental.pallas import tpu as pltpu
from jax.sharding import PartitionSpec as P

PE = 16
GX = 256
GY = 256
GZ = 128
ROWS = 8
COLS = 32
BX = GX // ROWS
BY = GY // COLS
CAP = 16
LINES = 16
BRICK = 5 * PE
HALO = 4

time_step = 0.03
four_pi_g = 10.0

PARAMS = pltpu.CompilerParams(vmem_limit_bytes=40 * 2**20)
VM = pl.BlockSpec(memory_space=pltpu.VMEM)
SM = pl.BlockSpec(memory_space=pltpu.SMEM)


def hartley(length):
    index = np.arange(length)
    angle = 2.0 * np.pi / length * (index[:, None] * index[None, :] % length)
    return ((np.cos(angle) + np.sin(angle)) / math.sqrt(length)).astype(np.float32)


def eigenvalues(length):
    return (-4.0 * np.sin(np.pi * np.arange(length) / length) ** 2).astype(np.float32)


def dot(left, right, dims=((1,), (0,))):
    return lax.dot_general(
        left,
        right,
        (dims, ((), ())),
        precision=lax.Precision.HIGHEST,
        preferred_element_type=jnp.float32,
    )


def swap_groups(arrays, group):
    count = len(arrays)
    lane = lax.broadcasted_iota(jnp.int32, arrays[0].shape, 1) // group
    arrays = list(arrays)
    distance = count // 2
    while distance:
        upper = (lane & distance) != 0
        for i in range(count):
            if i & distance:
                continue
            low, high = arrays[i], arrays[i + distance]
            arrays[i] = jnp.where(upper, pltpu.roll(high, distance * group, 1), low)
            arrays[i + distance] = jnp.where(
                upper, high, pltpu.roll(low, 128 - distance * group, 1)
            )
        distance //= 2
    return arrays


def pack_kernel(start_ref, fields_ref, out_ref):
    shift = start_ref[0]
    for q in range(5):
        for tile in range(2 * PE):
            a, half = tile // 2, tile % 2
            slots = fields_ref[q, :, tile * 128 : (tile + 1) * 128]
            turned = pltpu.roll(slots, shift, 0)
            out_ref[pl.ds(half * BRICK + q * PE + a, CAP, stride=2 * BRICK), :] = turned


def unpack_kernel(owner_ref, recv_ref, own_ref, xfirst_ref, xlast_ref, yfirst_ref, ylast_ref, flat_ref):
    for q in range(5):
        for xl in range(2):
            for part in range(2):
                rows = q * PE + part * 8
                lines = [
                    recv_ref[owner_ref[xl * 8 + zl], rows : rows + 8, :] for zl in range(8)
                ]
                for b, value in enumerate(swap_groups(lines, PE)):
                    base = (q * BX + xl * PE + part * 8) * BY + b
                    flat_ref[pl.ds(base, 8, stride=BY), :] = value
    block = flat_ref[...].reshape(5, BX, BY, GZ)
    own_ref[...] = block
    xfirst_ref[...] = block[:, :HALO]
    xlast_ref[...] = block[:, BX - HALO :]
    yfirst_ref[...] = block[:, :, :HALO]
    ylast_ref[...] = block[:, :, BY - HALO :]


def minmod(p, q):
    return jnp.maximum(jnp.minimum(p, q), 0.0) + jnp.minimum(jnp.maximum(p, q), 0.0)


def half_flux(states, direction, sign):
    density, energy = states[0], states[4]
    inverse = 1.0 / density
    velocity = 0.5 * states[1 + direction] * inverse
    squares = states[1] * states[1] + states[2] * states[2] + states[3] * states[3]
    pressure = 0.4 * energy - (0.2 * squares) * inverse
    pieces = [0.5 * states[1 + direction]]
    for component in range(3):
        term = states[1 + component] * velocity
        if component == direction:
            term = term + 0.5 * pressure
        pieces.append(term)
    pieces.append((energy + pressure) * velocity)
    if sign > 0:
        return [piece + 2.0 * state for piece, state in zip(pieces, states)]
    return [piece - 2.0 * state for piece, state in zip(pieces, states)]


def edge_terms(states, slopes, direction):
    halves = [0.5 * slope for slope in slopes]
    upper = half_flux([u + h for u, h in zip(states, halves)], direction, 1)
    lower = half_flux([u - h for u, h in zip(states, halves)], direction, -1)
    return upper, lower


def line_change(states, direction, axis):
    size = states[0].shape[axis]
    gaps = [pltpu.roll(u, size - 1, axis) - u for u in states]
    slopes = [minmod(pltpu.roll(g, 1, axis), g) for g in gaps]
    upper, lower = edge_terms(states, slopes, direction)
    faces = [u + pltpu.roll(w, size - 1, axis) for u, w in zip(upper, lower)]
    return [f - pltpu.roll(f, 1, axis) for f in faces]


def euler_stage(load, store, first_row, count, keep):
    def slopes_of(low, mid, high):
        return [minmod(b - a, c - b) for a, b, c in zip(low, mid, high)]

    cut = lambda states: [u[:keep] for u in states]
    r0, r1, r2, r3 = [cut(load(first_row + k)) for k in (-2, -1, 0, 1)]
    upper_prev, _ = edge_terms(r1, slopes_of(r0, r1, r2), 0)
    upper_now, lower_now = edge_terms(r2, slopes_of(r1, r2, r3), 0)
    face = [u + w for u, w in zip(upper_prev, lower_now)]

    def step(k, carry):
        face_low, upper_here = carry
        i = first_row + k
        here, above, far = load(i), cut(load(i + 1)), cut(load(i + 2))
        mine = cut(here)
        upper_next, lower_next = edge_terms(above, slopes_of(mine, above, far), 0)
        face_high = [u + w for u, w in zip(upper_here, lower_next)]
        change = [h - l for h, l in zip(face_high, face_low)]
        along_y = cut(line_change(here, 1, 0))
        along_z = line_change(mine, 2, 1)
        rate = [-(a + b + c) for a, b, c in zip(change, along_y, along_z)]
        store(i, mine, rate)
        return tuple(face_high), tuple(upper_next)

    lax.fori_loop(0, count, step, (tuple(face), tuple(upper_now)))


def euler_kernel(
    own_ref, xlow_ref, xhigh_ref, ylow_ref, yhigh_ref, clow_ref, chigh_ref, table_ref,
    stepped_ref, modes_ref, ext_ref, first_ref, flat_ref,
):
    low, high = slice(BY + HALO, BY + 2 * HALO), slice(BY, BY + HALO)
    inner = slice(HALO, HALO + BX)
    ext_ref[:, inner, 0:BY] = own_ref[...]
    ext_ref[:, 0:HALO, 0:BY] = xlow_ref[...]
    ext_ref[:, HALO + BX :, 0:BY] = xhigh_ref[...]
    ext_ref[:, inner, high] = yhigh_ref[...]
    ext_ref[:, inner, low] = ylow_ref[...]
    for part, ref in ((low, clow_ref), (high, chigh_ref)):
        corner = ref[...]
        ext_ref[:, 0:2, part] = corner[:, 0:2]
        ext_ref[:, 2:4, part] = corner[:, 0:2]
        ext_ref[:, HALO + BX : HALO + BX + 2, part] = corner[:, 2:4]
        ext_ref[:, HALO + BX + 2 :, part] = corner[:, 2:4]

    def load_ext(i):
        return [ext_ref[q, i] for q in range(5)]

    def store_first(i, states, rates):
        for q in range(5):
            first_ref[q, i] = states[q] + time_step * rates[q]

    euler_stage(load_ext, store_first, 2, BX + 4, BY + 2 * HALO)

    def load_first(i):
        return [first_ref[q, i] for q in range(5)]

    def store_stepped(i, states, rates):
        for q in range(5):
            second = states[q] + time_step * rates[q]
            value = 0.5 * ext_ref[q, i, 0:BY] + 0.5 * second
            stepped_ref[q, i - HALO] = value
            if q == 0:
                flat_ref[pl.ds(pl.multiple_of((i - HALO) * BY, BY), BY), :] = value

    euler_stage(load_first, store_stepped, HALO, BX, BY)
    density = jnp.concatenate(
        [flat_ref[pl.ds(b, BX, stride=BY), :] for b in range(BY)], axis=0
    )
    spread = dot(table_ref[...], density, ((1,), (1,)))
    modes_ref[pl.ds(0, 256, stride=2), :] = spread[:, :128]
    modes_ref[pl.ds(1, 256, stride=2), :] = spread[:, 128:]


def plane_kernel(place_ref, wave_ref, modes_ref, table_ref, eigx_ref, eigy_ref, out_ref, plane_ref, wide_ref):
    for high in range(2):
        for tile in range(2):
            lines = [
                modes_ref[pl.ds((high * 4 + r) * COLS * 2 + tile, COLS, stride=2), :]
                for r in range(4)
            ]
            for p, value in enumerate(swap_groups(lines, 32)):
                plane_ref[pl.ds(high * GY + tile * 4 + p, COLS, stride=BY), :] = value
    half = pl.multiple_of(place_ref[0] * 128, 128)
    table = table_ref[...]
    half_table = table_ref[pl.ds(half, 128), :]
    plane = jnp.concatenate([plane_ref[0:GY, :], plane_ref[GY:, :]], axis=1)
    spectrum = dot(dot(half_table, plane), table)
    eigen = eigx_ref[...] + eigy_ref[pl.ds(half, 128), :][:, 0:1] + wave_ref[0]
    flat = eigen >= 0.0
    green = jnp.where(flat, 0.0, four_pi_g / jnp.where(flat, -1.0, eigen))
    back = dot(spectrum * green, table)
    potential = dot(half_table, back, ((0,), (0,)))
    for high in range(2):
        base, side = high * (GY + 16), potential[:, high * 128 : high * 128 + 128]
        wide_ref[base + 8 : base + 8 + GY, :] = side
        wide_ref[base : base + 8, :] = side[GY - 8 :]
        wide_ref[base + 8 + GY : base + 16 + GY, :] = side[:8]

    def strip(row):
        return jnp.concatenate(
            [wide_ref[pl.ds(b + row, COLS, stride=BY), :] for b in (0, GY + 16)], axis=1
        )

    strips = [strip(8 + yl) for yl in range(BY)]
    below, above = strip(7), strip(16)
    lane = lax.broadcasted_iota(jnp.int32, (COLS, GX), 1) % 32
    sides = jnp.zeros((COLS, GX), jnp.float32)
    for yl in range(BY):
        sides = jnp.where(lane == yl, pltpu.roll(strips[yl], 1 + yl, 1), sides)
        sides = jnp.where(lane == 8 + yl, pltpu.roll(strips[yl], GX - 24 + yl, 1), sides)
    strips = strips + [below, above, sides, sides]
    for high in range(2):
        for quad in range(3):
            lines = [s[:, high * 128 : high * 128 + 128] for s in strips[quad * 4 : quad * 4 + 4]]
            for p, value in enumerate(swap_groups(lines, 32)):
                out_ref[pl.ds((high * 4 + p) * COLS * 3 + quad, COLS, stride=3), :] = value


def kick_kernel(owner_ref, stepped_ref, modes_ref, table_ref, out_ref, phi_ref, kicked_ref):
    table = table_ref[...]
    parts = []
    for quad in range(3):
        block = modes_ref[pl.ds(quad, 256, stride=3), :]
        parts.append(dot(block, table, ((0,), (0,))))
    for yl in range(BY):
        phi_ref[pl.ds(BY + yl, BX, stride=BY), :] = parts[yl // 4][(yl % 4) * 32 : (yl % 4) * 32 + 32]
    phi_ref[0:BY, :] = parts[2][64 : 64 + BY]
    phi_ref[BY + BX * BY :, :] = parts[2][64 + BY : 64 + 2 * BY]
    phi = phi_ref[...].reshape(BX + 2, BY, GZ)
    mid = phi[1 : 1 + BX]
    below = parts[2][0:32].reshape(BX, 1, GZ)
    above = parts[2][32:64].reshape(BX, 1, GZ)
    grad_x = 0.5 * (phi[2:] - phi[:BX])
    lower = jnp.concatenate([below, mid[:, : BY - 1]], axis=1)
    upper = jnp.concatenate([mid[:, 1:], above], axis=1)
    grad_y = 0.5 * (upper - lower)
    grad_z = 0.5 * (pltpu.roll(mid, GZ - 1, 2) - pltpu.roll(mid, 1, 2))
    grads = (grad_x, grad_y, grad_z)
    density = stepped_ref[0]
    momenta = [stepped_ref[1 + d] for d in range(3)]
    work = momenta[0] * grad_x + momenta[1] * grad_y + momenta[2] * grad_z
    cells = BX * BY
    kicked_ref[0:cells, :] = density.reshape(cells, GZ)
    for d in range(3):
        value = momenta[d] - time_step * density * grads[d]
        kicked_ref[(1 + d) * cells : (2 + d) * cells, :] = value.reshape(cells, GZ)
    kicked_ref[4 * cells :, :] = (stepped_ref[4] - time_step * work).reshape(cells, GZ)
    for q in range(5):
        for xl in range(2):
            for part in range(2):
                base = (q * BX + xl * PE + part * 8) * BY
                lines = [kicked_ref[pl.ds(base + b, 8, stride=BY), :] for b in range(BY)]
                rows = q * PE + part * 8
                for zl, value in enumerate(swap_groups(lines, PE)):
                    out_ref[owner_ref[xl * 8 + zl], rows : rows + 8, :] = value


def spread_kernel(place_ref, recv_ref, out_ref):
    shift = place_ref[0]
    live = lax.broadcasted_iota(jnp.int32, (CAP, 128), 0) < place_ref[1]
    for q in range(5):
        for tile in range(2 * PE):
            a, half = tile // 2, tile % 2
            lines = recv_ref[pl.ds(half * BRICK + q * PE + a, CAP, stride=2 * BRICK), :]
            turned = pltpu.roll(lines, shift, 0)
            out_ref[q, :, tile * 128 : (tile + 1) * 128] = jnp.where(live, turned, 0.0)


def call(kernel, outs, ins, scratch=()):
    shapes = [jax.ShapeDtypeStruct(s, jnp.float32) for s in outs]
    many = len(outs) > 1
    return pl.pallas_call(
        kernel,
        out_shape=tuple(shapes) if many else shapes[0],
        in_specs=[SM if i in ins[1] else VM for i in range(ins[0])],
        out_specs=tuple([VM] * len(outs)) if many else VM,
        scratch_shapes=[pltpu.VMEM(s, jnp.float32) for s in scratch],
        compiler_params=PARAMS,
    )


def gather_counts(counts):
    return lax.all_gather(counts, "col", axis=1, tiled=True).reshape(COLS)


def on_device(fields, counts):
    my_row = lax.axis_index("row")
    my_column = lax.axis_index("col")
    row_counts = gather_counts(counts)
    column_ids = jnp.arange(COLS, dtype=jnp.int32)
    starts = jnp.sum(
        jnp.where(column_ids[None, :] < column_ids[:, None], row_counts[None, :], 0), axis=1
    )
    own_start = jnp.sum(jnp.where(column_ids < my_column, row_counts, 0))
    y_patch = my_column // 2
    wanted = jnp.arange(LINES, dtype=jnp.int32) * 16 + y_patch
    owners = jnp.sum((starts[None, :] <= wanted[:, None]).astype(jnp.int32), axis=1) - 1
    turn = own_start % CAP

    sent = call(pack_kernel, [(COLS * BRICK, 128)], (2, (0,)))(
        turn.reshape(1), fields.transpose(1, 0, 2)
    )
    arrived = lax.all_to_all(
        sent.reshape(COLS, BRICK, 128), "col", split_axis=0, concat_axis=0, tiled=True
    )
    own, xfirst, xlast, yfirst, ylast = call(
        unpack_kernel,
        [
            (5, BX, BY, GZ),
            (5, HALO, BY, GZ),
            (5, HALO, BY, GZ),
            (5, BX, HALO, GZ),
            (5, BX, HALO, GZ),
        ],
        (2, (0,)),
        [(5 * BX * BY, GZ)],
    )(owners, arrived)

    def ring(count, step):
        return [(i, (i + step) % count) for i in range(count)]

    xlow = lax.ppermute(xlast, "row", ring(ROWS, 1))
    xhigh = lax.ppermute(xfirst, "row", ring(ROWS, -1))
    ylow = lax.ppermute(ylast, "col", ring(COLS, 1))
    yhigh = lax.ppermute(yfirst, "col", ring(COLS, -1))
    edges = jnp.concatenate([xlow[:, 2:4], xhigh[:, 0:2]], axis=1)
    clow = lax.ppermute(edges[:, :, BY - HALO :], "col", ring(COLS, 1))
    chigh = lax.ppermute(edges[:, :, :HALO], "col", ring(COLS, -1))

    table_z = hartley(GZ)
    table_x = hartley(GX)
    modes_of = np.arange(256) % GZ
    stepped, modes = call(
        euler_kernel,
        [(5, BX, BY, GZ), (512, 128)],
        (8, ()),
        [(5, BX + 2 * HALO, BY + 2 * HALO, GZ), (5, BX + 2 * HALO, BY + 2 * HALO, GZ), (BX * BY, GZ)],
    )(own, xlow, xhigh, ylow, yhigh, clow, chigh, jnp.asarray(table_z[modes_of]))
    planes = lax.all_to_all(
        modes.reshape(256, 2, 128), ("row", "col"), split_axis=0, concat_axis=0, tiled=True
    )
    place = my_row * COLS + my_column
    wave_z = place % GZ
    eig = eigenvalues(GX)
    eig_z = -4.0 * jnp.sin((math.pi / GZ) * wave_z.astype(jnp.float32)) ** 2
    strips = call(plane_kernel, [(768, 128)], (6, (0, 1)), [(2 * GY, 128), (2 * (GY + 16), 128)])(
        (place // GZ).reshape(1),
        eig_z.reshape(1),
        planes.reshape(512, 128),
        jnp.asarray(table_x),
        jnp.asarray(eig[None, :]),
        jnp.asarray(np.broadcast_to(eig[:, None], (GX, 128))),
    )
    strips = lax.all_to_all(
        strips.reshape(256, 3, 128), ("row", "col"), split_axis=0, concat_axis=0, tiled=True
    )
    returned = call(
        kick_kernel,
        [(COLS, BRICK, 128)],
        (4, (0,)),
        [((BX + 2) * BY, GZ), (5 * BX * BY, GZ)],
    )(owners, stepped, strips.reshape(768, 128), jnp.asarray(table_z[modes_of]))
    came_back = lax.all_to_all(returned, "col", split_axis=0, concat_axis=0, tiled=True)
    home = jnp.stack([(CAP - turn) % CAP, counts[0, 0]])
    result = call(spread_kernel, [(5, CAP, PE * PE * PE)], (2, (0,)))(
        home, came_back.reshape(COLS * BRICK, 128)
    )
    return result.transpose(1, 0, 2)


def solution(mesh):
    return jax.shard_map(
        on_device,
        mesh=mesh,
        in_specs=(P(("row", "col"), None, None), P("row", "col")),
        out_specs=P(("row", "col"), None, None),
        check_vma=False,
    )
```

```python
import math

import jax
import jax.numpy as jnp
import numpy as np
from jax import lax
from jax.experimental import pallas as pl
from jax.experimental.pallas import tpu as pltpu
from jax.sharding import PartitionSpec as P

PE = 16
GX = 256
GY = 256
GZ = 128
ROWS = 8
COLS = 32
BX = GX // ROWS
BY = GY // COLS
CAP = 16
LINES = 16
BRICK = 5 * PE
HALO = 4
CORNERS = ((1, 1), (-1, 1), (1, -1), (-1, -1))

time_step = 0.03
four_pi_g = 10.0

PARAMS = pltpu.CompilerParams(vmem_limit_bytes=40 * 2**20)
VM = pl.BlockSpec(memory_space=pltpu.VMEM)
SM = pl.BlockSpec(memory_space=pltpu.SMEM)


def hartley(length):
    index = np.arange(length)
    angle = 2.0 * np.pi / length * (index[:, None] * index[None, :] % length)
    return ((np.cos(angle) + np.sin(angle)) / math.sqrt(length)).astype(np.float32)


def eigenvalues(length):
    return (-4.0 * np.sin(np.pi * np.arange(length) / length) ** 2).astype(np.float32)


def dot(left, right, dims=((1,), (0,))):
    return lax.dot_general(
        left,
        right,
        (dims, ((), ())),
        precision=lax.Precision.HIGHEST,
        preferred_element_type=jnp.float32,
    )


def swap_groups(arrays, group):
    count = len(arrays)
    lane = lax.broadcasted_iota(jnp.int32, arrays[0].shape, 1) // group
    arrays = list(arrays)
    distance = count // 2
    while distance:
        upper = (lane & distance) != 0
        for i in range(count):
            if i & distance:
                continue
            low, high = arrays[i], arrays[i + distance]
            arrays[i] = jnp.where(upper, pltpu.roll(high, distance * group, 1), low)
            arrays[i + distance] = jnp.where(
                upper, high, pltpu.roll(low, 128 - distance * group, 1)
            )
        distance //= 2
    return arrays


def pack_kernel(start_ref, fields_ref, out_ref):
    shift = start_ref[0]
    for q in range(5):
        for tile in range(2 * PE):
            a, half = tile // 2, tile % 2
            slots = fields_ref[q, :, tile * 128 : (tile + 1) * 128]
            turned = pltpu.roll(slots, shift, 0)
            out_ref[pl.ds(half * BRICK + q * PE + a, CAP, stride=2 * BRICK), :] = turned


def unpack_kernel(
    owner_ref, recv_ref, own_ref, xfirst_ref, xlast_ref, yfirst_ref, ylast_ref, *rest
):
    corner_refs, flat_ref = rest[:4], rest[4]
    for q in range(5):
        for xl in range(2):
            for part in range(2):
                rows = q * PE + part * 8
                lines = [
                    recv_ref[owner_ref[xl * 8 + zl], rows : rows + 8, :] for zl in range(8)
                ]
                for b, value in enumerate(swap_groups(lines, PE)):
                    base = (q * BX + xl * PE + part * 8) * BY + b
                    flat_ref[pl.ds(base, 8, stride=BY), :] = value
    block = flat_ref[...].reshape(5, BX, BY, GZ)
    own_ref[...] = block
    xfirst_ref[...] = block[:, :HALO]
    xlast_ref[...] = block[:, BX - HALO :]
    yfirst_ref[...] = block[:, :, :HALO]
    ylast_ref[...] = block[:, :, BY - HALO :]
    for ref, (row_step, col_step) in zip(corner_refs, CORNERS):
        part = block[:, BX - 2 :] if row_step > 0 else block[:, :2]
        ref[...] = part[:, :, BY - HALO :] if col_step > 0 else part[:, :, :HALO]


def minmod(p, q):
    return jnp.maximum(jnp.minimum(p, q), 0.0) + jnp.minimum(jnp.maximum(p, q), 0.0)


def half_flux(states, direction, sign):
    density, energy = states[0], states[4]
    inverse = 1.0 / density
    velocity = 0.5 * states[1 + direction] * inverse
    squares = states[1] * states[1] + states[2] * states[2] + states[3] * states[3]
    pressure = 0.4 * energy - (0.2 * squares) * inverse
    pieces = [0.5 * states[1 + direction]]
    for component in range(3):
        term = states[1 + component] * velocity
        if component == direction:
            term = term + 0.5 * pressure
        pieces.append(term)
    pieces.append((energy + pressure) * velocity)
    if sign > 0:
        return [piece + 2.0 * state for piece, state in zip(pieces, states)]
    return [piece - 2.0 * state for piece, state in zip(pieces, states)]


def edge_terms(states, slopes, direction):
    halves = [0.5 * slope for slope in slopes]
    upper = half_flux([u + h for u, h in zip(states, halves)], direction, 1)
    lower = half_flux([u - h for u, h in zip(states, halves)], direction, -1)
    return upper, lower


def line_change(states, direction, axis):
    size = states[0].shape[axis]
    gaps = [pltpu.roll(u, size - 1, axis) - u for u in states]
    slopes = [minmod(pltpu.roll(g, 1, axis), g) for g in gaps]
    upper, lower = edge_terms(states, slopes, direction)
    faces = [u + pltpu.roll(w, size - 1, axis) for u, w in zip(upper, lower)]
    return [f - pltpu.roll(f, 1, axis) for f in faces]


def euler_stage(load, store, first_row, count, keep):
    def slopes_of(low, mid, high):
        return [minmod(b - a, c - b) for a, b, c in zip(low, mid, high)]

    cut = lambda states: [u[:keep] for u in states]
    r0, r1, r2, r3 = [cut(load(first_row + k)) for k in (-2, -1, 0, 1)]
    upper_prev, _ = edge_terms(r1, slopes_of(r0, r1, r2), 0)
    upper_now, lower_now = edge_terms(r2, slopes_of(r1, r2, r3), 0)
    face = [u + w for u, w in zip(upper_prev, lower_now)]

    def step(k, carry):
        face_low, upper_here = carry
        i = first_row + k
        here, above, far = load(i), cut(load(i + 1)), cut(load(i + 2))
        mine = cut(here)
        upper_next, lower_next = edge_terms(above, slopes_of(mine, above, far), 0)
        face_high = [u + w for u, w in zip(upper_here, lower_next)]
        change = [h - l for h, l in zip(face_high, face_low)]
        along_y = cut(line_change(here, 1, 0))
        along_z = line_change(mine, 2, 1)
        rate = [-(a + b + c) for a, b, c in zip(change, along_y, along_z)]
        store(i, mine, rate)
        return tuple(face_high), tuple(upper_next)

    lax.fori_loop(0, count, step, (tuple(face), tuple(upper_now)))


def euler_kernel(
    own_ref, xlow_ref, xhigh_ref, ylow_ref, yhigh_ref, c0_ref, c1_ref, c2_ref, c3_ref, table_ref,
    stepped_ref, modes_ref, ext_ref, first_ref, flat_ref,
):
    low, high = slice(BY + HALO, BY + 2 * HALO), slice(BY, BY + HALO)
    inner = slice(HALO, HALO + BX)
    ext_ref[:, inner, 0:BY] = own_ref[...]
    ext_ref[:, 0:HALO, 0:BY] = xlow_ref[...]
    ext_ref[:, HALO + BX :, 0:BY] = xhigh_ref[...]
    ext_ref[:, inner, high] = yhigh_ref[...]
    ext_ref[:, inner, low] = ylow_ref[...]
    for ref, (row_step, col_step) in zip((c0_ref, c1_ref, c2_ref, c3_ref), CORNERS):
        part = low if col_step > 0 else high
        corner = ref[...]
        outer = 0 if row_step > 0 else HALO + BX
        ext_ref[:, outer : outer + 2, part] = corner
        ext_ref[:, outer + 2 : outer + 4, part] = corner

    def load_ext(i):
        return [ext_ref[q, i] for q in range(5)]

    def store_first(i, states, rates):
        for q in range(5):
            first_ref[q, i] = states[q] + time_step * rates[q]

    euler_stage(load_ext, store_first, 2, BX + 4, BY + 2 * HALO)

    def load_first(i):
        return [first_ref[q, i] for q in range(5)]

    def store_stepped(i, states, rates):
        for q in range(5):
            second = states[q] + time_step * rates[q]
            value = 0.5 * ext_ref[q, i, 0:BY] + 0.5 * second
            stepped_ref[q, i - HALO] = value
            if q == 0:
                flat_ref[pl.ds(pl.multiple_of((i - HALO) * BY, BY), BY), :] = value

    euler_stage(load_first, store_stepped, HALO, BX, BY)
    density = jnp.concatenate(
        [flat_ref[pl.ds(b, BX, stride=BY), :] for b in range(BY)], axis=0
    )
    spread = dot(table_ref[...], density, ((1,), (1,)))
    modes_ref[pl.ds(0, 256, stride=2), :] = spread[:, :128]
    modes_ref[pl.ds(1, 256, stride=2), :] = spread[:, 128:]


def plane_kernel(place_ref, wave_ref, modes_ref, table_ref, eigx_ref, eigy_ref, out_ref, plane_ref, wide_ref):
    for high in range(2):
        for tile in range(2):
            lines = [
                modes_ref[pl.ds((high * 4 + r) * COLS * 2 + tile, COLS, stride=2), :]
                for r in range(4)
            ]
            for p, value in enumerate(swap_groups(lines, 32)):
                plane_ref[pl.ds(high * GY + tile * 4 + p, COLS, stride=BY), :] = value
    half = pl.multiple_of(place_ref[0] * 128, 128)
    table = table_ref[...]
    half_table = table_ref[pl.ds(half, 128), :]
    plane = jnp.concatenate([plane_ref[0:GY, :], plane_ref[GY:, :]], axis=1)
    spectrum = dot(dot(half_table, plane), table)
    eigen = eigx_ref[...] + eigy_ref[pl.ds(half, 128), :][:, 0:1] + wave_ref[0]
    flat = eigen >= 0.0
    green = jnp.where(flat, 0.0, four_pi_g / jnp.where(flat, -1.0, eigen))
    back = dot(spectrum * green, table)
    potential = dot(half_table, back, ((0,), (0,)))
    for high in range(2):
        base, side = high * (GY + 16), potential[:, high * 128 : high * 128 + 128]
        wide_ref[base + 8 : base + 8 + GY, :] = side
        wide_ref[base : base + 8, :] = side[GY - 8 :]
        wide_ref[base + 8 + GY : base + 16 + GY, :] = side[:8]

    def strip(row):
        return jnp.concatenate(
            [wide_ref[pl.ds(b + row, COLS, stride=BY), :] for b in (0, GY + 16)], axis=1
        )

    strips = [strip(8 + yl) for yl in range(BY)]
    below, above = strip(7), strip(16)
    lane = lax.broadcasted_iota(jnp.int32, (COLS, GX), 1) % 32
    sides = jnp.zeros((COLS, GX), jnp.float32)
    for yl in range(BY):
        sides = jnp.where(lane == yl, pltpu.roll(strips[yl], 1 + yl, 1), sides)
        sides = jnp.where(lane == 8 + yl, pltpu.roll(strips[yl], GX - 24 + yl, 1), sides)
    strips = strips + [below, above, sides, sides]
    for high in range(2):
        for quad in range(3):
            lines = [s[:, high * 128 : high * 128 + 128] for s in strips[quad * 4 : quad * 4 + 4]]
            for p, value in enumerate(swap_groups(lines, 32)):
                out_ref[pl.ds((high * 4 + p) * COLS * 3 + quad, COLS, stride=3), :] = value


def kick_kernel(owner_ref, stepped_ref, modes_ref, table_ref, out_ref, phi_ref, kicked_ref):
    table = table_ref[...]
    parts = []
    for quad in range(3):
        block = modes_ref[pl.ds(quad, 256, stride=3), :]
        parts.append(dot(block, table, ((0,), (0,))))
    for yl in range(BY):
        phi_ref[pl.ds(BY + yl, BX, stride=BY), :] = parts[yl // 4][(yl % 4) * 32 : (yl % 4) * 32 + 32]
    phi_ref[0:BY, :] = parts[2][64 : 64 + BY]
    phi_ref[BY + BX * BY :, :] = parts[2][64 + BY : 64 + 2 * BY]
    phi = phi_ref[...].reshape(BX + 2, BY, GZ)
    mid = phi[1 : 1 + BX]
    below = parts[2][0:32].reshape(BX, 1, GZ)
    above = parts[2][32:64].reshape(BX, 1, GZ)
    grad_x = 0.5 * (phi[2:] - phi[:BX])
    lower = jnp.concatenate([below, mid[:, : BY - 1]], axis=1)
    upper = jnp.concatenate([mid[:, 1:], above], axis=1)
    grad_y = 0.5 * (upper - lower)
    grad_z = 0.5 * (pltpu.roll(mid, GZ - 1, 2) - pltpu.roll(mid, 1, 2))
    grads = (grad_x, grad_y, grad_z)
    density = stepped_ref[0]
    momenta = [stepped_ref[1 + d] for d in range(3)]
    work = momenta[0] * grad_x + momenta[1] * grad_y + momenta[2] * grad_z
    cells = BX * BY
    kicked_ref[0:cells, :] = density.reshape(cells, GZ)
    for d in range(3):
        value = momenta[d] - time_step * density * grads[d]
        kicked_ref[(1 + d) * cells : (2 + d) * cells, :] = value.reshape(cells, GZ)
    kicked_ref[4 * cells :, :] = (stepped_ref[4] - time_step * work).reshape(cells, GZ)
    for q in range(5):
        for xl in range(2):
            for part in range(2):
                base = (q * BX + xl * PE + part * 8) * BY
                lines = [kicked_ref[pl.ds(base + b, 8, stride=BY), :] for b in range(BY)]
                rows = q * PE + part * 8
                for zl, value in enumerate(swap_groups(lines, PE)):
                    out_ref[owner_ref[xl * 8 + zl], rows : rows + 8, :] = value


def spread_kernel(place_ref, recv_ref, out_ref):
    shift = place_ref[0]
    live = lax.broadcasted_iota(jnp.int32, (CAP, 128), 0) < place_ref[1]
    for q in range(5):
        for tile in range(2 * PE):
            a, half = tile // 2, tile % 2
            lines = recv_ref[pl.ds(half * BRICK + q * PE + a, CAP, stride=2 * BRICK), :]
            turned = pltpu.roll(lines, shift, 0)
            out_ref[q, :, tile * 128 : (tile + 1) * 128] = jnp.where(live, turned, 0.0)


def call(kernel, outs, ins, scratch=()):
    shapes = [jax.ShapeDtypeStruct(s, jnp.float32) for s in outs]
    many = len(outs) > 1
    return pl.pallas_call(
        kernel,
        out_shape=tuple(shapes) if many else shapes[0],
        in_specs=[SM if i in ins[1] else VM for i in range(ins[0])],
        out_specs=tuple([VM] * len(outs)) if many else VM,
        scratch_shapes=[pltpu.VMEM(s, jnp.float32) for s in scratch],
        compiler_params=PARAMS,
    )


def ring(count, step):
    return [(i, (i + step) % count) for i in range(count)]


def gather_counts(counts, column):
    own = counts.reshape(1)
    inner, outer = column % 4, column // 4
    quad = jnp.arange(4, dtype=jnp.int32)
    four = jnp.where(quad == inner, own, 0)
    for k in range(1, 4):
        pairs = [(c, c // 4 * 4 + (c + k) % 4) for c in range(COLS)]
        four = jnp.where(quad == (inner - k) % 4, lax.ppermute(own, "col", pairs), four)
    groups = jnp.arange(8, dtype=jnp.int32)[:, None]
    every = jnp.where(groups == outer, four[None, :], 0)
    for k in range(1, 8):
        moved = lax.ppermute(four, "col", ring(COLS, 4 * k))
        every = jnp.where(groups == (outer - k) % 8, moved[None, :], every)
    return every.reshape(COLS)


def on_device(fields, counts):
    my_row = lax.axis_index("row")
    my_column = lax.axis_index("col")
    row_counts = gather_counts(counts, my_column)
    column_ids = jnp.arange(COLS, dtype=jnp.int32)
    starts = jnp.sum(
        jnp.where(column_ids[None, :] < column_ids[:, None], row_counts[None, :], 0), axis=1
    )
    own_start = jnp.sum(jnp.where(column_ids < my_column, row_counts, 0))
    y_patch = my_column // 2
    wanted = jnp.arange(LINES, dtype=jnp.int32) * 16 + y_patch
    owners = jnp.sum((starts[None, :] <= wanted[:, None]).astype(jnp.int32), axis=1) - 1
    turn = own_start % CAP

    sent = call(pack_kernel, [(COLS * BRICK, 128)], (2, (0,)))(
        turn.reshape(1), fields.transpose(1, 0, 2)
    )
    arrived = lax.all_to_all(
        sent.reshape(COLS, BRICK, 128), "col", split_axis=0, concat_axis=0, tiled=True
    )
    own, xfirst, xlast, yfirst, ylast, *edges = call(
        unpack_kernel,
        [
            (5, BX, BY, GZ),
            (5, HALO, BY, GZ),
            (5, HALO, BY, GZ),
            (5, BX, HALO, GZ),
            (5, BX, HALO, GZ),
        ]
        + [(5, 2, HALO, GZ)] * 4,
        (2, (0,)),
        [(5 * BX * BY, GZ)],
    )(owners, arrived)

    def diagonal(row_step, col_step):
        return [
            (r * COLS + c, (r + row_step) % ROWS * COLS + (c + col_step) % COLS)
            for r in range(ROWS)
            for c in range(COLS)
        ]

    xlow = lax.ppermute(xlast, "row", ring(ROWS, 1))
    xhigh = lax.ppermute(xfirst, "row", ring(ROWS, -1))
    ylow = lax.ppermute(ylast, "col", ring(COLS, 1))
    yhigh = lax.ppermute(yfirst, "col", ring(COLS, -1))
    both = ("row", "col")
    corners = [
        lax.ppermute(corner, both, diagonal(row_step, col_step))
        for corner, (row_step, col_step) in zip(edges, CORNERS)
    ]

    table_z = hartley(GZ)
    table_x = hartley(GX)
    modes_of = np.arange(256) % GZ
    stepped, modes = call(
        euler_kernel,
        [(5, BX, BY, GZ), (512, 128)],
        (10, ()),
        [(5, BX + 2 * HALO, BY + 2 * HALO, GZ), (5, BX + 2 * HALO, BY + 2 * HALO, GZ), (BX * BY, GZ)],
    )(own, xlow, xhigh, ylow, yhigh, *corners, jnp.asarray(table_z[modes_of]))
    planes = lax.all_to_all(
        modes.reshape(256, 2, 128), ("row", "col"), split_axis=0, concat_axis=0, tiled=True
    )
    place = my_row * COLS + my_column
    wave_z = place % GZ
    eig = eigenvalues(GX)
    eig_z = -4.0 * jnp.sin((math.pi / GZ) * wave_z.astype(jnp.float32)) ** 2
    strips = call(plane_kernel, [(768, 128)], (6, (0, 1)), [(2 * GY, 128), (2 * (GY + 16), 128)])(
        (place // GZ).reshape(1),
        eig_z.reshape(1),
        planes.reshape(512, 128),
        jnp.asarray(table_x),
        jnp.asarray(eig[None, :]),
        jnp.asarray(np.broadcast_to(eig[:, None], (GX, 128))),
    )
    strips = lax.all_to_all(
        strips.reshape(256, 3, 128), ("row", "col"), split_axis=0, concat_axis=0, tiled=True
    )
    returned = call(
        kick_kernel,
        [(COLS, BRICK, 128)],
        (4, (0,)),
        [((BX + 2) * BY, GZ), (5 * BX * BY, GZ)],
    )(owners, stepped, strips.reshape(768, 128), jnp.asarray(table_z[modes_of]))
    came_back = lax.all_to_all(returned, "col", split_axis=0, concat_axis=0, tiled=True)
    home = jnp.stack([(CAP - turn) % CAP, counts[0, 0]])
    result = call(spread_kernel, [(5, CAP, PE * PE * PE)], (2, (0,)))(
        home, came_back.reshape(COLS * BRICK, 128)
    )
    return result.transpose(1, 0, 2)


def solution(mesh):
    return jax.shard_map(
        on_device,
        mesh=mesh,
        in_specs=(P(("row", "col"), None, None), P("row", "col")),
        out_specs=P(("row", "col"), None, None),
        check_vma=False,
    )
```

```python
import math

import jax
import jax.numpy as jnp
import numpy as np
from jax import lax
from jax.experimental import pallas as pl
from jax.experimental.pallas import tpu as pltpu
from jax.sharding import PartitionSpec as P

PE = 16
GX = 256
GY = 256
GZ = 128
ROWS = 8
COLS = 32
BX = GX // ROWS
BY = GY // COLS
CAP = 16
LINES = 16
BRICK = 5 * PE
HALO = 4

time_step = 0.03
four_pi_g = 10.0

PARAMS = pltpu.CompilerParams(vmem_limit_bytes=40 * 2**20)
VM = pl.BlockSpec(memory_space=pltpu.VMEM)
SM = pl.BlockSpec(memory_space=pltpu.SMEM)


def hartley(length):
    index = np.arange(length)
    angle = 2.0 * np.pi / length * (index[:, None] * index[None, :] % length)
    return ((np.cos(angle) + np.sin(angle)) / math.sqrt(length)).astype(np.float32)


def eigenvalues(length):
    return (-4.0 * np.sin(np.pi * np.arange(length) / length) ** 2).astype(np.float32)


def dot(left, right, dims=((1,), (0,))):
    return lax.dot_general(
        left,
        right,
        (dims, ((), ())),
        precision=lax.Precision.HIGHEST,
        preferred_element_type=jnp.float32,
    )


def swap_groups(arrays, group):
    count = len(arrays)
    lane = lax.broadcasted_iota(jnp.int32, arrays[0].shape, 1) // group
    arrays = list(arrays)
    distance = count // 2
    while distance:
        upper = (lane & distance) != 0
        for i in range(count):
            if i & distance:
                continue
            low, high = arrays[i], arrays[i + distance]
            arrays[i] = jnp.where(upper, pltpu.roll(high, distance * group, 1), low)
            arrays[i + distance] = jnp.where(
                upper, high, pltpu.roll(low, 128 - distance * group, 1)
            )
        distance //= 2
    return arrays


def pack_kernel(start_ref, fields_ref, out_ref):
    shift = start_ref[0]
    for q in range(5):
        for tile in range(2 * PE):
            a, half = tile // 2, tile % 2
            slots = fields_ref[q, :, tile * 128 : (tile + 1) * 128]
            turned = pltpu.roll(slots, shift, 0)
            out_ref[pl.ds(half * BRICK + q * PE + a, CAP, stride=2 * BRICK), :] = turned


def unpack_kernel(owner_ref, recv_ref, own_ref, xfirst_ref, xlast_ref, yfirst_ref, ylast_ref, flat_ref):
    for q in range(5):
        for xl in range(2):
            for part in range(2):
                rows = q * PE + part * 8
                lines = [
                    recv_ref[owner_ref[xl * 8 + zl], rows : rows + 8, :] for zl in range(8)
                ]
                for b, value in enumerate(swap_groups(lines, PE)):
                    base = (q * BX + xl * PE + part * 8) * BY + b
                    flat_ref[pl.ds(base, 8, stride=BY), :] = value
    block = flat_ref[...].reshape(5, BX, BY, GZ)
    own_ref[...] = block
    xfirst_ref[...] = block[:, :HALO]
    xlast_ref[...] = block[:, BX - HALO :]
    yfirst_ref[...] = block[:, :, :HALO]
    ylast_ref[...] = block[:, :, BY - HALO :]


def minmod(p, q):
    return jnp.maximum(jnp.minimum(p, q), 0.0) + jnp.minimum(jnp.maximum(p, q), 0.0)


def half_flux(states, direction, sign):
    density, energy = states[0], states[4]
    inverse = 1.0 / density
    velocity = 0.5 * states[1 + direction] * inverse
    squares = states[1] * states[1] + states[2] * states[2] + states[3] * states[3]
    pressure = 0.4 * energy - (0.2 * squares) * inverse
    pieces = [0.5 * states[1 + direction]]
    for component in range(3):
        term = states[1 + component] * velocity
        if component == direction:
            term = term + 0.5 * pressure
        pieces.append(term)
    pieces.append((energy + pressure) * velocity)
    if sign > 0:
        return [piece + 2.0 * state for piece, state in zip(pieces, states)]
    return [piece - 2.0 * state for piece, state in zip(pieces, states)]


def edge_terms(states, slopes, direction):
    halves = [0.5 * slope for slope in slopes]
    upper = half_flux([u + h for u, h in zip(states, halves)], direction, 1)
    lower = half_flux([u - h for u, h in zip(states, halves)], direction, -1)
    return upper, lower


def line_change(states, direction, axis):
    size = states[0].shape[axis]
    gaps = [pltpu.roll(u, size - 1, axis) - u for u in states]
    slopes = [minmod(pltpu.roll(g, 1, axis), g) for g in gaps]
    upper, lower = edge_terms(states, slopes, direction)
    faces = [u + pltpu.roll(w, size - 1, axis) for u, w in zip(upper, lower)]
    return [f - pltpu.roll(f, 1, axis) for f in faces]


def euler_stage(load, store, first_row, count, keep):
    def slopes_of(low, mid, high):
        return [minmod(b - a, c - b) for a, b, c in zip(low, mid, high)]

    cut = lambda states: [u[:keep] for u in states]
    r0, r1, r2, r3 = [cut(load(first_row + k)) for k in (-2, -1, 0, 1)]
    upper_prev, _ = edge_terms(r1, slopes_of(r0, r1, r2), 0)
    upper_now, lower_now = edge_terms(r2, slopes_of(r1, r2, r3), 0)
    face = [u + w for u, w in zip(upper_prev, lower_now)]

    def step(k, carry):
        face_low, upper_here = carry
        i = first_row + k
        here, above, far = load(i), cut(load(i + 1)), cut(load(i + 2))
        mine = cut(here)
        upper_next, lower_next = edge_terms(above, slopes_of(mine, above, far), 0)
        face_high = [u + w for u, w in zip(upper_here, lower_next)]
        change = [h - l for h, l in zip(face_high, face_low)]
        along_y = cut(line_change(here, 1, 0))
        along_z = line_change(mine, 2, 1)
        rate = [-(a + b + c) for a, b, c in zip(change, along_y, along_z)]
        store(i, mine, rate)
        return tuple(face_high), tuple(upper_next)

    lax.fori_loop(0, count, step, (tuple(face), tuple(upper_now)), unroll=4)


def euler_kernel(
    own_ref, xlow_ref, xhigh_ref, ylow_ref, yhigh_ref, clow_ref, chigh_ref, table_ref,
    stepped_ref, modes_ref, ext_ref, first_ref, flat_ref,
):
    low, high = slice(BY + HALO, BY + 2 * HALO), slice(BY, BY + HALO)
    inner = slice(HALO, HALO + BX)
    ext_ref[:, inner, 0:BY] = own_ref[...]
    ext_ref[:, 0:HALO, 0:BY] = xlow_ref[...]
    ext_ref[:, HALO + BX :, 0:BY] = xhigh_ref[...]
    ext_ref[:, inner, high] = yhigh_ref[...]
    ext_ref[:, inner, low] = ylow_ref[...]
    for part, ref in ((low, clow_ref), (high, chigh_ref)):
        corner = ref[...]
        ext_ref[:, 0:2, part] = corner[:, 0:2]
        ext_ref[:, 2:4, part] = corner[:, 0:2]
        ext_ref[:, HALO + BX : HALO + BX + 2, part] = corner[:, 2:4]
        ext_ref[:, HALO + BX + 2 :, part] = corner[:, 2:4]

    def load_ext(i):
        return [ext_ref[q, i] for q in range(5)]

    def store_first(i, states, rates):
        for q in range(5):
            first_ref[q, i] = states[q] + time_step * rates[q]

    euler_stage(load_ext, store_first, 2, BX + 4, BY + 2 * HALO)

    def load_first(i):
        return [first_ref[q, i] for q in range(5)]

    def store_stepped(i, states, rates):
        for q in range(5):
            second = states[q] + time_step * rates[q]
            value = 0.5 * ext_ref[q, i, 0:BY] + 0.5 * second
            stepped_ref[q, i - HALO] = value
            if q == 0:
                flat_ref[pl.ds(pl.multiple_of((i - HALO) * BY, BY), BY), :] = value

    euler_stage(load_first, store_stepped, HALO, BX, BY)
    density = jnp.concatenate(
        [flat_ref[pl.ds(b, BX, stride=BY), :] for b in range(BY)], axis=0
    )
    spread = dot(table_ref[...], density, ((1,), (1,)))
    modes_ref[pl.ds(0, 256, stride=2), :] = spread[:, :128]
    modes_ref[pl.ds(1, 256, stride=2), :] = spread[:, 128:]


def plane_kernel(place_ref, wave_ref, modes_ref, table_ref, eigx_ref, eigy_ref, out_ref, plane_ref, wide_ref):
    for high in range(2):
        for tile in range(2):
            lines = [
                modes_ref[pl.ds((high * 4 + r) * COLS * 2 + tile, COLS, stride=2), :]
                for r in range(4)
            ]
            for p, value in enumerate(swap_groups(lines, 32)):
                plane_ref[pl.ds(high * GY + tile * 4 + p, COLS, stride=BY), :] = value
    half = pl.multiple_of(place_ref[0] * 128, 128)
    table = table_ref[...]
    half_table = table_ref[pl.ds(half, 128), :]
    plane = jnp.concatenate([plane_ref[0:GY, :], plane_ref[GY:, :]], axis=1)
    spectrum = dot(dot(half_table, plane), table)
    eigen = eigx_ref[...] + eigy_ref[pl.ds(half, 128), :][:, 0:1] + wave_ref[0]
    flat = eigen >= 0.0
    green = jnp.where(flat, 0.0, four_pi_g / jnp.where(flat, -1.0, eigen))
    back = dot(spectrum * green, table)
    potential = dot(half_table, back, ((0,), (0,)))
    for high in range(2):
        base, side = high * (GY + 16), potential[:, high * 128 : high * 128 + 128]
        wide_ref[base + 8 : base + 8 + GY, :] = side
        wide_ref[base : base + 8, :] = side[GY - 8 :]
        wide_ref[base + 8 + GY : base + 16 + GY, :] = side[:8]

    def strip(row):
        return jnp.concatenate(
            [wide_ref[pl.ds(b + row, COLS, stride=BY), :] for b in (0, GY + 16)], axis=1
        )

    strips = [strip(8 + yl) for yl in range(BY)]
    below, above = strip(7), strip(16)
    lane = lax.broadcasted_iota(jnp.int32, (COLS, GX), 1) % 32
    sides = jnp.zeros((COLS, GX), jnp.float32)
    for yl in range(BY):
        sides = jnp.where(lane == yl, pltpu.roll(strips[yl], 1 + yl, 1), sides)
        sides = jnp.where(lane == 8 + yl, pltpu.roll(strips[yl], GX - 24 + yl, 1), sides)
    strips = strips + [below, above, sides, sides]
    for high in range(2):
        for quad in range(3):
            lines = [s[:, high * 128 : high * 128 + 128] for s in strips[quad * 4 : quad * 4 + 4]]
            for p, value in enumerate(swap_groups(lines, 32)):
                out_ref[pl.ds((high * 4 + p) * COLS * 3 + quad, COLS, stride=3), :] = value


def kick_kernel(owner_ref, stepped_ref, modes_ref, table_ref, out_ref, phi_ref, kicked_ref):
    table = table_ref[...]
    parts = []
    for quad in range(3):
        block = modes_ref[pl.ds(quad, 256, stride=3), :]
        parts.append(dot(block, table, ((0,), (0,))))
    for yl in range(BY):
        phi_ref[pl.ds(BY + yl, BX, stride=BY), :] = parts[yl // 4][(yl % 4) * 32 : (yl % 4) * 32 + 32]
    phi_ref[0:BY, :] = parts[2][64 : 64 + BY]
    phi_ref[BY + BX * BY :, :] = parts[2][64 + BY : 64 + 2 * BY]
    phi = phi_ref[...].reshape(BX + 2, BY, GZ)
    mid = phi[1 : 1 + BX]
    below = parts[2][0:32].reshape(BX, 1, GZ)
    above = parts[2][32:64].reshape(BX, 1, GZ)
    grad_x = 0.5 * (phi[2:] - phi[:BX])
    lower = jnp.concatenate([below, mid[:, : BY - 1]], axis=1)
    upper = jnp.concatenate([mid[:, 1:], above], axis=1)
    grad_y = 0.5 * (upper - lower)
    grad_z = 0.5 * (pltpu.roll(mid, GZ - 1, 2) - pltpu.roll(mid, 1, 2))
    grads = (grad_x, grad_y, grad_z)
    density = stepped_ref[0]
    momenta = [stepped_ref[1 + d] for d in range(3)]
    work = momenta[0] * grad_x + momenta[1] * grad_y + momenta[2] * grad_z
    cells = BX * BY
    kicked_ref[0:cells, :] = density.reshape(cells, GZ)
    for d in range(3):
        value = momenta[d] - time_step * density * grads[d]
        kicked_ref[(1 + d) * cells : (2 + d) * cells, :] = value.reshape(cells, GZ)
    kicked_ref[4 * cells :, :] = (stepped_ref[4] - time_step * work).reshape(cells, GZ)
    for q in range(5):
        for xl in range(2):
            for part in range(2):
                base = (q * BX + xl * PE + part * 8) * BY
                lines = [kicked_ref[pl.ds(base + b, 8, stride=BY), :] for b in range(BY)]
                rows = q * PE + part * 8
                for zl, value in enumerate(swap_groups(lines, PE)):
                    out_ref[owner_ref[xl * 8 + zl], rows : rows + 8, :] = value


def spread_kernel(place_ref, recv_ref, out_ref):
    shift = place_ref[0]
    live = lax.broadcasted_iota(jnp.int32, (CAP, 128), 0) < place_ref[1]
    for q in range(5):
        for tile in range(2 * PE):
            a, half = tile // 2, tile % 2
            lines = recv_ref[pl.ds(half * BRICK + q * PE + a, CAP, stride=2 * BRICK), :]
            turned = pltpu.roll(lines, shift, 0)
            out_ref[q, :, tile * 128 : (tile + 1) * 128] = jnp.where(live, turned, 0.0)


def call(kernel, outs, ins, scratch=()):
    shapes = [jax.ShapeDtypeStruct(s, jnp.float32) for s in outs]
    many = len(outs) > 1
    return pl.pallas_call(
        kernel,
        out_shape=tuple(shapes) if many else shapes[0],
        in_specs=[SM if i in ins[1] else VM for i in range(ins[0])],
        out_specs=tuple([VM] * len(outs)) if many else VM,
        scratch_shapes=[pltpu.VMEM(s, jnp.float32) for s in scratch],
        compiler_params=PARAMS,
    )


def gather_counts(counts):
    copies = jnp.broadcast_to(counts.reshape(1, 1, 1), (COLS, 1, 128))
    return lax.all_to_all(copies, "col", split_axis=0, concat_axis=0, tiled=True)[:, 0, 0]


def on_device(fields, counts):
    my_row = lax.axis_index("row")
    my_column = lax.axis_index("col")
    row_counts = gather_counts(counts)
    column_ids = jnp.arange(COLS, dtype=jnp.int32)
    starts = jnp.sum(
        jnp.where(column_ids[None, :] < column_ids[:, None], row_counts[None, :], 0), axis=1
    )
    own_start = jnp.sum(jnp.where(column_ids < my_column, row_counts, 0))
    y_patch = my_column // 2
    wanted = jnp.arange(LINES, dtype=jnp.int32) * 16 + y_patch
    owners = jnp.sum((starts[None, :] <= wanted[:, None]).astype(jnp.int32), axis=1) - 1
    turn = own_start % CAP

    sent = call(pack_kernel, [(COLS * BRICK, 128)], (2, (0,)))(
        turn.reshape(1), fields.transpose(1, 0, 2)
    )
    arrived = lax.all_to_all(
        sent.reshape(COLS, BRICK, 128), "col", split_axis=0, concat_axis=0, tiled=True
    )
    own, xfirst, xlast, yfirst, ylast = call(
        unpack_kernel,
        [
            (5, BX, BY, GZ),
            (5, HALO, BY, GZ),
            (5, HALO, BY, GZ),
            (5, BX, HALO, GZ),
            (5, BX, HALO, GZ),
        ],
        (2, (0,)),
        [(5 * BX * BY, GZ)],
    )(owners, arrived)

    def ring(count, step):
        return [(i, (i + step) % count) for i in range(count)]

    xlow = lax.ppermute(xlast, "row", ring(ROWS, 1))
    xhigh = lax.ppermute(xfirst, "row", ring(ROWS, -1))
    ylow = lax.ppermute(ylast, "col", ring(COLS, 1))
    yhigh = lax.ppermute(yfirst, "col", ring(COLS, -1))
    edges = jnp.concatenate([xlow[:, 2:4], xhigh[:, 0:2]], axis=1)
    clow = lax.ppermute(edges[:, :, BY - HALO :], "col", ring(COLS, 1))
    chigh = lax.ppermute(edges[:, :, :HALO], "col", ring(COLS, -1))

    table_z = hartley(GZ)
    table_x = hartley(GX)
    modes_of = np.arange(256) % GZ
    stepped, modes = call(
        euler_kernel,
        [(5, BX, BY, GZ), (512, 128)],
        (8, ()),
        [(5, BX + 2 * HALO, BY + 2 * HALO, GZ), (5, BX + 2 * HALO, BY + 2 * HALO, GZ), (BX * BY, GZ)],
    )(own, xlow, xhigh, ylow, yhigh, clow, chigh, jnp.asarray(table_z[modes_of]))
    planes = lax.all_to_all(
        modes.reshape(256, 2, 128), ("row", "col"), split_axis=0, concat_axis=0, tiled=True
    )
    place = my_row * COLS + my_column
    wave_z = place % GZ
    eig = eigenvalues(GX)
    eig_z = -4.0 * jnp.sin((math.pi / GZ) * wave_z.astype(jnp.float32)) ** 2
    strips = call(plane_kernel, [(768, 128)], (6, (0, 1)), [(2 * GY, 128), (2 * (GY + 16), 128)])(
        (place // GZ).reshape(1),
        eig_z.reshape(1),
        planes.reshape(512, 128),
        jnp.asarray(table_x),
        jnp.asarray(eig[None, :]),
        jnp.asarray(np.broadcast_to(eig[:, None], (GX, 128))),
    )
    strips = lax.all_to_all(
        strips.reshape(256, 3, 128), ("row", "col"), split_axis=0, concat_axis=0, tiled=True
    )
    returned = call(
        kick_kernel,
        [(COLS, BRICK, 128)],
        (4, (0,)),
        [((BX + 2) * BY, GZ), (5 * BX * BY, GZ)],
    )(owners, stepped, strips.reshape(768, 128), jnp.asarray(table_z[modes_of]))
    came_back = lax.all_to_all(returned, "col", split_axis=0, concat_axis=0, tiled=True)
    home = jnp.stack([(CAP - turn) % CAP, counts[0, 0]])
    result = call(spread_kernel, [(5, CAP, PE * PE * PE)], (2, (0,)))(
        home, came_back.reshape(COLS * BRICK, 128)
    )
    return result.transpose(1, 0, 2)


def solution(mesh):
    return jax.shard_map(
        on_device,
        mesh=mesh,
        in_specs=(P(("row", "col"), None, None), P("row", "col")),
        out_specs=P(("row", "col"), None, None),
        check_vma=False,
    )
```

```python
import math

import jax
import jax.numpy as jnp
import numpy as np
from jax import lax
from jax.experimental import pallas as pl
from jax.experimental.pallas import tpu as pltpu
from jax.sharding import PartitionSpec as P

PE = 16
GX = 256
GY = 256
GZ = 128
ROWS = 8
COLS = 32
BX = GX // ROWS
BY = GY // COLS
CAP = 16
LINES = 16
BRICK = 5 * PE
HALO = 4

time_step = 0.03
four_pi_g = 10.0

PARAMS = pltpu.CompilerParams(vmem_limit_bytes=40 * 2**20)
VM = pl.BlockSpec(memory_space=pltpu.VMEM)
SM = pl.BlockSpec(memory_space=pltpu.SMEM)


def hartley(length):
    index = np.arange(length)
    angle = 2.0 * np.pi / length * (index[:, None] * index[None, :] % length)
    return ((np.cos(angle) + np.sin(angle)) / math.sqrt(length)).astype(np.float32)


def eigenvalues(length):
    return (-4.0 * np.sin(np.pi * np.arange(length) / length) ** 2).astype(np.float32)


def dot(left, right, dims=((1,), (0,))):
    return lax.dot_general(
        left,
        right,
        (dims, ((), ())),
        precision=lax.Precision.HIGHEST,
        preferred_element_type=jnp.float32,
    )


def swap_groups(arrays, group):
    count = len(arrays)
    lane = lax.broadcasted_iota(jnp.int32, arrays[0].shape, 1) // group
    arrays = list(arrays)
    distance = count // 2
    while distance:
        upper = (lane & distance) != 0
        for i in range(count):
            if i & distance:
                continue
            low, high = arrays[i], arrays[i + distance]
            arrays[i] = jnp.where(upper, pltpu.roll(high, distance * group, 1), low)
            arrays[i + distance] = jnp.where(
                upper, high, pltpu.roll(low, 128 - distance * group, 1)
            )
        distance //= 2
    return arrays


def pack_kernel(start_ref, fields_ref, out_ref):
    shift = start_ref[0]
    for q in range(5):
        for tile in range(2 * PE):
            a, half = tile // 2, tile % 2
            slots = fields_ref[q, :, tile * 128 : (tile + 1) * 128]
            turned = pltpu.roll(slots, shift, 0)
            out_ref[pl.ds(half * BRICK + q * PE + a, CAP, stride=2 * BRICK), :] = turned


def unpack_kernel(owner_ref, recv_ref, own_ref, xfirst_ref, xlast_ref, yfirst_ref, ylast_ref, flat_ref):
    for q in range(5):
        for xl in range(2):
            for part in range(2):
                rows = q * PE + part * 8
                lines = [
                    recv_ref[owner_ref[xl * 8 + zl], rows : rows + 8, :] for zl in range(8)
                ]
                for b, value in enumerate(swap_groups(lines, PE)):
                    base = (q * BX + xl * PE + part * 8) * BY + b
                    flat_ref[pl.ds(base, 8, stride=BY), :] = value
    block = flat_ref[...].reshape(5, BX, BY, GZ)
    own_ref[...] = block
    xfirst_ref[...] = block[:, :HALO]
    xlast_ref[...] = block[:, BX - HALO :]
    yfirst_ref[...] = block[:, :, :HALO]
    ylast_ref[...] = block[:, :, BY - HALO :]


def minmod(p, q):
    return jnp.maximum(jnp.minimum(p, q), 0.0) + jnp.minimum(jnp.maximum(p, q), 0.0)


def half_flux(states, direction, sign):
    density, energy = states[0], states[4]
    inverse = 1.0 / density
    velocity = 0.5 * states[1 + direction] * inverse
    squares = states[1] * states[1] + states[2] * states[2] + states[3] * states[3]
    pressure = 0.4 * energy - (0.2 * squares) * inverse
    pieces = [0.5 * states[1 + direction]]
    for component in range(3):
        term = states[1 + component] * velocity
        if component == direction:
            term = term + 0.5 * pressure
        pieces.append(term)
    pieces.append((energy + pressure) * velocity)
    if sign > 0:
        return [piece + 2.0 * state for piece, state in zip(pieces, states)]
    return [piece - 2.0 * state for piece, state in zip(pieces, states)]


def edge_terms(states, slopes, direction):
    halves = [0.5 * slope for slope in slopes]
    upper = half_flux([u + h for u, h in zip(states, halves)], direction, 1)
    lower = half_flux([u - h for u, h in zip(states, halves)], direction, -1)
    return upper, lower


def line_change(states, direction, axis):
    size = states[0].shape[axis]
    gaps = [pltpu.roll(u, size - 1, axis) - u for u in states]
    slopes = [minmod(pltpu.roll(g, 1, axis), g) for g in gaps]
    upper, lower = edge_terms(states, slopes, direction)
    faces = [u + pltpu.roll(w, size - 1, axis) for u, w in zip(upper, lower)]
    return [f - pltpu.roll(f, 1, axis) for f in faces]


def euler_stage(load, store, first_row, count, keep):
    def slopes_of(low, mid, high):
        return [minmod(b - a, c - b) for a, b, c in zip(low, mid, high)]

    cut = lambda states: [u[:keep] for u in states]
    r0, r1, r2, r3 = [cut(load(first_row + k)) for k in (-2, -1, 0, 1)]
    upper_prev, _ = edge_terms(r1, slopes_of(r0, r1, r2), 0)
    upper_now, lower_now = edge_terms(r2, slopes_of(r1, r2, r3), 0)
    face = [u + w for u, w in zip(upper_prev, lower_now)]

    def step(k, carry):
        face_low, upper_here = carry
        i = first_row + k
        here, above, far = load(i), cut(load(i + 1)), cut(load(i + 2))
        mine = cut(here)
        upper_next, lower_next = edge_terms(above, slopes_of(mine, above, far), 0)
        face_high = [u + w for u, w in zip(upper_here, lower_next)]
        change = [h - l for h, l in zip(face_high, face_low)]
        along_y = cut(line_change(here, 1, 0))
        along_z = line_change(mine, 2, 1)
        rate = [-(a + b + c) for a, b, c in zip(change, along_y, along_z)]
        store(i, mine, rate)
        return tuple(face_high), tuple(upper_next)

    lax.fori_loop(0, count, step, (tuple(face), tuple(upper_now)), unroll=4)


def send_home(owner_ref, cells_ref, out_ref, fields):
    for q in range(fields):
        for xl in range(2):
            for part in range(2):
                base = (q * BX + xl * PE + part * 8) * BY
                lines = [cells_ref[pl.ds(base + b, 8, stride=BY), :] for b in range(BY)]
                rows = q * PE + part * 8
                for zl, value in enumerate(swap_groups(lines, PE)):
                    out_ref[owner_ref[xl * 8 + zl], rows : rows + 8, :] = value


def euler_kernel(
    owner_ref, own_ref, xlow_ref, xhigh_ref, ylow_ref, yhigh_ref, clow_ref, chigh_ref, table_ref,
    home_ref, modes_ref, ext_ref, first_ref, cells_ref,
):
    low, high = slice(BY + HALO, BY + 2 * HALO), slice(BY, BY + HALO)
    inner = slice(HALO, HALO + BX)
    ext_ref[:, inner, 0:BY] = own_ref[...]
    ext_ref[:, 0:HALO, 0:BY] = xlow_ref[...]
    ext_ref[:, HALO + BX :, 0:BY] = xhigh_ref[...]
    ext_ref[:, inner, high] = yhigh_ref[...]
    ext_ref[:, inner, low] = ylow_ref[...]
    for part, ref in ((low, clow_ref), (high, chigh_ref)):
        corner = ref[...]
        ext_ref[:, 0:2, part] = corner[:, 0:2]
        ext_ref[:, 2:4, part] = corner[:, 0:2]
        ext_ref[:, HALO + BX : HALO + BX + 2, part] = corner[:, 2:4]
        ext_ref[:, HALO + BX + 2 :, part] = corner[:, 2:4]

    def load_ext(i):
        return [ext_ref[q, i] for q in range(5)]

    def store_first(i, states, rates):
        for q in range(5):
            first_ref[q, i] = states[q] + time_step * rates[q]

    euler_stage(load_ext, store_first, 2, BX + 4, BY + 2 * HALO)

    def load_first(i):
        return [first_ref[q, i] for q in range(5)]

    def store_stepped(i, states, rates):
        for q in range(5):
            second = states[q] + time_step * rates[q]
            value = 0.5 * ext_ref[q, i, 0:BY] + 0.5 * second
            row = pl.multiple_of((q * BX + i - HALO) * BY, BY)
            cells_ref[pl.ds(row, BY), :] = value

    euler_stage(load_first, store_stepped, HALO, BX, BY)
    density = jnp.concatenate(
        [cells_ref[pl.ds(b, BX, stride=BY), :] for b in range(BY)], axis=0
    )
    spread = dot(table_ref[...], density, ((1,), (1,)))
    modes_ref[pl.ds(0, 256, stride=2), :] = spread[:, :128]
    modes_ref[pl.ds(1, 256, stride=2), :] = spread[:, 128:]
    send_home(owner_ref, cells_ref, home_ref, 5)


def plane_kernel(place_ref, wave_ref, modes_ref, table_ref, eigx_ref, eigy_ref, out_ref, plane_ref, wide_ref):
    for high in range(2):
        for tile in range(2):
            lines = [
                modes_ref[pl.ds((high * 4 + r) * COLS * 2 + tile, COLS, stride=2), :]
                for r in range(4)
            ]
            for p, value in enumerate(swap_groups(lines, 32)):
                plane_ref[pl.ds(high * GY + tile * 4 + p, COLS, stride=BY), :] = value
    half = pl.multiple_of(place_ref[0] * 128, 128)
    table = table_ref[...]
    half_table = table_ref[pl.ds(half, 128), :]
    plane = jnp.concatenate([plane_ref[0:GY, :], plane_ref[GY:, :]], axis=1)
    spectrum = dot(dot(half_table, plane), table)
    eigen = eigx_ref[...] + eigy_ref[pl.ds(half, 128), :][:, 0:1] + wave_ref[0]
    flat = eigen >= 0.0
    green = jnp.where(flat, 0.0, four_pi_g / jnp.where(flat, -1.0, eigen))
    back = dot(spectrum * green, table)
    potential = dot(half_table, back, ((0,), (0,)))
    for high in range(2):
        base, side = high * (GY + 16), potential[:, high * 128 : high * 128 + 128]
        wide_ref[base + 8 : base + 8 + GY, :] = side
        wide_ref[base : base + 8, :] = side[GY - 8 :]
        wide_ref[base + 8 + GY : base + 16 + GY, :] = side[:8]

    def strip(row):
        return jnp.concatenate(
            [wide_ref[pl.ds(b + row, COLS, stride=BY), :] for b in (0, GY + 16)], axis=1
        )

    strips = [strip(8 + yl) for yl in range(BY)]
    below, above = strip(7), strip(16)
    lane = lax.broadcasted_iota(jnp.int32, (COLS, GX), 1) % 32
    sides = jnp.zeros((COLS, GX), jnp.float32)
    for yl in range(BY):
        sides = jnp.where(lane == yl, pltpu.roll(strips[yl], 1 + yl, 1), sides)
        sides = jnp.where(lane == 8 + yl, pltpu.roll(strips[yl], GX - 24 + yl, 1), sides)
    strips = strips + [below, above, sides, sides]
    for high in range(2):
        for quad in range(3):
            lines = [s[:, high * 128 : high * 128 + 128] for s in strips[quad * 4 : quad * 4 + 4]]
            for p, value in enumerate(swap_groups(lines, 32)):
                out_ref[pl.ds((high * 4 + p) * COLS * 3 + quad, COLS, stride=3), :] = value


def gradient_kernel(owner_ref, modes_ref, table_ref, out_ref, phi_ref, cells_ref):
    table = table_ref[...]
    parts = []
    for quad in range(3):
        block = modes_ref[pl.ds(quad, 256, stride=3), :]
        parts.append(dot(block, table, ((0,), (0,))))
    for yl in range(BY):
        phi_ref[pl.ds(BY + yl, BX, stride=BY), :] = parts[yl // 4][(yl % 4) * 32 : (yl % 4) * 32 + 32]
    phi_ref[0:BY, :] = parts[2][64 : 64 + BY]
    phi_ref[BY + BX * BY :, :] = parts[2][64 + BY : 64 + 2 * BY]
    phi = phi_ref[...].reshape(BX + 2, BY, GZ)
    mid = phi[1 : 1 + BX]
    below = parts[2][0:32].reshape(BX, 1, GZ)
    above = parts[2][32:64].reshape(BX, 1, GZ)
    lower = jnp.concatenate([below, mid[:, : BY - 1]], axis=1)
    upper = jnp.concatenate([mid[:, 1:], above], axis=1)
    cells = BX * BY
    cells_ref[0:cells, :] = (0.5 * (phi[2:] - phi[:BX])).reshape(cells, GZ)
    cells_ref[cells : 2 * cells, :] = (0.5 * (upper - lower)).reshape(cells, GZ)
    turned = pltpu.roll(mid, GZ - 1, 2) - pltpu.roll(mid, 1, 2)
    cells_ref[2 * cells :, :] = (0.5 * turned).reshape(cells, GZ)
    send_home(owner_ref, cells_ref, out_ref, 3)


def kick_kernel(place_ref, state_ref, gradient_ref, out_ref):
    shift = place_ref[0]
    live = lax.broadcasted_iota(jnp.int32, (CAP, 128), 0) < place_ref[1]

    def rows(ref, fields, tile):
        a, half = tile // 2, tile % 2
        bricks = fields * PE
        return [
            ref[pl.ds(half * bricks + q * PE + a, CAP, stride=2 * bricks), :]
            for q in range(fields)
        ]

    for tile in range(2 * PE):
        density, mx, my, mz, energy = rows(state_ref, 5, tile)
        gx, gy, gz = rows(gradient_ref, 3, tile)
        pull = time_step * density
        energy = energy - time_step * (mx * gx + my * gy + mz * gz)
        kicked = (density, mx - pull * gx, my - pull * gy, mz - pull * gz, energy)
        for q in range(5):
            turned = pltpu.roll(kicked[q], shift, 0)
            out_ref[q, :, tile * 128 : (tile + 1) * 128] = jnp.where(live, turned, 0.0)


def call(kernel, outs, ins, scratch=()):
    shapes = [jax.ShapeDtypeStruct(s, jnp.float32) for s in outs]
    many = len(outs) > 1
    return pl.pallas_call(
        kernel,
        out_shape=tuple(shapes) if many else shapes[0],
        in_specs=[SM if i in ins[1] else VM for i in range(ins[0])],
        out_specs=tuple([VM] * len(outs)) if many else VM,
        scratch_shapes=[pltpu.VMEM(s, jnp.float32) for s in scratch],
        compiler_params=PARAMS,
    )


def gather_counts(counts):
    copies = jnp.broadcast_to(counts.reshape(1, 1, 1), (COLS, 1, 128))
    return lax.all_to_all(copies, "col", split_axis=0, concat_axis=0, tiled=True)[:, 0, 0]


def on_device(fields, counts):
    my_row = lax.axis_index("row")
    my_column = lax.axis_index("col")
    row_counts = gather_counts(counts)
    column_ids = jnp.arange(COLS, dtype=jnp.int32)
    starts = jnp.sum(
        jnp.where(column_ids[None, :] < column_ids[:, None], row_counts[None, :], 0), axis=1
    )
    own_start = jnp.sum(jnp.where(column_ids < my_column, row_counts, 0))
    y_patch = my_column // 2
    wanted = jnp.arange(LINES, dtype=jnp.int32) * 16 + y_patch
    owners = jnp.sum((starts[None, :] <= wanted[:, None]).astype(jnp.int32), axis=1) - 1
    turn = own_start % CAP

    sent = call(pack_kernel, [(COLS * BRICK, 128)], (2, (0,)))(
        turn.reshape(1), fields.transpose(1, 0, 2)
    )
    arrived = lax.all_to_all(
        sent.reshape(COLS, BRICK, 128), "col", split_axis=0, concat_axis=0, tiled=True
    )
    own, xfirst, xlast, yfirst, ylast = call(
        unpack_kernel,
        [
            (5, BX, BY, GZ),
            (5, HALO, BY, GZ),
            (5, HALO, BY, GZ),
            (5, BX, HALO, GZ),
            (5, BX, HALO, GZ),
        ],
        (2, (0,)),
        [(5 * BX * BY, GZ)],
    )(owners, arrived)

    def ring(count, step):
        return [(i, (i + step) % count) for i in range(count)]

    xlow = lax.ppermute(xlast, "row", ring(ROWS, 1))
    xhigh = lax.ppermute(xfirst, "row", ring(ROWS, -1))
    ylow = lax.ppermute(ylast, "col", ring(COLS, 1))
    yhigh = lax.ppermute(yfirst, "col", ring(COLS, -1))
    edges = jnp.concatenate([xlow[:, 2:4], xhigh[:, 0:2]], axis=1)
    clow = lax.ppermute(edges[:, :, BY - HALO :], "col", ring(COLS, 1))
    chigh = lax.ppermute(edges[:, :, :HALO], "col", ring(COLS, -1))

    table_z = hartley(GZ)
    table_x = hartley(GX)
    modes_of = np.arange(256) % GZ
    home, modes = call(
        euler_kernel,
        [(COLS, BRICK, 128), (512, 128)],
        (9, (0,)),
        [(5, BX + 2 * HALO, BY + 2 * HALO, GZ), (5, BX + 2 * HALO, BY + 2 * HALO, GZ), (5 * BX * BY, GZ)],
    )(owners, own, xlow, xhigh, ylow, yhigh, clow, chigh, jnp.asarray(table_z[modes_of]))
    state = lax.all_to_all(home, "col", split_axis=0, concat_axis=0, tiled=True)
    place = my_row * COLS + my_column
    wave_z = place % GZ
    eig = eigenvalues(GX)
    eig_z = -4.0 * jnp.sin((math.pi / GZ) * wave_z.astype(jnp.float32)) ** 2
    def poisson(step, strips):
        planes = lax.all_to_all(
            modes.reshape(256, 2, 128), ("row", "col"), split_axis=0, concat_axis=0, tiled=True
        )
        strips = call(plane_kernel, [(768, 128)], (6, (0, 1)), [(2 * GY, 128), (2 * (GY + 16), 128)])(
            (place // GZ).reshape(1),
            eig_z.reshape(1),
            planes.reshape(512, 128),
            jnp.asarray(table_x),
            jnp.asarray(eig[None, :]),
            jnp.asarray(np.broadcast_to(eig[:, None], (GX, 128))),
        )
        strips = lax.all_to_all(
            strips.reshape(256, 3, 128), ("row", "col"), split_axis=0, concat_axis=0, tiled=True
        )
        return strips

    strips = lax.fori_loop(0, jnp.minimum(counts[0, 0], 1), poisson, jnp.zeros((256, 3, 128), jnp.float32))
    pulls = call(
        gradient_kernel,
        [(COLS, 3 * PE, 128)],
        (3, (0,)),
        [((BX + 2) * BY, GZ), (3 * BX * BY, GZ)],
    )(owners, strips.reshape(768, 128), jnp.asarray(table_z[modes_of]))
    gradient = lax.all_to_all(pulls, "col", split_axis=0, concat_axis=0, tiled=True)
    result = call(kick_kernel, [(5, CAP, PE * PE * PE)], (3, (0,)))(
        jnp.stack([(CAP - turn) % CAP, counts[0, 0]]),
        state.reshape(COLS * BRICK, 128),
        gradient.reshape(COLS * 3 * PE, 128),
    )
    return result.transpose(1, 0, 2)


def solution(mesh):
    return jax.shard_map(
        on_device,
        mesh=mesh,
        in_specs=(P(("row", "col"), None, None), P("row", "col")),
        out_specs=P(("row", "col"), None, None),
        check_vma=False,
    )
```

```python
import math

import jax
import jax.numpy as jnp
import numpy as np
from jax import lax
from jax.experimental import pallas as pl
from jax.experimental.pallas import tpu as pltpu
from jax.sharding import PartitionSpec as P

PE = 16
GX = 256
GY = 256
GZ = 128
ROWS = 8
COLS = 32
BX = GX // ROWS
BY = GY // COLS
CAP = 16
LINES = 16
BRICK = 5 * PE
HALO = 4

time_step = 0.03
four_pi_g = 10.0

PARAMS = pltpu.CompilerParams(vmem_limit_bytes=40 * 2**20)
VM = pl.BlockSpec(memory_space=pltpu.VMEM)
SM = pl.BlockSpec(memory_space=pltpu.SMEM)


def hartley(length):
    index = np.arange(length)
    angle = 2.0 * np.pi / length * (index[:, None] * index[None, :] % length)
    return ((np.cos(angle) + np.sin(angle)) / math.sqrt(length)).astype(np.float32)


def eigenvalues(length):
    return (-4.0 * np.sin(np.pi * np.arange(length) / length) ** 2).astype(np.float32)


def dot(left, right, dims=((1,), (0,))):
    return lax.dot_general(
        left,
        right,
        (dims, ((), ())),
        precision=lax.Precision.HIGHEST,
        preferred_element_type=jnp.float32,
    )


def swap_groups(arrays, group):
    count = len(arrays)
    lane = lax.broadcasted_iota(jnp.int32, arrays[0].shape, 1) // group
    arrays = list(arrays)
    distance = count // 2
    while distance:
        upper = (lane & distance) != 0
        for i in range(count):
            if i & distance:
                continue
            low, high = arrays[i], arrays[i + distance]
            arrays[i] = jnp.where(upper, pltpu.roll(high, distance * group, 1), low)
            arrays[i + distance] = jnp.where(
                upper, high, pltpu.roll(low, 128 - distance * group, 1)
            )
        distance //= 2
    return arrays


def stage_kernel(fields_ref, out_ref):
    for q in range(5):
        for tile in range(2 * PE):
            a, half = tile // 2, tile % 2
            slots = fields_ref[q, :, tile * 128 : (tile + 1) * 128]
            out_ref[pl.ds(half * BRICK + q * PE + a, CAP, stride=2 * BRICK), :] = slots


def turn_kernel(column_ref, counts_ref, staged_ref, out_ref):
    counts = counts_ref[...].reshape(COLS, 128)
    before = lax.broadcasted_iota(jnp.int32, (COLS, 128), 0) < column_ref[0]
    start = (jnp.sum(jnp.where(before, counts, 0.0)) * (1.0 / 128.0)).astype(jnp.int32)
    size = 2 * BRICK
    for y in range(CAP):
        source = pl.multiple_of(((y - start) & (CAP - 1)) * size, 8)
        out_ref[y * size : (y + 1) * size, :] = staged_ref[pl.ds(source, size), :]


def unpack_kernel(owner_ref, recv_ref, own_ref, xfirst_ref, xlast_ref, yfirst_ref, ylast_ref, flat_ref):
    for q in range(5):
        for xl in range(2):
            for part in range(2):
                rows = q * PE + part * 8
                lines = [
                    recv_ref[owner_ref[xl * 8 + zl], rows : rows + 8, :] for zl in range(8)
                ]
                for b, value in enumerate(swap_groups(lines, PE)):
                    base = (q * BX + xl * PE + part * 8) * BY + b
                    flat_ref[pl.ds(base, 8, stride=BY), :] = value
    block = flat_ref[...].reshape(5, BX, BY, GZ)
    own_ref[...] = block
    xfirst_ref[...] = block[:, :HALO]
    xlast_ref[...] = block[:, BX - HALO :]
    yfirst_ref[...] = block[:, :, :HALO]
    ylast_ref[...] = block[:, :, BY - HALO :]


def minmod(p, q):
    return jnp.maximum(jnp.minimum(p, q), 0.0) + jnp.minimum(jnp.maximum(p, q), 0.0)


def half_flux(states, direction, sign):
    density, energy = states[0], states[4]
    inverse = 1.0 / density
    velocity = 0.5 * states[1 + direction] * inverse
    squares = states[1] * states[1] + states[2] * states[2] + states[3] * states[3]
    pressure = 0.4 * energy - (0.2 * squares) * inverse
    pieces = [0.5 * states[1 + direction]]
    for component in range(3):
        term = states[1 + component] * velocity
        if component == direction:
            term = term + 0.5 * pressure
        pieces.append(term)
    pieces.append((energy + pressure) * velocity)
    if sign > 0:
        return [piece + 2.0 * state for piece, state in zip(pieces, states)]
    return [piece - 2.0 * state for piece, state in zip(pieces, states)]


def edge_terms(states, slopes, direction):
    halves = [0.5 * slope for slope in slopes]
    upper = half_flux([u + h for u, h in zip(states, halves)], direction, 1)
    lower = half_flux([u - h for u, h in zip(states, halves)], direction, -1)
    return upper, lower


def line_change(states, direction, axis):
    size = states[0].shape[axis]
    gaps = [pltpu.roll(u, size - 1, axis) - u for u in states]
    slopes = [minmod(pltpu.roll(g, 1, axis), g) for g in gaps]
    upper, lower = edge_terms(states, slopes, direction)
    faces = [u + pltpu.roll(w, size - 1, axis) for u, w in zip(upper, lower)]
    return [f - pltpu.roll(f, 1, axis) for f in faces]


def euler_stage(load, store, first_row, count, keep):
    def slopes_of(low, mid, high):
        return [minmod(b - a, c - b) for a, b, c in zip(low, mid, high)]

    cut = lambda states: [u[:keep] for u in states]
    r0, r1, r2, r3 = [cut(load(first_row + k)) for k in (-2, -1, 0, 1)]
    upper_prev, _ = edge_terms(r1, slopes_of(r0, r1, r2), 0)
    upper_now, lower_now = edge_terms(r2, slopes_of(r1, r2, r3), 0)
    face = [u + w for u, w in zip(upper_prev, lower_now)]

    def step(k, carry):
        face_low, upper_here = carry
        i = first_row + k
        here, above, far = load(i), cut(load(i + 1)), cut(load(i + 2))
        mine = cut(here)
        upper_next, lower_next = edge_terms(above, slopes_of(mine, above, far), 0)
        face_high = [u + w for u, w in zip(upper_here, lower_next)]
        change = [h - l for h, l in zip(face_high, face_low)]
        along_y = cut(line_change(here, 1, 0))
        along_z = line_change(mine, 2, 1)
        rate = [-(a + b + c) for a, b, c in zip(change, along_y, along_z)]
        store(i, mine, rate)
        return tuple(face_high), tuple(upper_next)

    lax.fori_loop(0, count, step, (tuple(face), tuple(upper_now)), unroll=4)


def euler_kernel(
    own_ref, xlow_ref, xhigh_ref, ylow_ref, yhigh_ref, clow_ref, chigh_ref, table_ref,
    stepped_ref, modes_ref, ext_ref, first_ref, flat_ref,
):
    low, high = slice(BY + HALO, BY + 2 * HALO), slice(BY, BY + HALO)
    inner = slice(HALO, HALO + BX)
    ext_ref[:, inner, 0:BY] = own_ref[...]
    ext_ref[:, 0:HALO, 0:BY] = xlow_ref[...]
    ext_ref[:, HALO + BX :, 0:BY] = xhigh_ref[...]
    ext_ref[:, inner, high] = yhigh_ref[...]
    ext_ref[:, inner, low] = ylow_ref[...]
    for part, ref in ((low, clow_ref), (high, chigh_ref)):
        corner = ref[...]
        ext_ref[:, 0:2, part] = corner[:, 0:2]
        ext_ref[:, 2:4, part] = corner[:, 0:2]
        ext_ref[:, HALO + BX : HALO + BX + 2, part] = corner[:, 2:4]
        ext_ref[:, HALO + BX + 2 :, part] = corner[:, 2:4]

    def load_ext(i):
        return [ext_ref[q, i] for q in range(5)]

    def store_first(i, states, rates):
        for q in range(5):
            first_ref[q, i] = states[q] + time_step * rates[q]

    euler_stage(load_ext, store_first, 2, BX + 4, BY + 2 * HALO)

    def load_first(i):
        return [first_ref[q, i] for q in range(5)]

    def store_stepped(i, states, rates):
        for q in range(5):
            second = states[q] + time_step * rates[q]
            value = 0.5 * ext_ref[q, i, 0:BY] + 0.5 * second
            stepped_ref[q, i - HALO] = value
            if q == 0:
                flat_ref[pl.ds(pl.multiple_of((i - HALO) * BY, BY), BY), :] = value

    euler_stage(load_first, store_stepped, HALO, BX, BY)
    density = jnp.concatenate(
        [flat_ref[pl.ds(b, BX, stride=BY), :] for b in range(BY)], axis=0
    )
    spread = dot(table_ref[...], density, ((1,), (1,)))
    modes_ref[pl.ds(0, 256, stride=2), :] = spread[:, :128]
    modes_ref[pl.ds(1, 256, stride=2), :] = spread[:, 128:]


def plane_kernel(place_ref, wave_ref, modes_ref, table_ref, eigx_ref, eigy_ref, out_ref, plane_ref, wide_ref):
    for high in range(2):
        for tile in range(2):
            lines = [
                modes_ref[pl.ds((high * 4 + r) * COLS * 2 + tile, COLS, stride=2), :]
                for r in range(4)
            ]
            for p, value in enumerate(swap_groups(lines, 32)):
                plane_ref[pl.ds(high * GY + tile * 4 + p, COLS, stride=BY), :] = value
    half = pl.multiple_of(place_ref[0] * 128, 128)
    table = table_ref[...]
    half_table = table_ref[pl.ds(half, 128), :]
    plane = jnp.concatenate([plane_ref[0:GY, :], plane_ref[GY:, :]], axis=1)
    spectrum = dot(dot(half_table, plane), table)
    eigen = eigx_ref[...] + eigy_ref[pl.ds(half, 128), :][:, 0:1] + wave_ref[0]
    flat = eigen >= 0.0
    green = jnp.where(flat, 0.0, four_pi_g / jnp.where(flat, -1.0, eigen))
    back = dot(spectrum * green, table)
    potential = dot(half_table, back, ((0,), (0,)))
    for high in range(2):
        base, side = high * (GY + 16), potential[:, high * 128 : high * 128 + 128]
        wide_ref[base + 8 : base + 8 + GY, :] = side
        wide_ref[base : base + 8, :] = side[GY - 8 :]
        wide_ref[base + 8 + GY : base + 16 + GY, :] = side[:8]

    def strip(row):
        return jnp.concatenate(
            [wide_ref[pl.ds(b + row, COLS, stride=BY), :] for b in (0, GY + 16)], axis=1
        )

    strips = [strip(8 + yl) for yl in range(BY)]
    below, above = strip(7), strip(16)
    lane = lax.broadcasted_iota(jnp.int32, (COLS, GX), 1) % 32
    sides = jnp.zeros((COLS, GX), jnp.float32)
    for yl in range(BY):
        sides = jnp.where(lane == yl, pltpu.roll(strips[yl], 1 + yl, 1), sides)
        sides = jnp.where(lane == 8 + yl, pltpu.roll(strips[yl], GX - 24 + yl, 1), sides)
    strips = strips + [below, above, sides, sides]
    for high in range(2):
        for quad in range(3):
            lines = [s[:, high * 128 : high * 128 + 128] for s in strips[quad * 4 : quad * 4 + 4]]
            for p, value in enumerate(swap_groups(lines, 32)):
                out_ref[pl.ds((high * 4 + p) * COLS * 3 + quad, COLS, stride=3), :] = value


def kick_kernel(owner_ref, stepped_ref, modes_ref, table_ref, out_ref, phi_ref, kicked_ref):
    table = table_ref[...]
    parts = []
    for quad in range(3):
        block = modes_ref[pl.ds(quad, 256, stride=3), :]
        parts.append(dot(block, table, ((0,), (0,))))
    for yl in range(BY):
        phi_ref[pl.ds(BY + yl, BX, stride=BY), :] = parts[yl // 4][(yl % 4) * 32 : (yl % 4) * 32 + 32]
    phi_ref[0:BY, :] = parts[2][64 : 64 + BY]
    phi_ref[BY + BX * BY :, :] = parts[2][64 + BY : 64 + 2 * BY]
    phi = phi_ref[...].reshape(BX + 2, BY, GZ)
    mid = phi[1 : 1 + BX]
    below = parts[2][0:32].reshape(BX, 1, GZ)
    above = parts[2][32:64].reshape(BX, 1, GZ)
    grad_x = 0.5 * (phi[2:] - phi[:BX])
    lower = jnp.concatenate([below, mid[:, : BY - 1]], axis=1)
    upper = jnp.concatenate([mid[:, 1:], above], axis=1)
    grad_y = 0.5 * (upper - lower)
    grad_z = 0.5 * (pltpu.roll(mid, GZ - 1, 2) - pltpu.roll(mid, 1, 2))
    grads = (grad_x, grad_y, grad_z)
    density = stepped_ref[0]
    momenta = [stepped_ref[1 + d] for d in range(3)]
    work = momenta[0] * grad_x + momenta[1] * grad_y + momenta[2] * grad_z
    cells = BX * BY
    kicked_ref[0:cells, :] = density.reshape(cells, GZ)
    for d in range(3):
        value = momenta[d] - time_step * density * grads[d]
        kicked_ref[(1 + d) * cells : (2 + d) * cells, :] = value.reshape(cells, GZ)
    kicked_ref[4 * cells :, :] = (stepped_ref[4] - time_step * work).reshape(cells, GZ)
    for q in range(5):
        for xl in range(2):
            for part in range(2):
                base = (q * BX + xl * PE + part * 8) * BY
                lines = [kicked_ref[pl.ds(base + b, 8, stride=BY), :] for b in range(BY)]
                rows = q * PE + part * 8
                for zl, value in enumerate(swap_groups(lines, PE)):
                    out_ref[owner_ref[xl * 8 + zl], rows : rows + 8, :] = value


def spread_kernel(place_ref, recv_ref, out_ref):
    shift = place_ref[0]
    live = lax.broadcasted_iota(jnp.int32, (CAP, 128), 0) < place_ref[1]
    for q in range(5):
        for tile in range(2 * PE):
            a, half = tile // 2, tile % 2
            lines = recv_ref[pl.ds(half * BRICK + q * PE + a, CAP, stride=2 * BRICK), :]
            turned = pltpu.roll(lines, shift, 0)
            out_ref[q, :, tile * 128 : (tile + 1) * 128] = jnp.where(live, turned, 0.0)


def call(kernel, outs, ins, scratch=()):
    shapes = [jax.ShapeDtypeStruct(s, jnp.float32) for s in outs]
    many = len(outs) > 1
    return pl.pallas_call(
        kernel,
        out_shape=tuple(shapes) if many else shapes[0],
        in_specs=[SM if i in ins[1] else VM for i in range(ins[0])],
        out_specs=tuple([VM] * len(outs)) if many else VM,
        scratch_shapes=[pltpu.VMEM(s, jnp.float32) for s in scratch],
        compiler_params=PARAMS,
    )


def gather_counts(counts):
    copies = jnp.broadcast_to(counts.astype(jnp.float32).reshape(1, 1, 1), (COLS, 1, 128))
    return lax.all_to_all(copies, "col", split_axis=0, concat_axis=0, tiled=True)


def on_device(fields, counts):
    my_row = lax.axis_index("row")
    my_column = lax.axis_index("col")
    staged = call(stage_kernel, [(COLS * BRICK, 128)], (1, ()))(fields.transpose(1, 0, 2))
    spread_counts = gather_counts(counts)
    row_counts = spread_counts[:, 0, 0].astype(jnp.int32)
    column_ids = jnp.arange(COLS, dtype=jnp.int32)
    starts = jnp.sum(
        jnp.where(column_ids[None, :] < column_ids[:, None], row_counts[None, :], 0), axis=1
    )
    own_start = jnp.sum(jnp.where(column_ids < my_column, row_counts, 0))
    y_patch = my_column // 2
    wanted = jnp.arange(LINES, dtype=jnp.int32) * 16 + y_patch
    owners = jnp.sum((starts[None, :] <= wanted[:, None]).astype(jnp.int32), axis=1) - 1
    turn = own_start % CAP

    sent = call(turn_kernel, [(COLS * BRICK, 128)], (3, (0,)))(
        my_column.reshape(1), spread_counts, staged
    )
    arrived = lax.all_to_all(
        sent.reshape(COLS, BRICK, 128), "col", split_axis=0, concat_axis=0, tiled=True
    )
    own, xfirst, xlast, yfirst, ylast = call(
        unpack_kernel,
        [
            (5, BX, BY, GZ),
            (5, HALO, BY, GZ),
            (5, HALO, BY, GZ),
            (5, BX, HALO, GZ),
            (5, BX, HALO, GZ),
        ],
        (2, (0,)),
        [(5 * BX * BY, GZ)],
    )(owners, arrived)

    def ring(count, step):
        return [(i, (i + step) % count) for i in range(count)]

    xlow = lax.ppermute(xlast, "row", ring(ROWS, 1))
    xhigh = lax.ppermute(xfirst, "row", ring(ROWS, -1))
    ylow = lax.ppermute(ylast, "col", ring(COLS, 1))
    yhigh = lax.ppermute(yfirst, "col", ring(COLS, -1))
    edges = jnp.concatenate([xlow[:, 2:4], xhigh[:, 0:2]], axis=1)
    clow = lax.ppermute(edges[:, :, BY - HALO :], "col", ring(COLS, 1))
    chigh = lax.ppermute(edges[:, :, :HALO], "col", ring(COLS, -1))

    table_z = hartley(GZ)
    table_x = hartley(GX)
    modes_of = np.arange(256) % GZ
    stepped, modes = call(
        euler_kernel,
        [(5, BX, BY, GZ), (512, 128)],
        (8, ()),
        [(5, BX + 2 * HALO, BY + 2 * HALO, GZ), (5, BX + 2 * HALO, BY + 2 * HALO, GZ), (BX * BY, GZ)],
    )(own, xlow, xhigh, ylow, yhigh, clow, chigh, jnp.asarray(table_z[modes_of]))
    planes = lax.all_to_all(
        modes.reshape(256, 2, 128), ("row", "col"), split_axis=0, concat_axis=0, tiled=True
    )
    place = my_row * COLS + my_column
    wave_z = place % GZ
    eig = eigenvalues(GX)
    eig_z = -4.0 * jnp.sin((math.pi / GZ) * wave_z.astype(jnp.float32)) ** 2
    strips = call(plane_kernel, [(768, 128)], (6, (0, 1)), [(2 * GY, 128), (2 * (GY + 16), 128)])(
        (place // GZ).reshape(1),
        eig_z.reshape(1),
        planes.reshape(512, 128),
        jnp.asarray(table_x),
        jnp.asarray(eig[None, :]),
        jnp.asarray(np.broadcast_to(eig[:, None], (GX, 128))),
    )
    strips = lax.all_to_all(
        strips.reshape(256, 1, 384), ("row", "col"), split_axis=0, concat_axis=0, tiled=True
    )
    returned = call(
        kick_kernel,
        [(COLS, BRICK, 128)],
        (4, (0,)),
        [((BX + 2) * BY, GZ), (5 * BX * BY, GZ)],
    )(owners, stepped, strips.reshape(768, 128), jnp.asarray(table_z[modes_of]))
    came_back = lax.all_to_all(returned, "col", split_axis=0, concat_axis=0, tiled=True)
    home = jnp.stack([(CAP - turn) % CAP, counts[0, 0]])
    result = call(spread_kernel, [(5, CAP, PE * PE * PE)], (2, (0,)))(
        home, came_back.reshape(COLS * BRICK, 128)
    )
    return result.transpose(1, 0, 2)


def solution(mesh):
    return jax.shard_map(
        on_device,
        mesh=mesh,
        in_specs=(P(("row", "col"), None, None), P("row", "col")),
        out_specs=P(("row", "col"), None, None),
        check_vma=False,
    )
```

```python
import math

import jax
import jax.numpy as jnp
import numpy as np
from jax import lax
from jax.experimental import pallas as pl
from jax.experimental.pallas import tpu as pltpu
from jax.sharding import PartitionSpec as P

PE = 16
GX = 256
GY = 256
GZ = 128
ROWS = 8
COLS = 32
BX = GX // ROWS
BY = GY // COLS
CAP = 16
LINES = 16
BRICK = 5 * PE
HALO = 4

time_step = 0.03
four_pi_g = 10.0

PARAMS = pltpu.CompilerParams(vmem_limit_bytes=16 * 2**20)
VM = pl.BlockSpec(memory_space=pltpu.VMEM)
SM = pl.BlockSpec(memory_space=pltpu.SMEM)


def hartley(length):
    index = np.arange(length)
    angle = 2.0 * np.pi / length * (index[:, None] * index[None, :] % length)
    return ((np.cos(angle) + np.sin(angle)) / math.sqrt(length)).astype(np.float32)


def eigenvalues(length):
    return (-4.0 * np.sin(np.pi * np.arange(length) / length) ** 2).astype(np.float32)


def dot(left, right, dims=((1,), (0,))):
    return lax.dot_general(
        left,
        right,
        (dims, ((), ())),
        precision=lax.Precision.HIGHEST,
        preferred_element_type=jnp.float32,
    )


def swap_groups(arrays, group):
    count = len(arrays)
    lane = lax.broadcasted_iota(jnp.int32, arrays[0].shape, 1) // group
    arrays = list(arrays)
    distance = count // 2
    while distance:
        upper = (lane & distance) != 0
        for i in range(count):
            if i & distance:
                continue
            low, high = arrays[i], arrays[i + distance]
            arrays[i] = jnp.where(upper, pltpu.roll(high, distance * group, 1), low)
            arrays[i + distance] = jnp.where(
                upper, high, pltpu.roll(low, 128 - distance * group, 1)
            )
        distance //= 2
    return arrays


def stage_kernel(fields_ref, out_ref):
    for q in range(5):
        for tile in range(2 * PE):
            a, half = tile // 2, tile % 2
            slots = fields_ref[q, :, tile * 128 : (tile + 1) * 128]
            out_ref[pl.ds(half * BRICK + q * PE + a, CAP, stride=2 * BRICK), :] = slots


def turn_kernel(column_ref, counts_ref, staged_ref, out_ref):
    counts = counts_ref[...].reshape(COLS, 128)
    before = lax.broadcasted_iota(jnp.int32, (COLS, 128), 0) < column_ref[0]
    start = (jnp.sum(jnp.where(before, counts, 0.0)) * (1.0 / 128.0)).astype(jnp.int32)
    size = 2 * BRICK
    for y in range(CAP):
        source = pl.multiple_of(((y - start) & (CAP - 1)) * size, 8)
        out_ref[y * size : (y + 1) * size, :] = staged_ref[pl.ds(source, size), :]


def unpack_kernel(owner_ref, recv_ref, own_ref, xfirst_ref, xlast_ref, yfirst_ref, ylast_ref, flat_ref):
    for q in range(5):
        for xl in range(2):
            for part in range(2):
                rows = q * PE + part * 8
                lines = [
                    recv_ref[owner_ref[xl * 8 + zl], rows : rows + 8, :] for zl in range(8)
                ]
                for b, value in enumerate(swap_groups(lines, PE)):
                    base = (q * BX + xl * PE + part * 8) * BY + b
                    flat_ref[pl.ds(base, 8, stride=BY), :] = value
    block = flat_ref[...].reshape(5, BX, BY, GZ)
    own_ref[...] = block
    xfirst_ref[...] = block[:, :HALO]
    xlast_ref[...] = block[:, BX - HALO :]
    yfirst_ref[...] = block[:, :, :HALO]
    ylast_ref[...] = block[:, :, BY - HALO :]


def minmod(p, q):
    return jnp.maximum(jnp.minimum(p, q), 0.0) + jnp.minimum(jnp.maximum(p, q), 0.0)


def half_flux(states, direction, sign):
    if len(states) == 2:
        return [0.5 * states[1] + sign * 2.0 * states[0]]
    density, energy = states[0], states[4]
    inverse = 1.0 / density
    velocity = 0.5 * states[1 + direction] * inverse
    squares = states[1] * states[1] + states[2] * states[2] + states[3] * states[3]
    pressure = 0.4 * energy - (0.2 * squares) * inverse
    pieces = [0.5 * states[1 + direction]]
    for component in range(3):
        term = states[1 + component] * velocity
        if component == direction:
            term = term + 0.5 * pressure
        pieces.append(term)
    pieces.append((energy + pressure) * velocity)
    if sign > 0:
        return [piece + 2.0 * state for piece, state in zip(pieces, states)]
    return [piece - 2.0 * state for piece, state in zip(pieces, states)]


def edge_terms(states, slopes, direction):
    halves = [0.5 * slope for slope in slopes]
    upper = half_flux([u + h for u, h in zip(states, halves)], direction, 1)
    lower = half_flux([u - h for u, h in zip(states, halves)], direction, -1)
    return upper, lower


def line_change(states, direction, axis):
    size = states[0].shape[axis]
    gaps = [pltpu.roll(u, size - 1, axis) - u for u in states]
    slopes = [minmod(pltpu.roll(g, 1, axis), g) for g in gaps]
    upper, lower = edge_terms(states, slopes, direction)
    faces = [u + pltpu.roll(w, size - 1, axis) for u, w in zip(upper, lower)]
    return [f - pltpu.roll(f, 1, axis) for f in faces]


def all_fields(states, direction):
    return states


def mass_fields(states, direction):
    return [states[0], states[1 + direction]]


def euler_stage(load, store, first_row, count, keep, pick=all_fields):
    def slopes_of(low, mid, high):
        return [minmod(b - a, c - b) for a, b, c in zip(low, mid, high)]

    cut = lambda states: [u[:keep] for u in states]
    cut_x = lambda states: cut(pick(states, 0))
    r0, r1, r2, r3 = [cut_x(load(first_row + k)) for k in (-2, -1, 0, 1)]
    upper_prev, _ = edge_terms(r1, slopes_of(r0, r1, r2), 0)
    upper_now, lower_now = edge_terms(r2, slopes_of(r1, r2, r3), 0)
    face = [u + w for u, w in zip(upper_prev, lower_now)]

    def step(k, carry):
        face_low, upper_here = carry
        i = first_row + k
        here, above, far = load(i), cut_x(load(i + 1)), cut_x(load(i + 2))
        mine = cut(here)
        upper_next, lower_next = edge_terms(above, slopes_of(pick(mine, 0), above, far), 0)
        face_high = [u + w for u, w in zip(upper_here, lower_next)]
        change = [h - l for h, l in zip(face_high, face_low)]
        along_y = cut(line_change(pick(here, 1), 1, 0))
        along_z = line_change(pick(mine, 2), 2, 1)
        rate = [-(a + b + c) for a, b, c in zip(change, along_y, along_z)]
        store(i, mine, rate)
        return tuple(face_high), tuple(upper_next)

    lax.fori_loop(0, count, step, (tuple(face), tuple(upper_now)), unroll=4)


def euler_kernel(
    own_ref, xlow_ref, xhigh_ref, ylow_ref, yhigh_ref, clow_ref, chigh_ref, table_ref,
    first_ref, modes_ref, ext_ref, flat_ref,
):
    low, high = slice(BY + HALO, BY + 2 * HALO), slice(BY, BY + HALO)
    inner = slice(HALO, HALO + BX)
    ext_ref[:, inner, 0:BY] = own_ref[...]
    ext_ref[:, 0:HALO, 0:BY] = xlow_ref[...]
    ext_ref[:, HALO + BX :, 0:BY] = xhigh_ref[...]
    ext_ref[:, inner, high] = yhigh_ref[...]
    ext_ref[:, inner, low] = ylow_ref[...]
    for part, ref in ((low, clow_ref), (high, chigh_ref)):
        corner = ref[...]
        ext_ref[:, 0:2, part] = corner[:, 0:2]
        ext_ref[:, 2:4, part] = corner[:, 0:2]
        ext_ref[:, HALO + BX : HALO + BX + 2, part] = corner[:, 2:4]
        ext_ref[:, HALO + BX + 2 :, part] = corner[:, 2:4]

    def load_ext(i):
        return [ext_ref[q, i] for q in range(5)]

    def store_first(i, states, rates):
        for q in range(5):
            first_ref[q, i] = states[q] + time_step * rates[q]

    euler_stage(load_ext, store_first, 2, BX + 4, BY + 2 * HALO)

    def load_mass(i):
        return [first_ref[q, i] for q in range(4)]

    def store_density(i, states, rates):
        second = states[0] + time_step * rates[0]
        row = pl.multiple_of((i - HALO) * BY, BY)
        flat_ref[pl.ds(row, BY), :] = 0.5 * ext_ref[0, i, 0:BY] + 0.5 * second

    euler_stage(load_mass, store_density, HALO, BX, BY, mass_fields)
    density = jnp.concatenate(
        [flat_ref[pl.ds(b, BX, stride=BY), :] for b in range(BY)], axis=0
    )
    spread = dot(table_ref[...], density, ((1,), (1,)))
    modes_ref[pl.ds(0, 256, stride=2), :] = spread[:, :128]
    modes_ref[pl.ds(1, 256, stride=2), :] = spread[:, 128:]


def second_kernel(own_ref, first_ref, stepped_ref):
    def load_first(i):
        return [first_ref[q, i] for q in range(5)]

    def store_stepped(i, states, rates):
        for q in range(5):
            second = states[q] + time_step * rates[q]
            stepped_ref[q, i - HALO] = 0.5 * own_ref[q, i - HALO] + 0.5 * second

    euler_stage(load_first, store_stepped, HALO, BX, BY)


def plane_kernel(place_ref, wave_ref, modes_ref, table_ref, eigx_ref, eigy_ref, out_ref, plane_ref, wide_ref):
    for high in range(2):
        for tile in range(2):
            lines = [
                modes_ref[pl.ds((high * 4 + r) * COLS * 2 + tile, COLS, stride=2), :]
                for r in range(4)
            ]
            for p, value in enumerate(swap_groups(lines, 32)):
                plane_ref[pl.ds(high * GY + tile * 4 + p, COLS, stride=BY), :] = value
    half = pl.multiple_of(place_ref[0] * 128, 128)
    table = table_ref[...]
    half_table = table_ref[pl.ds(half, 128), :]
    plane = jnp.concatenate([plane_ref[0:GY, :], plane_ref[GY:, :]], axis=1)
    spectrum = dot(dot(half_table, plane), table)
    eigen = eigx_ref[...] + eigy_ref[pl.ds(half, 128), :][:, 0:1] + wave_ref[0]
    flat = eigen >= 0.0
    green = jnp.where(flat, 0.0, four_pi_g / jnp.where(flat, -1.0, eigen))
    back = dot(spectrum * green, table)
    potential = dot(half_table, back, ((0,), (0,)))
    for high in range(2):
        base, side = high * (GY + 16), potential[:, high * 128 : high * 128 + 128]
        wide_ref[base + 8 : base + 8 + GY, :] = side
        wide_ref[base : base + 8, :] = side[GY - 8 :]
        wide_ref[base + 8 + GY : base + 16 + GY, :] = side[:8]

    def strip(row):
        return jnp.concatenate(
            [wide_ref[pl.ds(b + row, COLS, stride=BY), :] for b in (0, GY + 16)], axis=1
        )

    strips = [strip(8 + yl) for yl in range(BY)]
    below, above = strip(7), strip(16)
    lane = lax.broadcasted_iota(jnp.int32, (COLS, GX), 1) % 32
    sides = jnp.zeros((COLS, GX), jnp.float32)
    for yl in range(BY):
        sides = jnp.where(lane == yl, pltpu.roll(strips[yl], 1 + yl, 1), sides)
        sides = jnp.where(lane == 8 + yl, pltpu.roll(strips[yl], GX - 24 + yl, 1), sides)
    strips = strips + [below, above, sides, sides]
    for high in range(2):
        for quad in range(3):
            lines = [s[:, high * 128 : high * 128 + 128] for s in strips[quad * 4 : quad * 4 + 4]]
            for p, value in enumerate(swap_groups(lines, 32)):
                out_ref[pl.ds((high * 4 + p) * COLS * 3 + quad, COLS, stride=3), :] = value


def kick_kernel(owner_ref, stepped_ref, modes_ref, table_ref, out_ref, phi_ref, kicked_ref):
    table = table_ref[...]
    parts = []
    for quad in range(3):
        block = modes_ref[pl.ds(quad, 256, stride=3), :]
        parts.append(dot(block, table, ((0,), (0,))))
    for yl in range(BY):
        phi_ref[pl.ds(BY + yl, BX, stride=BY), :] = parts[yl // 4][(yl % 4) * 32 : (yl % 4) * 32 + 32]
    phi_ref[0:BY, :] = parts[2][64 : 64 + BY]
    phi_ref[BY + BX * BY :, :] = parts[2][64 + BY : 64 + 2 * BY]
    phi = phi_ref[...].reshape(BX + 2, BY, GZ)
    mid = phi[1 : 1 + BX]
    below = parts[2][0:32].reshape(BX, 1, GZ)
    above = parts[2][32:64].reshape(BX, 1, GZ)
    grad_x = 0.5 * (phi[2:] - phi[:BX])
    lower = jnp.concatenate([below, mid[:, : BY - 1]], axis=1)
    upper = jnp.concatenate([mid[:, 1:], above], axis=1)
    grad_y = 0.5 * (upper - lower)
    grad_z = 0.5 * (pltpu.roll(mid, GZ - 1, 2) - pltpu.roll(mid, 1, 2))
    grads = (grad_x, grad_y, grad_z)
    density = stepped_ref[0]
    momenta = [stepped_ref[1 + d] for d in range(3)]
    work = momenta[0] * grad_x + momenta[1] * grad_y + momenta[2] * grad_z
    cells = BX * BY
    kicked_ref[0:cells, :] = density.reshape(cells, GZ)
    for d in range(3):
        value = momenta[d] - time_step * density * grads[d]
        kicked_ref[(1 + d) * cells : (2 + d) * cells, :] = value.reshape(cells, GZ)
    kicked_ref[4 * cells :, :] = (stepped_ref[4] - time_step * work).reshape(cells, GZ)
    for q in range(5):
        for xl in range(2):
            for part in range(2):
                base = (q * BX + xl * PE + part * 8) * BY
                lines = [kicked_ref[pl.ds(base + b, 8, stride=BY), :] for b in range(BY)]
                rows = q * PE + part * 8
                for zl, value in enumerate(swap_groups(lines, PE)):
                    out_ref[owner_ref[xl * 8 + zl], rows : rows + 8, :] = value


def spread_kernel(place_ref, recv_ref, out_ref):
    shift = place_ref[0]
    live = lax.broadcasted_iota(jnp.int32, (CAP, 128), 0) < place_ref[1]
    for q in range(5):
        for tile in range(2 * PE):
            a, half = tile // 2, tile % 2
            lines = recv_ref[pl.ds(half * BRICK + q * PE + a, CAP, stride=2 * BRICK), :]
            turned = pltpu.roll(lines, shift, 0)
            out_ref[q, :, tile * 128 : (tile + 1) * 128] = jnp.where(live, turned, 0.0)


def call(kernel, outs, ins, scratch=()):
    shapes = [jax.ShapeDtypeStruct(s, jnp.float32) for s in outs]
    many = len(outs) > 1
    return pl.pallas_call(
        kernel,
        out_shape=tuple(shapes) if many else shapes[0],
        in_specs=[SM if i in ins[1] else VM for i in range(ins[0])],
        out_specs=tuple([VM] * len(outs)) if many else VM,
        scratch_shapes=[pltpu.VMEM(s, jnp.float32) for s in scratch],
        compiler_params=PARAMS,
    )


def gather_counts(counts):
    copies = jnp.broadcast_to(counts.astype(jnp.float32).reshape(1, 1, 1), (COLS, 1, 128))
    return lax.all_to_all(copies, "col", split_axis=0, concat_axis=0, tiled=True)


def on_device(fields, counts):
    my_row = lax.axis_index("row")
    my_column = lax.axis_index("col")
    staged = call(stage_kernel, [(COLS * BRICK, 128)], (1, ()))(fields.transpose(1, 0, 2))
    spread_counts = gather_counts(counts)
    row_counts = spread_counts[:, 0, 0].astype(jnp.int32)
    column_ids = jnp.arange(COLS, dtype=jnp.int32)
    starts = jnp.sum(
        jnp.where(column_ids[None, :] < column_ids[:, None], row_counts[None, :], 0), axis=1
    )
    own_start = jnp.sum(jnp.where(column_ids < my_column, row_counts, 0))
    y_patch = my_column // 2
    wanted = jnp.arange(LINES, dtype=jnp.int32) * 16 + y_patch
    owners = jnp.sum((starts[None, :] <= wanted[:, None]).astype(jnp.int32), axis=1) - 1
    turn = own_start % CAP

    sent = call(turn_kernel, [(COLS * BRICK, 128)], (3, (0,)))(
        my_column.reshape(1), spread_counts, staged
    )
    arrived = lax.all_to_all(
        sent.reshape(COLS, BRICK, 128), "col", split_axis=0, concat_axis=0, tiled=True
    )
    own, xfirst, xlast, yfirst, ylast = call(
        unpack_kernel,
        [
            (5, BX, BY, GZ),
            (5, HALO, BY, GZ),
            (5, HALO, BY, GZ),
            (5, BX, HALO, GZ),
            (5, BX, HALO, GZ),
        ],
        (2, (0,)),
        [(5 * BX * BY, GZ)],
    )(owners, arrived)

    def ring(count, step):
        return [(i, (i + step) % count) for i in range(count)]

    xlow = lax.ppermute(xlast, "row", ring(ROWS, 1))
    xhigh = lax.ppermute(xfirst, "row", ring(ROWS, -1))
    ylow = lax.ppermute(ylast, "col", ring(COLS, 1))
    yhigh = lax.ppermute(yfirst, "col", ring(COLS, -1))
    edges = jnp.concatenate([xlow[:, 2:4], xhigh[:, 0:2]], axis=1)
    clow = lax.ppermute(edges[:, :, BY - HALO :], "col", ring(COLS, 1))
    chigh = lax.ppermute(edges[:, :, :HALO], "col", ring(COLS, -1))

    table_z = hartley(GZ)
    table_x = hartley(GX)
    modes_of = np.arange(256) % GZ
    wide = (5, BX + 2 * HALO, BY + 2 * HALO, GZ)
    first, modes = call(
        euler_kernel, [wide, (512, 128)], (8, ()), [wide, (BX * BY, GZ)]
    )(own, xlow, xhigh, ylow, yhigh, clow, chigh, jnp.asarray(table_z[modes_of]))
    planes = lax.all_to_all(
        modes.reshape(256, 2, 128), ("row", "col"), split_axis=0, concat_axis=0, tiled=True
    )
    stepped = call(second_kernel, [(5, BX, BY, GZ)], (2, ()))(own, first)
    planes, stepped = lax.optimization_barrier((planes, stepped))
    place = my_row * COLS + my_column
    wave_z = place % GZ
    eig = eigenvalues(GX)
    eig_z = -4.0 * jnp.sin((math.pi / GZ) * wave_z.astype(jnp.float32)) ** 2
    strips = call(plane_kernel, [(768, 128)], (6, (0, 1)), [(2 * GY, 128), (2 * (GY + 16), 128)])(
        (place // GZ).reshape(1),
        eig_z.reshape(1),
        planes.reshape(512, 128),
        jnp.asarray(table_x),
        jnp.asarray(eig[None, :]),
        jnp.asarray(np.broadcast_to(eig[:, None], (GX, 128))),
    )
    strips = lax.all_to_all(
        strips.reshape(256, 1, 384), ("row", "col"), split_axis=0, concat_axis=0, tiled=True
    )
    returned = call(
        kick_kernel,
        [(COLS, BRICK, 128)],
        (4, (0,)),
        [((BX + 2) * BY, GZ), (5 * BX * BY, GZ)],
    )(owners, stepped, strips.reshape(768, 128), jnp.asarray(table_z[modes_of]))
    came_back = lax.all_to_all(returned, "col", split_axis=0, concat_axis=0, tiled=True)
    home = jnp.stack([(CAP - turn) % CAP, counts[0, 0]])
    result = call(spread_kernel, [(5, CAP, PE * PE * PE)], (2, (0,)))(
        home, came_back.reshape(COLS * BRICK, 128)
    )
    return result.transpose(1, 0, 2)


def solution(mesh):
    return jax.shard_map(
        on_device,
        mesh=mesh,
        in_specs=(P(("row", "col"), None, None), P("row", "col")),
        out_specs=P(("row", "col"), None, None),
        check_vma=False,
    )
```

```python
import math

import jax
import jax.numpy as jnp
import numpy as np
from jax import lax
from jax.experimental import pallas as pl
from jax.experimental.pallas import tpu as pltpu
from jax.sharding import PartitionSpec as P

PE = 16
GX = 256
GY = 256
GZ = 128
ROWS = 8
COLS = 32
BX = GX // ROWS
BY = GY // COLS
CAP = 16
LINES = 16
BRICK = 5 * PE
HALO = 4

time_step = 0.03
four_pi_g = 10.0

PARAMS = pltpu.CompilerParams(vmem_limit_bytes=16 * 2**20)
VM = pl.BlockSpec(memory_space=pltpu.VMEM)
SM = pl.BlockSpec(memory_space=pltpu.SMEM)


def hartley(length):
    index = np.arange(length)
    angle = 2.0 * np.pi / length * (index[:, None] * index[None, :] % length)
    return ((np.cos(angle) + np.sin(angle)) / math.sqrt(length)).astype(np.float32)


def eigenvalues(length):
    return (-4.0 * np.sin(np.pi * np.arange(length) / length) ** 2).astype(np.float32)


def dot(left, right, dims=((1,), (0,))):
    return lax.dot_general(
        left,
        right,
        (dims, ((), ())),
        precision=lax.Precision.HIGHEST,
        preferred_element_type=jnp.float32,
    )


def swap_groups(arrays, group):
    count = len(arrays)
    lane = lax.broadcasted_iota(jnp.int32, arrays[0].shape, 1) // group
    arrays = list(arrays)
    distance = count // 2
    while distance:
        upper = (lane & distance) != 0
        for i in range(count):
            if i & distance:
                continue
            low, high = arrays[i], arrays[i + distance]
            arrays[i] = jnp.where(upper, pltpu.roll(high, distance * group, 1), low)
            arrays[i + distance] = jnp.where(
                upper, high, pltpu.roll(low, 128 - distance * group, 1)
            )
        distance //= 2
    return arrays


def stage_kernel(fields_ref, out_ref):
    for q in range(5):
        for tile in range(2 * PE):
            a, half = tile // 2, tile % 2
            slots = fields_ref[q, :, tile * 128 : (tile + 1) * 128]
            out_ref[pl.ds(half * BRICK + q * PE + a, CAP, stride=2 * BRICK), :] = slots


def turn_kernel(column_ref, counts_ref, staged_ref, out_ref):
    counts = counts_ref[...].reshape(COLS, 128)
    before = lax.broadcasted_iota(jnp.int32, (COLS, 128), 0) < column_ref[0]
    start = (jnp.sum(jnp.where(before, counts, 0.0)) * (1.0 / 128.0)).astype(jnp.int32)
    size = 2 * BRICK
    for y in range(CAP):
        source = pl.multiple_of(((y - start) & (CAP - 1)) * size, 8)
        out_ref[y * size : (y + 1) * size, :] = staged_ref[pl.ds(source, size), :]


def unpack_kernel(owner_ref, recv_ref, own_ref, xfirst_ref, xlast_ref, yfirst_ref, ylast_ref, flat_ref):
    for q in range(5):
        for xl in range(2):
            for part in range(2):
                rows = q * PE + part * 8
                lines = [
                    recv_ref[owner_ref[xl * 8 + zl], rows : rows + 8, :] for zl in range(8)
                ]
                for b, value in enumerate(swap_groups(lines, PE)):
                    base = (q * BX + xl * PE + part * 8) * BY + b
                    flat_ref[pl.ds(base, 8, stride=BY), :] = value
    block = flat_ref[...].reshape(5, BX, BY, GZ)
    own_ref[...] = block
    xfirst_ref[...] = block[:, :HALO]
    xlast_ref[...] = block[:, BX - HALO :]
    yfirst_ref[...] = block[:, :, :HALO]
    ylast_ref[...] = block[:, :, BY - HALO :]


def minmod(p, q):
    return jnp.maximum(jnp.minimum(p, q), 0.0) + jnp.minimum(jnp.maximum(p, q), 0.0)


def half_flux(states, direction, sign):
    if len(states) == 2:
        return [0.5 * states[1] + sign * 2.0 * states[0]]
    density, energy = states[0], states[4]
    inverse = 1.0 / density
    velocity = 0.5 * states[1 + direction] * inverse
    squares = states[1] * states[1] + states[2] * states[2] + states[3] * states[3]
    pressure = 0.4 * energy - (0.2 * squares) * inverse
    pieces = [0.5 * states[1 + direction]]
    for component in range(3):
        term = states[1 + component] * velocity
        if component == direction:
            term = term + 0.5 * pressure
        pieces.append(term)
    pieces.append((energy + pressure) * velocity)
    if sign > 0:
        return [piece + 2.0 * state for piece, state in zip(pieces, states)]
    return [piece - 2.0 * state for piece, state in zip(pieces, states)]


def edge_terms(states, slopes, direction):
    halves = [0.5 * slope for slope in slopes]
    upper = half_flux([u + h for u, h in zip(states, halves)], direction, 1)
    lower = half_flux([u - h for u, h in zip(states, halves)], direction, -1)
    return upper, lower


def line_change(states, direction, axis):
    size = states[0].shape[axis]
    gaps = [pltpu.roll(u, size - 1, axis) - u for u in states]
    slopes = [minmod(pltpu.roll(g, 1, axis), g) for g in gaps]
    upper, lower = edge_terms(states, slopes, direction)
    faces = [u + pltpu.roll(w, size - 1, axis) for u, w in zip(upper, lower)]
    return [f - pltpu.roll(f, 1, axis) for f in faces]


def all_fields(states, direction):
    return states


def mass_fields(states, direction):
    return [states[0], states[1 + direction]]


def euler_stage(load, store, first_row, count, keep, unroll, pick=all_fields):
    def slopes_of(low, mid, high):
        return [minmod(b - a, c - b) for a, b, c in zip(low, mid, high)]

    cut = lambda states: [u[:keep] for u in states]
    cut_x = lambda states: cut(pick(states, 0))
    r0, r1, r2, r3 = [cut_x(load(first_row + k)) for k in (-2, -1, 0, 1)]
    upper_prev, _ = edge_terms(r1, slopes_of(r0, r1, r2), 0)
    upper_now, lower_now = edge_terms(r2, slopes_of(r1, r2, r3), 0)
    face = [u + w for u, w in zip(upper_prev, lower_now)]

    def step(k, carry):
        face_low, upper_here = carry
        i = first_row + k
        here, above, far = load(i), cut_x(load(i + 1)), cut_x(load(i + 2))
        mine = cut(here)
        upper_next, lower_next = edge_terms(above, slopes_of(pick(mine, 0), above, far), 0)
        face_high = [u + w for u, w in zip(upper_here, lower_next)]
        change = [h - l for h, l in zip(face_high, face_low)]
        along_y = cut(line_change(pick(here, 1), 1, 0))
        along_z = line_change(pick(mine, 2), 2, 1)
        rate = [-(a + b + c) for a, b, c in zip(change, along_y, along_z)]
        store(i, mine, rate)
        return tuple(face_high), tuple(upper_next)

    lax.fori_loop(0, count, step, (tuple(face), tuple(upper_now)), unroll=unroll)


def euler_kernel(
    own_ref, xlow_ref, xhigh_ref, ylow_ref, yhigh_ref, clow_ref, chigh_ref, table_ref,
    first_ref, modes_ref, ext_ref, flat_ref,
):
    low, high = slice(BY + HALO, BY + 2 * HALO), slice(BY, BY + HALO)
    inner = slice(HALO, HALO + BX)
    ext_ref[:, inner, 0:BY] = own_ref[...]
    ext_ref[:, 0:HALO, 0:BY] = xlow_ref[...]
    ext_ref[:, HALO + BX :, 0:BY] = xhigh_ref[...]
    ext_ref[:, inner, high] = yhigh_ref[...]
    ext_ref[:, inner, low] = ylow_ref[...]
    for part, ref in ((low, clow_ref), (high, chigh_ref)):
        corner = ref[...]
        ext_ref[:, 0:2, part] = corner[:, 0:2]
        ext_ref[:, 2:4, part] = corner[:, 0:2]
        ext_ref[:, HALO + BX : HALO + BX + 2, part] = corner[:, 2:4]
        ext_ref[:, HALO + BX + 2 :, part] = corner[:, 2:4]

    def load_ext(i):
        return [ext_ref[q, i] for q in range(5)]

    def store_first(i, states, rates):
        for q in range(5):
            first_ref[q, i - 2] = states[q] + time_step * rates[q]

    euler_stage(load_ext, store_first, 2, BX + 4, BY + 2 * HALO, 6)

    def load_mass(i):
        return [first_ref[q, i - 2] for q in range(4)]

    def store_density(i, states, rates):
        second = states[0] + time_step * rates[0]
        row = pl.multiple_of((i - HALO) * BY, BY)
        flat_ref[pl.ds(row, BY), :] = 0.5 * ext_ref[0, i, 0:BY] + 0.5 * second

    euler_stage(load_mass, store_density, HALO, BX, BY, 32, mass_fields)
    density = jnp.concatenate(
        [flat_ref[pl.ds(b, BX, stride=BY), :] for b in range(BY)], axis=0
    )
    spread = dot(table_ref[...], density, ((1,), (1,)))
    modes_ref[pl.ds(0, 256, stride=2), :] = spread[:, :128]
    modes_ref[pl.ds(1, 256, stride=2), :] = spread[:, 128:]


def second_kernel(own_ref, first_ref, stepped_ref):
    def load_first(i):
        return [first_ref[q, i - 2] for q in range(5)]

    def store_stepped(i, states, rates):
        for q in range(5):
            second = states[q] + time_step * rates[q]
            stepped_ref[q, i - HALO] = 0.5 * own_ref[q, i - HALO] + 0.5 * second

    euler_stage(load_first, store_stepped, HALO, BX, BY, 8)


def plane_kernel(place_ref, wave_ref, modes_ref, table_ref, eigx_ref, eigy_ref, out_ref, plane_ref, wide_ref):
    for high in range(2):
        for tile in range(2):
            lines = [
                modes_ref[pl.ds((high * 4 + r) * COLS * 2 + tile, COLS, stride=2), :]
                for r in range(4)
            ]
            for p, value in enumerate(swap_groups(lines, 32)):
                plane_ref[pl.ds(high * GY + tile * 4 + p, COLS, stride=BY), :] = value
    half = pl.multiple_of(place_ref[0] * 128, 128)
    table = table_ref[...]
    half_table = table_ref[pl.ds(half, 128), :]
    plane = jnp.concatenate([plane_ref[0:GY, :], plane_ref[GY:, :]], axis=1)
    spectrum = dot(dot(half_table, plane), table)
    eigen = eigx_ref[...] + eigy_ref[pl.ds(half, 128), :][:, 0:1] + wave_ref[0]
    flat = eigen >= 0.0
    green = jnp.where(flat, 0.0, four_pi_g / jnp.where(flat, -1.0, eigen))
    back = dot(spectrum * green, table)
    potential = dot(half_table, back, ((0,), (0,)))
    for high in range(2):
        base, side = high * (GY + 16), potential[:, high * 128 : high * 128 + 128]
        wide_ref[base + 8 : base + 8 + GY, :] = side
        wide_ref[base : base + 8, :] = side[GY - 8 :]
        wide_ref[base + 8 + GY : base + 16 + GY, :] = side[:8]

    def strip(row):
        return jnp.concatenate(
            [wide_ref[pl.ds(b + row, COLS, stride=BY), :] for b in (0, GY + 16)], axis=1
        )

    strips = [strip(8 + yl) for yl in range(BY)]
    below, above = strip(7), strip(16)
    lane = lax.broadcasted_iota(jnp.int32, (COLS, GX), 1) % 32
    sides = jnp.zeros((COLS, GX), jnp.float32)
    for yl in range(BY):
        sides = jnp.where(lane == yl, pltpu.roll(strips[yl], 1 + yl, 1), sides)
        sides = jnp.where(lane == 8 + yl, pltpu.roll(strips[yl], GX - 24 + yl, 1), sides)
    strips = strips + [below, above, sides, sides]
    for high in range(2):
        for quad in range(3):
            lines = [s[:, high * 128 : high * 128 + 128] for s in strips[quad * 4 : quad * 4 + 4]]
            for p, value in enumerate(swap_groups(lines, 32)):
                out_ref[pl.ds((high * 4 + p) * COLS * 3 + quad, COLS, stride=3), :] = value


def kick_kernel(owner_ref, stepped_ref, modes_ref, table_ref, out_ref, phi_ref, kicked_ref):
    table = table_ref[...]
    parts = []
    for quad in range(3):
        block = modes_ref[pl.ds(quad, 256, stride=3), :]
        parts.append(dot(block, table, ((0,), (0,))))
    for yl in range(BY):
        phi_ref[pl.ds(BY + yl, BX, stride=BY), :] = parts[yl // 4][(yl % 4) * 32 : (yl % 4) * 32 + 32]
    phi_ref[0:BY, :] = parts[2][64 : 64 + BY]
    phi_ref[BY + BX * BY :, :] = parts[2][64 + BY : 64 + 2 * BY]
    phi = phi_ref[...].reshape(BX + 2, BY, GZ)
    mid = phi[1 : 1 + BX]
    below = parts[2][0:32].reshape(BX, 1, GZ)
    above = parts[2][32:64].reshape(BX, 1, GZ)
    grad_x = 0.5 * (phi[2:] - phi[:BX])
    lower = jnp.concatenate([below, mid[:, : BY - 1]], axis=1)
    upper = jnp.concatenate([mid[:, 1:], above], axis=1)
    grad_y = 0.5 * (upper - lower)
    grad_z = 0.5 * (pltpu.roll(mid, GZ - 1, 2) - pltpu.roll(mid, 1, 2))
    grads = (grad_x, grad_y, grad_z)
    density = stepped_ref[0]
    momenta = [stepped_ref[1 + d] for d in range(3)]
    work = momenta[0] * grad_x + momenta[1] * grad_y + momenta[2] * grad_z
    cells = BX * BY
    kicked_ref[0:cells, :] = density.reshape(cells, GZ)
    for d in range(3):
        value = momenta[d] - time_step * density * grads[d]
        kicked_ref[(1 + d) * cells : (2 + d) * cells, :] = value.reshape(cells, GZ)
    kicked_ref[4 * cells :, :] = (stepped_ref[4] - time_step * work).reshape(cells, GZ)
    for q in range(5):
        for xl in range(2):
            for part in range(2):
                base = (q * BX + xl * PE + part * 8) * BY
                lines = [kicked_ref[pl.ds(base + b, 8, stride=BY), :] for b in range(BY)]
                rows = q * PE + part * 8
                for zl, value in enumerate(swap_groups(lines, PE)):
                    out_ref[owner_ref[xl * 8 + zl], rows : rows + 8, :] = value


def spread_kernel(place_ref, recv_ref, out_ref):
    shift = place_ref[0]
    live = lax.broadcasted_iota(jnp.int32, (CAP, 128), 0) < place_ref[1]
    for q in range(5):
        for tile in range(2 * PE):
            a, half = tile // 2, tile % 2
            lines = recv_ref[pl.ds(half * BRICK + q * PE + a, CAP, stride=2 * BRICK), :]
            turned = pltpu.roll(lines, shift, 0)
            out_ref[q, :, tile * 128 : (tile + 1) * 128] = jnp.where(live, turned, 0.0)


def call(kernel, outs, ins, scratch=()):
    shapes = [jax.ShapeDtypeStruct(s, jnp.float32) for s in outs]
    many = len(outs) > 1
    return pl.pallas_call(
        kernel,
        out_shape=tuple(shapes) if many else shapes[0],
        in_specs=[SM if i in ins[1] else VM for i in range(ins[0])],
        out_specs=tuple([VM] * len(outs)) if many else VM,
        scratch_shapes=[pltpu.VMEM(s, jnp.float32) for s in scratch],
        compiler_params=PARAMS,
    )


def gather_counts(counts):
    copies = jnp.broadcast_to(counts.astype(jnp.float32).reshape(1, 1, 1), (COLS, 1, 128))
    return lax.all_to_all(copies, "col", split_axis=0, concat_axis=0, tiled=True)


def on_device(fields, counts):
    my_row = lax.axis_index("row")
    my_column = lax.axis_index("col")
    staged = call(stage_kernel, [(COLS * BRICK, 128)], (1, ()))(fields.transpose(1, 0, 2))
    spread_counts = gather_counts(counts)
    row_counts = spread_counts[:, 0, 0].astype(jnp.int32)
    column_ids = jnp.arange(COLS, dtype=jnp.int32)
    starts = jnp.sum(
        jnp.where(column_ids[None, :] < column_ids[:, None], row_counts[None, :], 0), axis=1
    )
    own_start = jnp.sum(jnp.where(column_ids < my_column, row_counts, 0))
    y_patch = my_column // 2
    wanted = jnp.arange(LINES, dtype=jnp.int32) * 16 + y_patch
    owners = jnp.sum((starts[None, :] <= wanted[:, None]).astype(jnp.int32), axis=1) - 1
    turn = own_start % CAP

    sent = call(turn_kernel, [(COLS * BRICK, 128)], (3, (0,)))(
        my_column.reshape(1), spread_counts, staged
    )
    arrived = lax.all_to_all(
        sent.reshape(COLS, BRICK, 128), "col", split_axis=0, concat_axis=0, tiled=True
    )
    own, xfirst, xlast, yfirst, ylast = call(
        unpack_kernel,
        [
            (5, BX, BY, GZ),
            (5, HALO, BY, GZ),
            (5, HALO, BY, GZ),
            (5, BX, HALO, GZ),
            (5, BX, HALO, GZ),
        ],
        (2, (0,)),
        [(5 * BX * BY, GZ)],
    )(owners, arrived)

    def ring(count, step):
        return [(i, (i + step) % count) for i in range(count)]

    xlow = lax.ppermute(xlast, "row", ring(ROWS, 1))
    xhigh = lax.ppermute(xfirst, "row", ring(ROWS, -1))
    ylow = lax.ppermute(ylast, "col", ring(COLS, 1))
    yhigh = lax.ppermute(yfirst, "col", ring(COLS, -1))
    edges = jnp.concatenate([xlow[:, 2:4], xhigh[:, 0:2]], axis=1)
    clow = lax.ppermute(edges[:, :, BY - HALO :], "col", ring(COLS, 1))
    chigh = lax.ppermute(edges[:, :, :HALO], "col", ring(COLS, -1))

    table_z = hartley(GZ)
    table_x = hartley(GX)
    modes_of = np.arange(256) % GZ
    wide = (5, BX + 2 * HALO, BY + 2 * HALO, GZ)
    first, modes = call(
        euler_kernel, [(5, BX + HALO, BY + 2 * HALO, GZ), (512, 128)], (8, ()), [wide, (BX * BY, GZ)]
    )(own, xlow, xhigh, ylow, yhigh, clow, chigh, jnp.asarray(table_z[modes_of]))
    planes = lax.all_to_all(
        modes.reshape(256, 2, 128), ("row", "col"), split_axis=0, concat_axis=0, tiled=True
    )
    stepped = call(second_kernel, [(5, BX, BY, GZ)], (2, ()))(own, first)
    planes, stepped = lax.optimization_barrier((planes, stepped))
    place = my_row * COLS + my_column
    wave_z = place % GZ
    eig = eigenvalues(GX)
    eig_z = -4.0 * jnp.sin((math.pi / GZ) * wave_z.astype(jnp.float32)) ** 2
    strips = call(plane_kernel, [(768, 128)], (6, (0, 1)), [(2 * GY, 128), (2 * (GY + 16), 128)])(
        (place // GZ).reshape(1),
        eig_z.reshape(1),
        planes.reshape(512, 128),
        jnp.asarray(table_x),
        jnp.asarray(eig[None, :]),
        jnp.asarray(np.broadcast_to(eig[:, None], (GX, 128))),
    )
    strips = lax.all_to_all(
        strips.reshape(256, 1, 384), ("row", "col"), split_axis=0, concat_axis=0, tiled=True
    )
    returned = call(
        kick_kernel,
        [(COLS, BRICK, 128)],
        (4, (0,)),
        [((BX + 2) * BY, GZ), (5 * BX * BY, GZ)],
    )(owners, stepped, strips.reshape(768, 128), jnp.asarray(table_z[modes_of]))
    came_back = lax.all_to_all(returned, "col", split_axis=0, concat_axis=0, tiled=True)
    home = jnp.stack([(CAP - turn) % CAP, counts[0, 0]])
    result = call(spread_kernel, [(5, CAP, PE * PE * PE)], (2, (0,)))(
        home, came_back.reshape(COLS * BRICK, 128)
    )
    return result.transpose(1, 0, 2)


def solution(mesh):
    return jax.shard_map(
        on_device,
        mesh=mesh,
        in_specs=(P(("row", "col"), None, None), P("row", "col")),
        out_specs=P(("row", "col"), None, None),
        check_vma=False,
    )
```

```python
import math

import jax
import jax.numpy as jnp
import numpy as np
from jax import lax
from jax.experimental import pallas as pl
from jax.experimental.pallas import tpu as pltpu
from jax.sharding import PartitionSpec as P

PE = 16
GX = 256
GY = 256
GZ = 128
ROWS = 8
COLS = 32
BX = GX // ROWS
BY = GY // COLS
CAP = 16
LINES = 16
BRICK = 5 * PE
HALO = 4

time_step = 0.03
four_pi_g = 10.0

PARAMS = pltpu.CompilerParams(vmem_limit_bytes=16 * 2**20)
VM = pl.BlockSpec(memory_space=pltpu.VMEM)
SM = pl.BlockSpec(memory_space=pltpu.SMEM)


def hartley(length):
    index = np.arange(length)
    angle = 2.0 * np.pi / length * (index[:, None] * index[None, :] % length)
    return ((np.cos(angle) + np.sin(angle)) / math.sqrt(length)).astype(np.float32)


def kappas():
    wave_y = np.sin(np.pi * np.arange(GY) / GY) ** 2
    wave_z = np.sin(np.pi * np.arange(GZ) / GZ) ** 2
    return 2.0 * np.arcsinh(np.sqrt(wave_z[:, None] + wave_y[None, :]))


def lane_spans():
    inner = np.arange(128) % BX
    return np.concatenate([inner, np.where(inner == 0, -1, BX)]).astype(np.float32)


def lane_expand():
    lanes = np.arange(256) % 128 // BX
    return 0.5 * (np.arange(8)[:, None] // 2 == lanes[None, :]).astype(np.float32)


def lane_picks():
    picks = np.zeros((16, 128), np.float32)
    for k in range(4):
        picks[2 * k, k * BX + BX - 1] = 1.0
        picks[8 + 2 * k + 1, k * BX] = 1.0
    return picks


def mean_line():
    lanes = np.arange(256)
    used = (lanes < BX) | (lanes == 128) | (lanes == 129)
    gap = np.arange(GX)[:, None] // BX * BX + lane_spans()[None, :] - np.arange(GX)[:, None] % BX
    gap = np.abs(gap)
    return (four_pi_g * np.where(used[None, :], gap / 2.0 - gap * gap / (2.0 * GX), 0.0)).astype(np.float32)


def dot(left, right, dims=((1,), (0,))):
    return lax.dot_general(
        left,
        right,
        (dims, ((), ())),
        precision=lax.Precision.HIGHEST,
        preferred_element_type=jnp.float32,
    )


def swap_groups(arrays, group):
    count = len(arrays)
    lane = lax.broadcasted_iota(jnp.int32, arrays[0].shape, 1) // group
    arrays = list(arrays)
    distance = count // 2
    while distance:
        upper = (lane & distance) != 0
        for i in range(count):
            if i & distance:
                continue
            low, high = arrays[i], arrays[i + distance]
            arrays[i] = jnp.where(upper, pltpu.roll(high, distance * group, 1), low)
            arrays[i + distance] = jnp.where(
                upper, high, pltpu.roll(low, 128 - distance * group, 1)
            )
        distance //= 2
    return arrays


def stage_kernel(fields_ref, out_ref):
    for q in range(5):
        for tile in range(2 * PE):
            a, half = tile // 2, tile % 2
            slots = fields_ref[q, :, tile * 128 : (tile + 1) * 128]
            out_ref[pl.ds(half * BRICK + q * PE + a, CAP, stride=2 * BRICK), :] = slots


def turn_kernel(column_ref, counts_ref, staged_ref, out_ref):
    counts = counts_ref[...].reshape(COLS, 128)
    before = lax.broadcasted_iota(jnp.int32, (COLS, 128), 0) < column_ref[0]
    start = (jnp.sum(jnp.where(before, counts, 0.0)) * (1.0 / 128.0)).astype(jnp.int32)
    size = 2 * BRICK
    for y in range(CAP):
        source = pl.multiple_of(((y - start) & (CAP - 1)) * size, 8)
        out_ref[y * size : (y + 1) * size, :] = staged_ref[pl.ds(source, size), :]


def unpack_kernel(owner_ref, recv_ref, own_ref, xfirst_ref, xlast_ref, yfirst_ref, ylast_ref, flat_ref):
    for q in range(5):
        for xl in range(2):
            for part in range(2):
                rows = q * PE + part * 8
                lines = [
                    recv_ref[owner_ref[xl * 8 + zl], rows : rows + 8, :] for zl in range(8)
                ]
                for b, value in enumerate(swap_groups(lines, PE)):
                    base = (q * BX + xl * PE + part * 8) * BY + b
                    flat_ref[pl.ds(base, 8, stride=BY), :] = value
    block = flat_ref[...].reshape(5, BX, BY, GZ)
    own_ref[...] = block
    xfirst_ref[...] = block[:, :HALO]
    xlast_ref[...] = block[:, BX - HALO :]
    yfirst_ref[...] = block[:, :, :HALO]
    ylast_ref[...] = block[:, :, BY - HALO :]


def minmod(p, q):
    return jnp.maximum(jnp.minimum(p, q), 0.0) + jnp.minimum(jnp.maximum(p, q), 0.0)


def half_flux(states, direction, sign):
    if len(states) == 2:
        return [0.5 * states[1] + sign * 2.0 * states[0]]
    density, energy = states[0], states[4]
    inverse = 1.0 / density
    velocity = 0.5 * states[1 + direction] * inverse
    squares = states[1] * states[1] + states[2] * states[2] + states[3] * states[3]
    pressure = 0.4 * energy - (0.2 * squares) * inverse
    pieces = [0.5 * states[1 + direction]]
    for component in range(3):
        term = states[1 + component] * velocity
        if component == direction:
            term = term + 0.5 * pressure
        pieces.append(term)
    pieces.append((energy + pressure) * velocity)
    if sign > 0:
        return [piece + 2.0 * state for piece, state in zip(pieces, states)]
    return [piece - 2.0 * state for piece, state in zip(pieces, states)]


def edge_terms(states, slopes, direction):
    halves = [0.5 * slope for slope in slopes]
    upper = half_flux([u + h for u, h in zip(states, halves)], direction, 1)
    lower = half_flux([u - h for u, h in zip(states, halves)], direction, -1)
    return upper, lower


def line_change(states, direction, axis):
    size = states[0].shape[axis]
    gaps = [pltpu.roll(u, size - 1, axis) - u for u in states]
    slopes = [minmod(pltpu.roll(g, 1, axis), g) for g in gaps]
    upper, lower = edge_terms(states, slopes, direction)
    faces = [u + pltpu.roll(w, size - 1, axis) for u, w in zip(upper, lower)]
    return [f - pltpu.roll(f, 1, axis) for f in faces]


def all_fields(states, direction):
    return states


def mass_fields(states, direction):
    return [states[0], states[1 + direction]]


def euler_stage(load, store, first_row, count, keep, unroll, pick=all_fields):
    def slopes_of(low, mid, high):
        return [minmod(b - a, c - b) for a, b, c in zip(low, mid, high)]

    cut = lambda states: [u[:keep] for u in states]
    cut_x = lambda states: cut(pick(states, 0))
    r0, r1, r2, r3 = [cut_x(load(first_row + k)) for k in (-2, -1, 0, 1)]
    upper_prev, _ = edge_terms(r1, slopes_of(r0, r1, r2), 0)
    upper_now, lower_now = edge_terms(r2, slopes_of(r1, r2, r3), 0)
    face = [u + w for u, w in zip(upper_prev, lower_now)]

    def step(k, carry):
        face_low, upper_here = carry
        i = first_row + k
        here, above, far = load(i), cut_x(load(i + 1)), cut_x(load(i + 2))
        mine = cut(here)
        upper_next, lower_next = edge_terms(above, slopes_of(pick(mine, 0), above, far), 0)
        face_high = [u + w for u, w in zip(upper_here, lower_next)]
        change = [h - l for h, l in zip(face_high, face_low)]
        along_y = cut(line_change(pick(here, 1), 1, 0))
        along_z = line_change(pick(mine, 2), 2, 1)
        rate = [-(a + b + c) for a, b, c in zip(change, along_y, along_z)]
        store(i, mine, rate)
        return tuple(face_high), tuple(upper_next)

    lax.fori_loop(0, count, step, (tuple(face), tuple(upper_now)), unroll=unroll)


def euler_kernel(
    own_ref, xlow_ref, xhigh_ref, ylow_ref, yhigh_ref, clow_ref, chigh_ref, table_ref,
    first_ref, modes_ref, ext_ref, flat_ref,
):
    low, high = slice(BY + HALO, BY + 2 * HALO), slice(BY, BY + HALO)
    inner = slice(HALO, HALO + BX)
    ext_ref[:, inner, 0:BY] = own_ref[...]
    ext_ref[:, 0:HALO, 0:BY] = xlow_ref[...]
    ext_ref[:, HALO + BX :, 0:BY] = xhigh_ref[...]
    ext_ref[:, inner, high] = yhigh_ref[...]
    ext_ref[:, inner, low] = ylow_ref[...]
    for part, ref in ((low, clow_ref), (high, chigh_ref)):
        corner = ref[...]
        ext_ref[:, 0:2, part] = corner[:, 0:2]
        ext_ref[:, 2:4, part] = corner[:, 0:2]
        ext_ref[:, HALO + BX : HALO + BX + 2, part] = corner[:, 2:4]
        ext_ref[:, HALO + BX + 2 :, part] = corner[:, 2:4]

    def load_ext(i):
        return [ext_ref[q, i] for q in range(5)]

    def store_first(i, states, rates):
        for q in range(5):
            first_ref[q, i - 2] = states[q] + time_step * rates[q]

    euler_stage(load_ext, store_first, 2, BX + 4, BY + 2 * HALO, 6)

    def load_mass(i):
        return [first_ref[q, i - 2] for q in range(4)]

    def store_density(i, states, rates):
        second = states[0] + time_step * rates[0]
        row = pl.multiple_of((i - HALO) * BY, BY)
        flat_ref[pl.ds(row, BY), :] = 0.5 * ext_ref[0, i, 0:BY] + 0.5 * second

    euler_stage(load_mass, store_density, HALO, BX, BY, 32, mass_fields)
    density = jnp.concatenate(
        [flat_ref[pl.ds(b, BX, stride=BY), :] for b in range(BY)], axis=0
    )
    spread = dot(table_ref[...], density, ((1,), (1,)))
    modes_ref[pl.ds(0, GZ, stride=2), :] = spread[:, :128]
    modes_ref[pl.ds(1, GZ, stride=2), :] = spread[:, 128:]


def second_kernel(own_ref, first_ref, stepped_ref):
    def load_first(i):
        return [first_ref[q, i - 2] for q in range(5)]

    def store_stepped(i, states, rates):
        for q in range(5):
            second = states[q] + time_step * rates[q]
            stepped_ref[q, i - HALO] = 0.5 * own_ref[q, i - HALO] + 0.5 * second

    euler_stage(load_first, store_stepped, HALO, BX, BY, 8)


def table_kernel(kappa_ref, expand_ref, span_ref, decay_ref, scale_ref, left_ref, right_ref):
    kappa = dot(kappa_ref[...], expand_ref[...], ((0,), (0,)))
    flat = kappa <= 0.0
    decay = jnp.exp(-kappa)
    width = jnp.where(flat, 1.0, jnp.exp(kappa) - decay)
    scale = jnp.where(flat, 0.0, -four_pi_g / width)
    images = scale / jnp.where(flat, 1.0, 1.0 - jnp.exp(-GX * kappa))
    span = span_ref[...]
    decay_ref[...] = decay
    scale_ref[...] = scale
    left_ref[...] = images * jnp.exp(-kappa * (span + 1.0))
    right_ref[...] = images * jnp.exp(-kappa * (BX - span))


def ends_kernel(modes_ref, table_ref, decay_ref, scale_ref, pick_ref, local_ref, ends_ref, plane_ref):
    for tile in range(2):
        lines = [modes_ref[pl.ds(k * 2 + tile, COLS, stride=8), :] for k in range(4)]
        for g, value in enumerate(swap_groups(lines, 32)):
            plane_ref[pl.ds(tile * 4 + g, COLS, stride=BY), :] = value
    source = dot(table_ref[...], plane_ref[...])
    x = lax.broadcasted_iota(jnp.int32, (GY, 128), 1) % BX
    power = decay_ref[:, :128]
    rising, falling = source, source
    step = 1
    while step < BX:
        rising = rising + jnp.where(x >= step, power * pltpu.roll(rising, step, 1), 0.0)
        falling = falling + jnp.where(x < BX - step, power * pltpu.roll(falling, 128 - step, 1), 0.0)
        power = power * power
        step *= 2
    local_ref[:, :128] = scale_ref[:, :128] * (rising + falling - source)
    side = jnp.where(x == 0, falling, pltpu.roll(rising, 128 - BX + 2, 1))
    local_ref[:, 128:] = scale_ref[:, 128:] * decay_ref[:, 128:] * side
    ends = dot(pick_ref[0:8, :], rising, ((1,), (1,))) + dot(pick_ref[8:16, :], falling, ((1,), (1,)))
    for r in range(ROWS):
        ends_ref[r * 24 : r * 24 + 8, :] = ends[:, :128]
        ends_ref[r * 24 + 8 : r * 24 + 16, :] = ends[:, 128:]
        ends_ref[r * 24 + 16 : r * 24 + 24, :] = source[0:8]


def join_kernel(
    place_ref, ends_ref, local_ref, left_ref, right_ref, kappa_ref, expand_ref, line_ref, table_ref,
    out_ref, wide_ref,
):
    row = place_ref[0]

    def slab(step):
        return pl.multiple_of(((row + step) & (ROWS - 1)) * 24, 8)

    rising = lax.broadcasted_iota(jnp.int32, (8, GY), 0) % 2 == 0
    block = jnp.exp(-BX * kappa_ref[...])
    total = None
    for d in range(ROWS, 0, -1):
        below, above = slab(ROWS - d), slab(d)
        both = []
        for part in (0, 8):
            both.append((ends_ref[pl.ds(below + part, 8), :], ends_ref[pl.ds(above + part, 8), :]))
        low = jnp.concatenate([both[0][0], both[1][0]], axis=1)
        high = jnp.concatenate([both[0][1], both[1][1]], axis=1)
        value = jnp.where(rising, low, high)
        total = value if total is None else value + block * total
    from_left = dot(jnp.where(rising, total, 0.0), expand_ref[0:8, :] * 2.0, ((0,), (0,)))
    from_right = dot(jnp.where(rising, 0.0, total), expand_ref[0:8, :] * 2.0, ((0,), (0,)))
    field = local_ref[...] + left_ref[...] * from_left + right_ref[...] * from_right
    lane = lax.broadcasted_iota(jnp.int32, (8, 128), 1)
    halves = []
    for half in range(2):
        line = jnp.zeros((8, 128), jnp.float32)
        for g in range(4):
            values = ends_ref[pl.ds(slab(ROWS - half * 4 - g) + 16, 8), :]
            values = jnp.where(lane < BX, values, 0.0)
            line = line + (pltpu.roll(values, g * BX, 1) if g else values)
        halves.append(line)
    mean = dot(jnp.concatenate(halves, axis=1), line_ref[...])
    first = lax.broadcasted_iota(jnp.int32, (8, 256), 0) == 0
    mean = jnp.where(jnp.logical_and(first, place_ref[1] == 0), mean, 0.0)
    field = jnp.concatenate([field[0:8] + mean, field[8:]], axis=0)
    potential = dot(table_ref[...], field)
    for part in range(2):
        base, side = part * (GY + 16), potential[:, part * 128 : part * 128 + 128]
        wide_ref[base + 8 : base + 8 + GY, :] = side
        wide_ref[base : base + 8, :] = side[GY - 8 :]
        wide_ref[base + 8 + GY : base + 16 + GY, :] = side[:8]
    strips = [wide_ref[pl.ds(8 + yl, COLS, stride=BY), :] for yl in range(BY)]
    below = wide_ref[pl.ds(7, COLS, stride=BY), :]
    above = wide_ref[pl.ds(16, COLS, stride=BY), :]
    x = lax.broadcasted_iota(jnp.int32, (COLS, 128), 1) % BX
    sides = jnp.zeros((COLS, 128), jnp.float32)
    for yl in range(BY):
        edge = wide_ref[pl.ds(GY + 16 + 8 + yl, COLS, stride=BY), :]
        sides = jnp.where(x == yl, pltpu.roll(edge, yl, 1) if yl else edge, sides)
        sides = jnp.where(x == BY + yl, pltpu.roll(edge, BY - 1 + yl, 1), sides)
    strips = strips + [below, above, sides, sides]
    for quad in range(3):
        for k, value in enumerate(swap_groups(strips[quad * 4 : quad * 4 + 4], 32)):
            out_ref[pl.ds(k * 3 + quad, COLS, stride=12), :] = value


def kick_kernel(owner_ref, stepped_ref, modes_ref, table_ref, out_ref, phi_ref, kicked_ref):
    table = table_ref[...]
    parts = []
    for quad in range(3):
        block = modes_ref[pl.ds(quad, GZ, stride=3), :]
        parts.append(dot(block, table, ((0,), (0,))))
    for yl in range(BY):
        phi_ref[pl.ds(BY + yl, BX, stride=BY), :] = parts[yl // 4][(yl % 4) * 32 : (yl % 4) * 32 + 32]
    phi_ref[0:BY, :] = parts[2][64 : 64 + BY]
    phi_ref[BY + BX * BY :, :] = parts[2][64 + BY : 64 + 2 * BY]
    phi = phi_ref[...].reshape(BX + 2, BY, GZ)
    mid = phi[1 : 1 + BX]
    below = parts[2][0:32].reshape(BX, 1, GZ)
    above = parts[2][32:64].reshape(BX, 1, GZ)
    grad_x = 0.5 * (phi[2:] - phi[:BX])
    lower = jnp.concatenate([below, mid[:, : BY - 1]], axis=1)
    upper = jnp.concatenate([mid[:, 1:], above], axis=1)
    grad_y = 0.5 * (upper - lower)
    grad_z = 0.5 * (pltpu.roll(mid, GZ - 1, 2) - pltpu.roll(mid, 1, 2))
    grads = (grad_x, grad_y, grad_z)
    density = stepped_ref[0]
    momenta = [stepped_ref[1 + d] for d in range(3)]
    work = momenta[0] * grad_x + momenta[1] * grad_y + momenta[2] * grad_z
    cells = BX * BY
    kicked_ref[0:cells, :] = density.reshape(cells, GZ)
    for d in range(3):
        value = momenta[d] - time_step * density * grads[d]
        kicked_ref[(1 + d) * cells : (2 + d) * cells, :] = value.reshape(cells, GZ)
    kicked_ref[4 * cells :, :] = (stepped_ref[4] - time_step * work).reshape(cells, GZ)
    for q in range(5):
        for xl in range(2):
            for part in range(2):
                base = (q * BX + xl * PE + part * 8) * BY
                lines = [kicked_ref[pl.ds(base + b, 8, stride=BY), :] for b in range(BY)]
                rows = q * PE + part * 8
                for zl, value in enumerate(swap_groups(lines, PE)):
                    out_ref[owner_ref[xl * 8 + zl], rows : rows + 8, :] = value


def spread_kernel(place_ref, recv_ref, out_ref):
    shift = place_ref[0]
    live = lax.broadcasted_iota(jnp.int32, (CAP, 128), 0) < place_ref[1]
    for q in range(5):
        for tile in range(2 * PE):
            a, half = tile // 2, tile % 2
            lines = recv_ref[pl.ds(half * BRICK + q * PE + a, CAP, stride=2 * BRICK), :]
            turned = pltpu.roll(lines, shift, 0)
            out_ref[q, :, tile * 128 : (tile + 1) * 128] = jnp.where(live, turned, 0.0)


def call(kernel, outs, ins, scratch=()):
    shapes = [jax.ShapeDtypeStruct(s, jnp.float32) for s in outs]
    many = len(outs) > 1
    return pl.pallas_call(
        kernel,
        out_shape=tuple(shapes) if many else shapes[0],
        in_specs=[SM if i in ins[1] else VM for i in range(ins[0])],
        out_specs=tuple([VM] * len(outs)) if many else VM,
        scratch_shapes=[pltpu.VMEM(s, jnp.float32) for s in scratch],
        compiler_params=PARAMS,
    )


def gather_counts(counts):
    copies = jnp.broadcast_to(counts.astype(jnp.float32).reshape(1, 1, 1), (COLS, 1, 128))
    return lax.all_to_all(copies, "col", split_axis=0, concat_axis=0, tiled=True)


def on_device(fields, counts):
    my_row = lax.axis_index("row")
    my_column = lax.axis_index("col")
    staged = call(stage_kernel, [(COLS * BRICK, 128)], (1, ()))(fields.transpose(1, 0, 2))
    spread_counts = gather_counts(counts)
    row_counts = spread_counts[:, 0, 0].astype(jnp.int32)
    column_ids = jnp.arange(COLS, dtype=jnp.int32)
    starts = jnp.sum(
        jnp.where(column_ids[None, :] < column_ids[:, None], row_counts[None, :], 0), axis=1
    )
    own_start = jnp.sum(jnp.where(column_ids < my_column, row_counts, 0))
    y_patch = my_column // 2
    wanted = jnp.arange(LINES, dtype=jnp.int32) * 16 + y_patch
    owners = jnp.sum((starts[None, :] <= wanted[:, None]).astype(jnp.int32), axis=1) - 1
    turn = own_start % CAP

    sent = call(turn_kernel, [(COLS * BRICK, 128)], (3, (0,)))(
        my_column.reshape(1), spread_counts, staged
    )
    arrived = lax.all_to_all(
        sent.reshape(COLS, BRICK, 128), "col", split_axis=0, concat_axis=0, tiled=True
    )
    own, xfirst, xlast, yfirst, ylast = call(
        unpack_kernel,
        [
            (5, BX, BY, GZ),
            (5, HALO, BY, GZ),
            (5, HALO, BY, GZ),
            (5, BX, HALO, GZ),
            (5, BX, HALO, GZ),
        ],
        (2, (0,)),
        [(5 * BX * BY, GZ)],
    )(owners, arrived)

    def ring(count, step):
        return [(i, (i + step) % count) for i in range(count)]

    xlow = lax.ppermute(xlast, "row", ring(ROWS, 1))
    xhigh = lax.ppermute(xfirst, "row", ring(ROWS, -1))
    ylow = lax.ppermute(ylast, "col", ring(COLS, 1))
    yhigh = lax.ppermute(yfirst, "col", ring(COLS, -1))
    edges = jnp.concatenate([xlow[:, 2:4], xhigh[:, 0:2]], axis=1)
    clow = lax.ppermute(edges[:, :, BY - HALO :], "col", ring(COLS, 1))
    chigh = lax.ppermute(edges[:, :, :HALO], "col", ring(COLS, -1))

    table_z = hartley(GZ)
    table_x = hartley(GX)
    wide = (5, BX + 2 * HALO, BY + 2 * HALO, GZ)
    first, modes = call(
        euler_kernel, [(5, BX + HALO, BY + 2 * HALO, GZ), (256, 128)], (8, ()), [wide, (BX * BY, GZ)]
    )(own, xlow, xhigh, ylow, yhigh, clow, chigh, jnp.asarray(table_z))
    planes = lax.all_to_all(
        modes.reshape(COLS, 8, 128), "col", split_axis=0, concat_axis=0, tiled=True
    )
    kappa = jnp.asarray(np.repeat(kappas(), 2, axis=0).astype(np.float32))
    kappa = lax.dynamic_slice_in_dim(kappa, my_column * 8, 8, axis=0)
    expand = jnp.asarray(lane_expand())
    square = (GY, 256)
    decay, scale, left, right = call(table_kernel, [square] * 4, (3, ()))(
        kappa, expand, jnp.asarray(lane_spans()[None, :])
    )
    stepped = call(second_kernel, [(5, BX, BY, GZ)], (2, ()))(own, first)
    planes, stepped, decay = lax.optimization_barrier((planes, stepped, decay))
    local, ends = call(ends_kernel, [square, (ROWS * 24, 128)], (5, ()), [(GY, 128)])(
        planes.reshape(256, 128), jnp.asarray(table_x), decay, scale, jnp.asarray(lane_picks())
    )
    ends = lax.all_to_all(
        ends.reshape(ROWS, 24, 128), "row", split_axis=0, concat_axis=0, tiled=True
    )
    strips = call(join_kernel, [(COLS * 12, 128)], (9, (0,)), [(2 * (GY + 16), 128)])(
        jnp.stack([my_row, my_column]),
        ends.reshape(ROWS * 24, 128),
        local,
        left,
        right,
        kappa,
        expand,
        jnp.asarray(mean_line()),
        jnp.asarray(table_x),
    )
    strips = lax.all_to_all(
        strips.reshape(COLS, 1, 1536), "col", split_axis=0, concat_axis=0, tiled=True
    )
    returned = call(
        kick_kernel,
        [(COLS, BRICK, 128)],
        (4, (0,)),
        [((BX + 2) * BY, GZ), (5 * BX * BY, GZ)],
    )(owners, stepped, strips.reshape(COLS * 12, 128), jnp.asarray(table_z))
    came_back = lax.all_to_all(returned, "col", split_axis=0, concat_axis=0, tiled=True)
    home = jnp.stack([(CAP - turn) % CAP, counts[0, 0]])
    result = call(spread_kernel, [(5, CAP, PE * PE * PE)], (2, (0,)))(
        home, came_back.reshape(COLS * BRICK, 128)
    )
    return result.transpose(1, 0, 2)


def solution(mesh):
    return jax.shard_map(
        on_device,
        mesh=mesh,
        in_specs=(P(("row", "col"), None, None), P("row", "col")),
        out_specs=P(("row", "col"), None, None),
        check_vma=False,
    )
```

```python
import math

import jax
import jax.numpy as jnp
import numpy as np
from jax import lax
from jax.experimental import pallas as pl
from jax.experimental.pallas import tpu as pltpu
from jax.sharding import PartitionSpec as P

PE = 16
GX = 256
GY = 256
GZ = 128
ROWS = 8
COLS = 32
BX = GX // ROWS
BY = GY // COLS
CAP = 16
LINES = 16
BRICK = 5 * PE
HALO = 4

time_step = 0.03
four_pi_g = 10.0

PARAMS = pltpu.CompilerParams(vmem_limit_bytes=16 * 2**20)
VM = pl.BlockSpec(memory_space=pltpu.VMEM)
SM = pl.BlockSpec(memory_space=pltpu.SMEM)


def hartley(length):
    index = np.arange(length)
    angle = 2.0 * np.pi / length * (index[:, None] * index[None, :] % length)
    return ((np.cos(angle) + np.sin(angle)) / math.sqrt(length)).astype(np.float32)


def kappas():
    wave_y = np.sin(np.pi * np.arange(GY) / GY) ** 2
    wave_z = np.sin(np.pi * np.arange(GZ) / GZ) ** 2
    return 2.0 * np.arcsinh(np.sqrt(wave_z[:, None] + wave_y[None, :]))


def lane_spans():
    inner = np.arange(128) % BX
    return np.concatenate([inner, np.where(inner == 0, -1, BX)]).astype(np.float32)


def lane_expand():
    lanes = np.arange(256) % 128 // BX
    return 0.5 * (np.arange(8)[:, None] // 2 == lanes[None, :]).astype(np.float32)


def lane_picks():
    picks = np.zeros((16, 128), np.float32)
    for k in range(4):
        picks[2 * k, k * BX + BX - 1] = 1.0
        picks[8 + 2 * k + 1, k * BX] = 1.0
    return picks


def mean_line():
    lanes = np.arange(256)
    used = (lanes < BX) | (lanes == 128) | (lanes == 129)
    gap = np.arange(GX)[:, None] // BX * BX + lane_spans()[None, :] - np.arange(GX)[:, None] % BX
    gap = np.abs(gap)
    shape = gap / 2.0 - gap * gap / (2.0 * GX)
    shape = shape - shape[:, 0].mean()
    return (four_pi_g * np.where(used[None, :], shape, 0.0)).astype(np.float32)


def dot(left, right, dims=((1,), (0,))):
    return lax.dot_general(
        left,
        right,
        (dims, ((), ())),
        precision=lax.Precision.HIGHEST,
        preferred_element_type=jnp.float32,
    )


def swap_groups(arrays, group):
    count = len(arrays)
    lane = lax.broadcasted_iota(jnp.int32, arrays[0].shape, 1) // group
    arrays = list(arrays)
    distance = count // 2
    while distance:
        upper = (lane & distance) != 0
        for i in range(count):
            if i & distance:
                continue
            low, high = arrays[i], arrays[i + distance]
            arrays[i] = jnp.where(upper, pltpu.roll(high, distance * group, 1), low)
            arrays[i + distance] = jnp.where(
                upper, high, pltpu.roll(low, 128 - distance * group, 1)
            )
        distance //= 2
    return arrays


def stage_kernel(fields_ref, out_ref):
    for q in range(5):
        for tile in range(2 * PE):
            a, half = tile // 2, tile % 2
            slots = fields_ref[q, :, tile * 128 : (tile + 1) * 128]
            out_ref[pl.ds(half * BRICK + q * PE + a, CAP, stride=2 * BRICK), :] = slots


def turn_kernel(column_ref, counts_ref, staged_ref, out_ref):
    counts = counts_ref[...].reshape(COLS, 128)
    before = lax.broadcasted_iota(jnp.int32, (COLS, 128), 0) < column_ref[0]
    start = (jnp.sum(jnp.where(before, counts, 0.0)) * (1.0 / 128.0)).astype(jnp.int32)
    size = 2 * BRICK
    for y in range(CAP):
        source = pl.multiple_of(((y - start) & (CAP - 1)) * size, 8)
        out_ref[y * size : (y + 1) * size, :] = staged_ref[pl.ds(source, size), :]


def unpack_kernel(owner_ref, recv_ref, own_ref, xfirst_ref, xlast_ref, yfirst_ref, ylast_ref, flat_ref):
    for q in range(5):
        for xl in range(2):
            for part in range(2):
                rows = q * PE + part * 8
                lines = [
                    recv_ref[owner_ref[xl * 8 + zl], rows : rows + 8, :] for zl in range(8)
                ]
                for b, value in enumerate(swap_groups(lines, PE)):
                    base = (q * BX + xl * PE + part * 8) * BY + b
                    flat_ref[pl.ds(base, 8, stride=BY), :] = value
    block = flat_ref[...].reshape(5, BX, BY, GZ)
    own_ref[...] = block
    xfirst_ref[...] = block[:, :HALO]
    xlast_ref[...] = block[:, BX - HALO :]
    yfirst_ref[...] = block[:, :, :HALO]
    ylast_ref[...] = block[:, :, BY - HALO :]


def minmod(p, q):
    return jnp.maximum(jnp.minimum(p, q), 0.0) + jnp.minimum(jnp.maximum(p, q), 0.0)


def half_flux(states, direction, sign):
    if len(states) == 2:
        return [0.5 * states[1] + sign * 2.0 * states[0]]
    density, energy = states[0], states[4]
    inverse = 1.0 / density
    velocity = 0.5 * states[1 + direction] * inverse
    squares = states[1] * states[1] + states[2] * states[2] + states[3] * states[3]
    pressure = 0.4 * energy - (0.2 * squares) * inverse
    pieces = [0.5 * states[1 + direction]]
    for component in range(3):
        term = states[1 + component] * velocity
        if component == direction:
            term = term + 0.5 * pressure
        pieces.append(term)
    pieces.append((energy + pressure) * velocity)
    if sign > 0:
        return [piece + 2.0 * state for piece, state in zip(pieces, states)]
    return [piece - 2.0 * state for piece, state in zip(pieces, states)]


def edge_terms(states, slopes, direction):
    halves = [0.5 * slope for slope in slopes]
    upper = half_flux([u + h for u, h in zip(states, halves)], direction, 1)
    lower = half_flux([u - h for u, h in zip(states, halves)], direction, -1)
    return upper, lower


def line_change(states, direction, axis):
    size = states[0].shape[axis]
    gaps = [pltpu.roll(u, size - 1, axis) - u for u in states]
    slopes = [minmod(pltpu.roll(g, 1, axis), g) for g in gaps]
    upper, lower = edge_terms(states, slopes, direction)
    faces = [u + pltpu.roll(w, size - 1, axis) for u, w in zip(upper, lower)]
    return [f - pltpu.roll(f, 1, axis) for f in faces]


def all_fields(states, direction):
    return states


def mass_fields(states, direction):
    return [states[0], states[1 + direction]]


def euler_stage(load, store, first_row, count, keep, unroll, pick=all_fields):
    def slopes_of(low, mid, high):
        return [minmod(b - a, c - b) for a, b, c in zip(low, mid, high)]

    cut = lambda states: [u[:keep] for u in states]
    cut_x = lambda states: cut(pick(states, 0))
    r0, r1, r2, r3 = [cut_x(load(first_row + k)) for k in (-2, -1, 0, 1)]
    upper_prev, _ = edge_terms(r1, slopes_of(r0, r1, r2), 0)
    upper_now, lower_now = edge_terms(r2, slopes_of(r1, r2, r3), 0)
    face = [u + w for u, w in zip(upper_prev, lower_now)]

    def step(k, carry):
        face_low, upper_here = carry
        i = first_row + k
        here, above, far = load(i), cut_x(load(i + 1)), cut_x(load(i + 2))
        mine = cut(here)
        upper_next, lower_next = edge_terms(above, slopes_of(pick(mine, 0), above, far), 0)
        face_high = [u + w for u, w in zip(upper_here, lower_next)]
        change = [h - l for h, l in zip(face_high, face_low)]
        along_y = cut(line_change(pick(here, 1), 1, 0))
        along_z = line_change(pick(mine, 2), 2, 1)
        rate = [-(a + b + c) for a, b, c in zip(change, along_y, along_z)]
        store(i, mine, rate)
        return tuple(face_high), tuple(upper_next)

    lax.fori_loop(0, count, step, (tuple(face), tuple(upper_now)), unroll=unroll)


def euler_kernel(
    own_ref, xlow_ref, xhigh_ref, ylow_ref, yhigh_ref, clow_ref, chigh_ref, table_ref,
    first_ref, modes_ref, ext_ref, flat_ref,
):
    low, high = slice(BY + HALO, BY + 2 * HALO), slice(BY, BY + HALO)
    inner = slice(HALO, HALO + BX)
    ext_ref[:, inner, 0:BY] = own_ref[...]
    ext_ref[:, 0:HALO, 0:BY] = xlow_ref[...]
    ext_ref[:, HALO + BX :, 0:BY] = xhigh_ref[...]
    ext_ref[:, inner, high] = yhigh_ref[...]
    ext_ref[:, inner, low] = ylow_ref[...]
    for part, ref in ((low, clow_ref), (high, chigh_ref)):
        corner = ref[...]
        ext_ref[:, 0:2, part] = corner[:, 0:2]
        ext_ref[:, 2:4, part] = corner[:, 0:2]
        ext_ref[:, HALO + BX : HALO + BX + 2, part] = corner[:, 2:4]
        ext_ref[:, HALO + BX + 2 :, part] = corner[:, 2:4]

    def load_ext(i):
        return [ext_ref[q, i] for q in range(5)]

    def store_first(i, states, rates):
        for q in range(5):
            first_ref[q, i - 2] = states[q] + time_step * rates[q]

    euler_stage(load_ext, store_first, 2, BX + 4, BY + 2 * HALO, 6)

    def load_mass(i):
        return [first_ref[q, i - 2] for q in range(4)]

    def store_density(i, states, rates):
        second = states[0] + time_step * rates[0]
        row = pl.multiple_of((i - HALO) * BY, BY)
        flat_ref[pl.ds(row, BY), :] = 0.5 * ext_ref[0, i, 0:BY] + 0.5 * second

    euler_stage(load_mass, store_density, HALO, BX, BY, 32, mass_fields)
    density = jnp.concatenate(
        [flat_ref[pl.ds(b, BX, stride=BY), :] for b in range(BY)], axis=0
    )
    spread = dot(table_ref[...], density, ((1,), (1,)))
    modes_ref[pl.ds(0, GZ, stride=2), :] = spread[:, :128]
    modes_ref[pl.ds(1, GZ, stride=2), :] = spread[:, 128:]


def second_kernel(own_ref, first_ref, stepped_ref):
    def load_first(i):
        return [first_ref[q, i - 2] for q in range(5)]

    def store_stepped(i, states, rates):
        for q in range(5):
            second = states[q] + time_step * rates[q]
            stepped_ref[q, i - HALO] = 0.5 * own_ref[q, i - HALO] + 0.5 * second

    euler_stage(load_first, store_stepped, HALO, BX, BY, 8)


def ends_kernel(modes_ref, table_ref, kappa_ref, expand_ref, pick_ref, raw_ref, ends_ref, plane_ref):
    for tile in range(2):
        lines = [modes_ref[pl.ds(k * 2 + tile, COLS, stride=8), :] for k in range(4)]
        for g, value in enumerate(swap_groups(lines, 32)):
            plane_ref[pl.ds(tile * 4 + g, COLS, stride=BY), :] = value
    power = jnp.exp(-dot(kappa_ref[...], expand_ref[:, :128], ((0,), (0,))))
    source = dot(table_ref[...], plane_ref[...])
    x = lax.broadcasted_iota(jnp.int32, (GY, 128), 1) % BX
    rising, falling = source, source
    step = 1
    while step < BX:
        rising = rising + jnp.where(x >= step, power * pltpu.roll(rising, step, 1), 0.0)
        falling = falling + jnp.where(x < BX - step, power * pltpu.roll(falling, 128 - step, 1), 0.0)
        power = power * power
        step *= 2
    ends = dot(pick_ref[0:8, :], rising, ((1,), (1,))) + dot(pick_ref[8:16, :], falling, ((1,), (1,)))
    for r in range(ROWS):
        ends_ref[r * 24 : r * 24 + 8, :] = ends[:, :128]
        ends_ref[r * 24 + 8 : r * 24 + 16, :] = ends[:, 128:]
        ends_ref[r * 24 + 16 : r * 24 + 24, :] = source[0:8]
    raw_ref[:, :128] = rising + falling - source
    raw_ref[:, 128:] = jnp.where(x == 0, falling, pltpu.roll(rising, 128 - BX + 2, 1))


def weigh_kernel(kappa_ref, expand_ref, span_ref, raw_ref, local_ref, left_ref, right_ref):
    kappa = dot(kappa_ref[...], expand_ref[:, :128], ((0,), (0,)))
    flat = kappa <= 0.0
    decay = jnp.exp(-kappa)
    width = jnp.where(flat, 1.0, jnp.exp(kappa) - decay)
    scale = jnp.where(flat, 0.0, -four_pi_g / width)
    images = scale / jnp.where(flat, 1.0, 1.0 - jnp.exp(-GX * kappa))
    for half in range(2):
        lanes = slice(half * 128, half * 128 + 128)
        span = span_ref[:, lanes]
        local_ref[:, lanes] = (scale * decay if half else scale) * raw_ref[:, lanes]
        left_ref[:, lanes] = images * jnp.exp(-kappa * (span + 1.0))
        right_ref[:, lanes] = images * jnp.exp(-kappa * (BX - span))


def join_kernel(
    place_ref, ends_ref, local_ref, left_ref, right_ref, kappa_ref, expand_ref, line_ref, table_ref,
    out_ref, wide_ref,
):
    row = place_ref[0]

    def slab(step):
        return pl.multiple_of(((row + step) & (ROWS - 1)) * 24, 8)

    rising = lax.broadcasted_iota(jnp.int32, (8, GY), 0) % 2 == 0
    block = jnp.exp(-BX * kappa_ref[...])
    total = None
    for d in range(ROWS, 0, -1):
        below, above = slab(ROWS - d), slab(d)
        both = []
        for part in (0, 8):
            both.append((ends_ref[pl.ds(below + part, 8), :], ends_ref[pl.ds(above + part, 8), :]))
        low = jnp.concatenate([both[0][0], both[1][0]], axis=1)
        high = jnp.concatenate([both[0][1], both[1][1]], axis=1)
        value = jnp.where(rising, low, high)
        total = value if total is None else value + block * total
    from_left = dot(jnp.where(rising, total, 0.0), expand_ref[0:8, :] * 2.0, ((0,), (0,)))
    from_right = dot(jnp.where(rising, 0.0, total), expand_ref[0:8, :] * 2.0, ((0,), (0,)))
    field = local_ref[...] + left_ref[...] * from_left + right_ref[...] * from_right
    lane = lax.broadcasted_iota(jnp.int32, (8, 128), 1)
    halves = []
    for half in range(2):
        line = jnp.zeros((8, 128), jnp.float32)
        for g in range(4):
            values = ends_ref[pl.ds(slab(ROWS - half * 4 - g) + 16, 8), :]
            values = jnp.where(lane < BX, values, 0.0)
            line = line + (pltpu.roll(values, g * BX, 1) if g else values)
        halves.append(line)
    line = jnp.concatenate(halves, axis=1)
    line = line - jnp.sum(line, axis=1, keepdims=True) * (1.0 / GX)
    mean = dot(line, line_ref[...])
    first = lax.broadcasted_iota(jnp.int32, (8, 256), 0) == 0
    mean = jnp.where(jnp.logical_and(first, place_ref[1] == 0), mean, 0.0)
    field = jnp.concatenate([field[0:8] + mean, field[8:]], axis=0)
    potential = dot(table_ref[...], field)
    for part in range(2):
        base, side = part * (GY + 16), potential[:, part * 128 : part * 128 + 128]
        wide_ref[base + 8 : base + 8 + GY, :] = side
        wide_ref[base : base + 8, :] = side[GY - 8 :]
        wide_ref[base + 8 + GY : base + 16 + GY, :] = side[:8]
    strips = [wide_ref[pl.ds(8 + yl, COLS, stride=BY), :] for yl in range(BY)]
    below = wide_ref[pl.ds(7, COLS, stride=BY), :]
    above = wide_ref[pl.ds(16, COLS, stride=BY), :]
    x = lax.broadcasted_iota(jnp.int32, (COLS, 128), 1) % BX
    sides = jnp.zeros((COLS, 128), jnp.float32)
    for yl in range(BY):
        edge = wide_ref[pl.ds(GY + 16 + 8 + yl, COLS, stride=BY), :]
        sides = jnp.where(x == yl, pltpu.roll(edge, yl, 1) if yl else edge, sides)
        sides = jnp.where(x == BY + yl, pltpu.roll(edge, BY - 1 + yl, 1), sides)
    strips = strips + [below, above, sides, sides]
    for quad in range(3):
        for k, value in enumerate(swap_groups(strips[quad * 4 : quad * 4 + 4], 32)):
            out_ref[pl.ds(k * 3 + quad, COLS, stride=12), :] = value


def kick_kernel(owner_ref, stepped_ref, modes_ref, table_ref, out_ref, phi_ref, kicked_ref):
    table = table_ref[...]
    parts = []
    for quad in range(3):
        block = modes_ref[pl.ds(quad, GZ, stride=3), :]
        parts.append(dot(block, table, ((0,), (0,))))
    for yl in range(BY):
        phi_ref[pl.ds(BY + yl, BX, stride=BY), :] = parts[yl // 4][(yl % 4) * 32 : (yl % 4) * 32 + 32]
    phi_ref[0:BY, :] = parts[2][64 : 64 + BY]
    phi_ref[BY + BX * BY :, :] = parts[2][64 + BY : 64 + 2 * BY]
    phi = phi_ref[...].reshape(BX + 2, BY, GZ)
    mid = phi[1 : 1 + BX]
    below = parts[2][0:32].reshape(BX, 1, GZ)
    above = parts[2][32:64].reshape(BX, 1, GZ)
    grad_x = 0.5 * (phi[2:] - phi[:BX])
    lower = jnp.concatenate([below, mid[:, : BY - 1]], axis=1)
    upper = jnp.concatenate([mid[:, 1:], above], axis=1)
    grad_y = 0.5 * (upper - lower)
    grad_z = 0.5 * (pltpu.roll(mid, GZ - 1, 2) - pltpu.roll(mid, 1, 2))
    grads = (grad_x, grad_y, grad_z)
    density = stepped_ref[0]
    momenta = [stepped_ref[1 + d] for d in range(3)]
    work = momenta[0] * grad_x + momenta[1] * grad_y + momenta[2] * grad_z
    cells = BX * BY
    kicked_ref[0:cells, :] = density.reshape(cells, GZ)
    for d in range(3):
        value = momenta[d] - time_step * density * grads[d]
        kicked_ref[(1 + d) * cells : (2 + d) * cells, :] = value.reshape(cells, GZ)
    kicked_ref[4 * cells :, :] = (stepped_ref[4] - time_step * work).reshape(cells, GZ)
    for q in range(5):
        for xl in range(2):
            for part in range(2):
                base = (q * BX + xl * PE + part * 8) * BY
                lines = [kicked_ref[pl.ds(base + b, 8, stride=BY), :] for b in range(BY)]
                rows = q * PE + part * 8
                for zl, value in enumerate(swap_groups(lines, PE)):
                    out_ref[owner_ref[xl * 8 + zl], rows : rows + 8, :] = value


def spread_kernel(place_ref, recv_ref, out_ref):
    shift = place_ref[0]
    live = lax.broadcasted_iota(jnp.int32, (CAP, 128), 0) < place_ref[1]
    for q in range(5):
        for tile in range(2 * PE):
            a, half = tile // 2, tile % 2
            lines = recv_ref[pl.ds(half * BRICK + q * PE + a, CAP, stride=2 * BRICK), :]
            turned = pltpu.roll(lines, shift, 0)
            out_ref[q, :, tile * 128 : (tile + 1) * 128] = jnp.where(live, turned, 0.0)


def call(kernel, outs, ins, scratch=()):
    shapes = [jax.ShapeDtypeStruct(s, jnp.float32) for s in outs]
    many = len(outs) > 1
    return pl.pallas_call(
        kernel,
        out_shape=tuple(shapes) if many else shapes[0],
        in_specs=[SM if i in ins[1] else VM for i in range(ins[0])],
        out_specs=tuple([VM] * len(outs)) if many else VM,
        scratch_shapes=[pltpu.VMEM(s, jnp.float32) for s in scratch],
        compiler_params=PARAMS,
    )


def gather_counts(counts):
    copies = jnp.broadcast_to(counts.astype(jnp.float32).reshape(1, 1, 1), (COLS, 1, 128))
    return lax.all_to_all(copies, "col", split_axis=0, concat_axis=0, tiled=True)


def on_device(fields, counts):
    my_row = lax.axis_index("row")
    my_column = lax.axis_index("col")
    staged = call(stage_kernel, [(COLS * BRICK, 128)], (1, ()))(fields.transpose(1, 0, 2))
    spread_counts = gather_counts(counts)
    row_counts = spread_counts[:, 0, 0].astype(jnp.int32)
    column_ids = jnp.arange(COLS, dtype=jnp.int32)
    starts = jnp.sum(
        jnp.where(column_ids[None, :] < column_ids[:, None], row_counts[None, :], 0), axis=1
    )
    own_start = jnp.sum(jnp.where(column_ids < my_column, row_counts, 0))
    y_patch = my_column // 2
    wanted = jnp.arange(LINES, dtype=jnp.int32) * 16 + y_patch
    owners = jnp.sum((starts[None, :] <= wanted[:, None]).astype(jnp.int32), axis=1) - 1
    turn = own_start % CAP

    sent = call(turn_kernel, [(COLS * BRICK, 128)], (3, (0,)))(
        my_column.reshape(1), spread_counts, staged
    )
    arrived = lax.all_to_all(
        sent.reshape(COLS, BRICK, 128), "col", split_axis=0, concat_axis=0, tiled=True
    )
    own, xfirst, xlast, yfirst, ylast = call(
        unpack_kernel,
        [
            (5, BX, BY, GZ),
            (5, HALO, BY, GZ),
            (5, HALO, BY, GZ),
            (5, BX, HALO, GZ),
            (5, BX, HALO, GZ),
        ],
        (2, (0,)),
        [(5 * BX * BY, GZ)],
    )(owners, arrived)

    def ring(count, step):
        return [(i, (i + step) % count) for i in range(count)]

    xlow = lax.ppermute(xlast, "row", ring(ROWS, 1))
    xhigh = lax.ppermute(xfirst, "row", ring(ROWS, -1))
    ylow = lax.ppermute(ylast, "col", ring(COLS, 1))
    yhigh = lax.ppermute(yfirst, "col", ring(COLS, -1))
    edges = jnp.concatenate([xlow[:, 2:4], xhigh[:, 0:2]], axis=1)
    clow = lax.ppermute(edges[:, :, BY - HALO :], "col", ring(COLS, 1))
    chigh = lax.ppermute(edges[:, :, :HALO], "col", ring(COLS, -1))

    table_z = hartley(GZ)
    table_x = hartley(GX)
    wide = (5, BX + 2 * HALO, BY + 2 * HALO, GZ)
    first, modes = call(
        euler_kernel, [(5, BX + HALO, BY + 2 * HALO, GZ), (256, 128)], (8, ()), [wide, (BX * BY, GZ)]
    )(own, xlow, xhigh, ylow, yhigh, clow, chigh, jnp.asarray(table_z))
    planes = lax.all_to_all(
        modes.reshape(COLS, 8, 128), "col", split_axis=0, concat_axis=0, tiled=True
    )
    kappa = jnp.asarray(np.repeat(kappas(), 2, axis=0).astype(np.float32))
    kappa = lax.dynamic_slice_in_dim(kappa, my_column * 8, 8, axis=0)
    expand = jnp.asarray(lane_expand())
    square = (GY, 256)
    stepped = call(second_kernel, [(5, BX, BY, GZ)], (2, ()))(own, first)
    planes, stepped, kappa = lax.optimization_barrier((planes, stepped, kappa))
    raw, ends = call(ends_kernel, [square, (ROWS * 24, 128)], (5, ()), [(GY, 128)])(
        planes.reshape(256, 128), jnp.asarray(table_x), kappa, expand, jnp.asarray(lane_picks())
    )
    local, left, right = call(weigh_kernel, [square] * 3, (4, ()))(
        kappa, expand, jnp.asarray(lane_spans()[None, :]), raw
    )
    ends = lax.all_to_all(
        ends.reshape(ROWS, 24, 128), "row", split_axis=0, concat_axis=0, tiled=True
    )
    strips = call(join_kernel, [(COLS * 12, 128)], (9, (0,)), [(2 * (GY + 16), 128)])(
        jnp.stack([my_row, my_column]),
        ends.reshape(ROWS * 24, 128),
        local,
        left,
        right,
        kappa,
        expand,
        jnp.asarray(mean_line()),
        jnp.asarray(table_x),
    )
    strips = lax.all_to_all(
        strips.reshape(COLS, 1, 1536), "col", split_axis=0, concat_axis=0, tiled=True
    )
    returned = call(
        kick_kernel,
        [(COLS, BRICK, 128)],
        (4, (0,)),
        [((BX + 2) * BY, GZ), (5 * BX * BY, GZ)],
    )(owners, stepped, strips.reshape(COLS * 12, 128), jnp.asarray(table_z))
    came_back = lax.all_to_all(returned, "col", split_axis=0, concat_axis=0, tiled=True)
    home = jnp.stack([(CAP - turn) % CAP, counts[0, 0]])
    result = call(spread_kernel, [(5, CAP, PE * PE * PE)], (2, (0,)))(
        home, came_back.reshape(COLS * BRICK, 128)
    )
    return result.transpose(1, 0, 2)


def solution(mesh):
    return jax.shard_map(
        on_device,
        mesh=mesh,
        in_specs=(P(("row", "col"), None, None), P("row", "col")),
        out_specs=P(("row", "col"), None, None),
        check_vma=False,
    )
```

```python
import math

import jax
import jax.numpy as jnp
import numpy as np
from jax import lax
from jax.experimental import pallas as pl
from jax.experimental.pallas import tpu as pltpu
from jax.sharding import PartitionSpec as P

PE = 16
GX = 256
GY = 256
GZ = 128
ROWS = 8
COLS = 32
BX = GX // ROWS
BY = GY // COLS
CAP = 16
LINES = 16
BRICK = 5 * PE
HALO = 4

time_step = 0.03
four_pi_g = 10.0

PARAMS = pltpu.CompilerParams(vmem_limit_bytes=16 * 2**20)
VM = pl.BlockSpec(memory_space=pltpu.VMEM)
SM = pl.BlockSpec(memory_space=pltpu.SMEM)


def hartley(length):
    index = np.arange(length)
    angle = 2.0 * np.pi / length * (index[:, None] * index[None, :] % length)
    return ((np.cos(angle) + np.sin(angle)) / math.sqrt(length)).astype(np.float32)


def kappas():
    wave_y = np.sin(np.pi * np.arange(GY) / GY) ** 2
    wave_z = np.sin(np.pi * np.arange(GZ) / GZ) ** 2
    return 2.0 * np.arcsinh(np.sqrt(wave_z[:, None] + wave_y[None, :]))


def lane_spans():
    inner = np.arange(128) % BX
    return np.concatenate([inner, np.where(inner == 0, -1, BX)]).astype(np.float32)


def lane_expand():
    lanes = np.arange(256) % 128 // BX
    return 0.5 * (np.arange(8)[:, None] // 2 == lanes[None, :]).astype(np.float32)


def lane_picks():
    picks = np.zeros((16, 128), np.float32)
    for k in range(4):
        picks[2 * k, k * BX + BX - 1] = 1.0
        picks[8 + 2 * k + 1, k * BX] = 1.0
    return picks


def dot(left, right, dims=((1,), (0,))):
    return lax.dot_general(
        left,
        right,
        (dims, ((), ())),
        precision=lax.Precision.HIGHEST,
        preferred_element_type=jnp.float32,
    )


def swap_groups(arrays, group):
    count = len(arrays)
    lane = lax.broadcasted_iota(jnp.int32, arrays[0].shape, 1) // group
    arrays = list(arrays)
    distance = count // 2
    while distance:
        upper = (lane & distance) != 0
        for i in range(count):
            if i & distance:
                continue
            low, high = arrays[i], arrays[i + distance]
            arrays[i] = jnp.where(upper, pltpu.roll(high, distance * group, 1), low)
            arrays[i + distance] = jnp.where(
                upper, high, pltpu.roll(low, 128 - distance * group, 1)
            )
        distance //= 2
    return arrays


def stage_kernel(fields_ref, out_ref):
    for q in range(5):
        for tile in range(2 * PE):
            a, half = tile // 2, tile % 2
            slots = fields_ref[q, :, tile * 128 : (tile + 1) * 128]
            out_ref[pl.ds(half * BRICK + q * PE + a, CAP, stride=2 * BRICK), :] = slots


def turn_kernel(column_ref, counts_ref, staged_ref, out_ref):
    counts = counts_ref[...].reshape(COLS, 128)
    before = lax.broadcasted_iota(jnp.int32, (COLS, 128), 0) < column_ref[0]
    start = (jnp.sum(jnp.where(before, counts, 0.0)) * (1.0 / 128.0)).astype(jnp.int32)
    size = 2 * BRICK
    for y in range(CAP):
        source = pl.multiple_of(((y - start) & (CAP - 1)) * size, 8)
        out_ref[y * size : (y + 1) * size, :] = staged_ref[pl.ds(source, size), :]


def unpack_kernel(owner_ref, recv_ref, own_ref, xfirst_ref, xlast_ref, yfirst_ref, ylast_ref, flat_ref):
    for q in range(5):
        for xl in range(2):
            for part in range(2):
                rows = q * PE + part * 8
                lines = [
                    recv_ref[owner_ref[xl * 8 + zl], rows : rows + 8, :] for zl in range(8)
                ]
                for b, value in enumerate(swap_groups(lines, PE)):
                    base = (q * BX + xl * PE + part * 8) * BY + b
                    flat_ref[pl.ds(base, 8, stride=BY), :] = value
    block = flat_ref[...].reshape(5, BX, BY, GZ)
    own_ref[...] = block
    xfirst_ref[...] = block[:, :HALO]
    xlast_ref[...] = block[:, BX - HALO :]
    yfirst_ref[...] = block[:, :, :HALO]
    ylast_ref[...] = block[:, :, BY - HALO :]


def corner_kernel(ylow_ref, yhigh_ref, up_ref, down_ref):
    for ref, first in ((up_ref, BX - 2), (down_ref, 0)):
        ref[:, :, :HALO] = yhigh_ref[:, first : first + 2]
        ref[:, :, HALO:] = ylow_ref[:, first : first + 2]


def minmod(p, q):
    return jnp.maximum(jnp.minimum(p, q), 0.0) + jnp.minimum(jnp.maximum(p, q), 0.0)


def half_flux(states, direction, sign):
    if len(states) == 2:
        return [0.5 * states[1] + sign * 2.0 * states[0]]
    density, energy = states[0], states[4]
    inverse = 1.0 / density
    velocity = 0.5 * states[1 + direction] * inverse
    squares = states[1] * states[1] + states[2] * states[2] + states[3] * states[3]
    pressure = 0.4 * energy - (0.2 * squares) * inverse
    pieces = [0.5 * states[1 + direction]]
    for component in range(3):
        term = states[1 + component] * velocity
        if component == direction:
            term = term + 0.5 * pressure
        pieces.append(term)
    pieces.append((energy + pressure) * velocity)
    if sign > 0:
        return [piece + 2.0 * state for piece, state in zip(pieces, states)]
    return [piece - 2.0 * state for piece, state in zip(pieces, states)]


def edge_terms(states, slopes, direction):
    halves = [0.5 * slope for slope in slopes]
    upper = half_flux([u + h for u, h in zip(states, halves)], direction, 1)
    lower = half_flux([u - h for u, h in zip(states, halves)], direction, -1)
    return upper, lower


def line_change(states, direction, axis):
    size = states[0].shape[axis]
    gaps = [pltpu.roll(u, size - 1, axis) - u for u in states]
    slopes = [minmod(pltpu.roll(g, 1, axis), g) for g in gaps]
    upper, lower = edge_terms(states, slopes, direction)
    faces = [u + pltpu.roll(w, size - 1, axis) for u, w in zip(upper, lower)]
    return [f - pltpu.roll(f, 1, axis) for f in faces]


def all_fields(states, direction):
    return states


def mass_fields(states, direction):
    return [states[0], states[1 + direction]]


def euler_stage(load, store, first_row, count, keep, unroll, pick=all_fields):
    def slopes_of(low, mid, high):
        return [minmod(b - a, c - b) for a, b, c in zip(low, mid, high)]

    cut = lambda states: [u[:keep] for u in states]
    cut_x = lambda states: cut(pick(states, 0))
    r0, r1, r2, r3 = [cut_x(load(first_row + k)) for k in (-2, -1, 0, 1)]
    upper_prev, _ = edge_terms(r1, slopes_of(r0, r1, r2), 0)
    upper_now, lower_now = edge_terms(r2, slopes_of(r1, r2, r3), 0)
    face = [u + w for u, w in zip(upper_prev, lower_now)]

    def step(k, carry):
        face_low, upper_here = carry
        i = first_row + k
        here, above, far = load(i), cut_x(load(i + 1)), cut_x(load(i + 2))
        mine = cut(here)
        upper_next, lower_next = edge_terms(above, slopes_of(pick(mine, 0), above, far), 0)
        face_high = [u + w for u, w in zip(upper_here, lower_next)]
        change = [h - l for h, l in zip(face_high, face_low)]
        along_y = cut(line_change(pick(here, 1), 1, 0))
        along_z = line_change(pick(mine, 2), 2, 1)
        rate = [-(a + b + c) for a, b, c in zip(change, along_y, along_z)]
        store(i, mine, rate)
        return tuple(face_high), tuple(upper_next)

    lax.fori_loop(0, count, step, (tuple(face), tuple(upper_now)), unroll=unroll)


def euler_kernel(
    own_ref, xlow_ref, xhigh_ref, ylow_ref, yhigh_ref, clow_ref, chigh_ref, table_ref,
    first_ref, modes_ref, ext_ref, flat_ref,
):
    low, high = slice(BY + HALO, BY + 2 * HALO), slice(BY, BY + HALO)
    inner = slice(HALO, HALO + BX)
    ext_ref[:, inner, 0:BY] = own_ref[...]
    ext_ref[:, 0:HALO, 0:BY] = xlow_ref[...]
    ext_ref[:, HALO + BX :, 0:BY] = xhigh_ref[...]
    ext_ref[:, inner, high] = yhigh_ref[...]
    ext_ref[:, inner, low] = ylow_ref[...]
    for start, ref in ((0, clow_ref), (HALO + BX, chigh_ref)):
        ext_ref[:, start : start + 2, BY:] = ref[...]
        ext_ref[:, start + 2 : start + 4, BY:] = ref[...]

    def load_ext(i):
        return [ext_ref[q, i] for q in range(5)]

    def store_first(i, states, rates):
        for q in range(5):
            first_ref[q, i - 2] = states[q] + time_step * rates[q]

    euler_stage(load_ext, store_first, 2, BX + 4, BY + 2 * HALO, 6)

    def load_mass(i):
        return [first_ref[q, i - 2] for q in range(4)]

    def store_density(i, states, rates):
        second = states[0] + time_step * rates[0]
        row = pl.multiple_of((i - HALO) * BY, BY)
        flat_ref[pl.ds(row, BY), :] = 0.5 * ext_ref[0, i, 0:BY] + 0.5 * second

    euler_stage(load_mass, store_density, HALO, BX, BY, 32, mass_fields)
    density = jnp.concatenate(
        [flat_ref[pl.ds(b, BX, stride=BY), :] for b in range(BY)], axis=0
    )
    spread = dot(table_ref[...], density, ((1,), (1,)))
    modes_ref[pl.ds(0, GZ, stride=2), :] = spread[:, :128]
    modes_ref[pl.ds(1, GZ, stride=2), :] = spread[:, 128:]


def second_kernel(own_ref, first_ref, stepped_ref):
    def load_first(i):
        return [first_ref[q, i - 2] for q in range(5)]

    def store_stepped(i, states, rates):
        for q in range(5):
            second = states[q] + time_step * rates[q]
            stepped_ref[q, i - HALO] = 0.5 * own_ref[q, i - HALO] + 0.5 * second

    euler_stage(load_first, store_stepped, HALO, BX, BY, 8)


def ends_kernel(modes_ref, table_ref, kappa_ref, expand_ref, pick_ref, raw_ref, ends_ref, plane_ref):
    for tile in range(2):
        lines = [modes_ref[pl.ds(k * 2 + tile, COLS, stride=8), :] for k in range(4)]
        for g, value in enumerate(swap_groups(lines, 32)):
            plane_ref[pl.ds(tile * 4 + g, COLS, stride=BY), :] = value
    power = jnp.exp(-dot(kappa_ref[...], expand_ref[:, :128], ((0,), (0,))))
    source = dot(table_ref[...], plane_ref[...])
    x = lax.broadcasted_iota(jnp.int32, (GY, 128), 1) % BX
    rising, falling = source, source
    step = 1
    while step < BX:
        rising = rising + jnp.where(x >= step, power * pltpu.roll(rising, step, 1), 0.0)
        falling = falling + jnp.where(x < BX - step, power * pltpu.roll(falling, 128 - step, 1), 0.0)
        power = power * power
        step *= 2
    ends = dot(pick_ref[0:8, :], rising, ((1,), (1,))) + dot(pick_ref[8:16, :], falling, ((1,), (1,)))
    for r in range(ROWS):
        ends_ref[r * 24 : r * 24 + 8, :] = ends[:, :128]
        ends_ref[r * 24 + 8 : r * 24 + 16, :] = ends[:, 128:]
        ends_ref[r * 24 + 16 : r * 24 + 24, :] = source[0:8]
    raw_ref[:, :128] = rising + falling - source
    raw_ref[:, 128:] = jnp.where(x == 0, falling, pltpu.roll(rising, 128 - BX + 2, 1))


def weigh_kernel(kappa_ref, expand_ref, span_ref, raw_ref, local_ref, left_ref, right_ref):
    kappa = dot(kappa_ref[...], expand_ref[:, :128], ((0,), (0,)))
    flat = kappa <= 0.0
    decay = jnp.exp(-kappa)
    width = jnp.where(flat, 1.0, jnp.exp(kappa) - decay)
    scale = jnp.where(flat, 0.0, -four_pi_g / width)
    images = scale / jnp.where(flat, 1.0, 1.0 - jnp.exp(-GX * kappa))
    for half in range(2):
        lanes = slice(half * 128, half * 128 + 128)
        span = span_ref[:, lanes]
        local_ref[:, lanes] = (scale * decay if half else scale) * raw_ref[:, lanes]
        left_ref[:, lanes] = images * jnp.exp(-kappa * (span + 1.0))
        right_ref[:, lanes] = images * jnp.exp(-kappa * (BX - span))


def join_kernel(
    place_ref, ends_ref, local_ref, left_ref, right_ref, kappa_ref, expand_ref, table_ref,
    out_ref, wide_ref,
):
    row = place_ref[0]

    def slab(step):
        return pl.multiple_of(((row + step) & (ROWS - 1)) * 24, 8)

    rising = lax.broadcasted_iota(jnp.int32, (8, GY), 0) % 2 == 0
    block = jnp.exp(-BX * kappa_ref[...])
    total = None
    for d in range(ROWS, 0, -1):
        below, above = slab(ROWS - d), slab(d)
        both = []
        for part in (0, 8):
            both.append((ends_ref[pl.ds(below + part, 8), :], ends_ref[pl.ds(above + part, 8), :]))
        low = jnp.concatenate([both[0][0], both[1][0]], axis=1)
        high = jnp.concatenate([both[0][1], both[1][1]], axis=1)
        value = jnp.where(rising, low, high)
        total = value if total is None else value + block * total
    from_left = dot(jnp.where(rising, total, 0.0), expand_ref[0:8, :] * 2.0, ((0,), (0,)))
    from_right = dot(jnp.where(rising, 0.0, total), expand_ref[0:8, :] * 2.0, ((0,), (0,)))
    field = local_ref[...] + left_ref[...] * from_left + right_ref[...] * from_right
    lane = lax.broadcasted_iota(jnp.int32, (8, 128), 1)
    halves = []
    for half in range(2):
        line = jnp.zeros((8, 128), jnp.float32)
        for g in range(4):
            values = ends_ref[pl.ds(slab(ROWS - half * 4 - g) + 16, 8), :]
            values = jnp.where(lane < BX, values, 0.0)
            line = line + (pltpu.roll(values, g * BX, 1) if g else values)
        halves.append(line)
    line = jnp.concatenate(halves, axis=1)
    line = line - jnp.sum(line, axis=1, keepdims=True) * (1.0 / GX)
    source = lax.broadcasted_iota(jnp.int32, (GX, 128), 0)
    target = lax.broadcasted_iota(jnp.int32, (GX, 128), 1)
    target = jnp.where(target == BX + 1, -1, target)
    gap = jnp.abs(source // BX * BX + target - source % BX).astype(jnp.float32)
    shape = four_pi_g * (gap * (0.5 - gap * (0.5 / GX)) - (GX * GX - 1.0) / (12.0 * GX))
    mean = dot(line, shape)
    first = lax.broadcasted_iota(jnp.int32, (8, 128), 0) == 0
    mean = jnp.where(jnp.logical_and(first, place_ref[1] == 0), mean, 0.0)
    inner = jnp.where(lane < BX, mean, 0.0)
    low, high = pltpu.roll(mean, 128 - BX - 1, 1), pltpu.roll(mean, 128 - BX + 1, 1)
    outer = jnp.where(lane == 0, low, jnp.where(lane == 1, high, 0.0))
    mean = jnp.concatenate([inner, outer], axis=1)
    field = jnp.concatenate([field[0:8] + mean, field[8:]], axis=0)
    potential = dot(table_ref[...], field)
    for part in range(2):
        base, side = part * (GY + 16), potential[:, part * 128 : part * 128 + 128]
        wide_ref[base + 8 : base + 8 + GY, :] = side
        wide_ref[base : base + 8, :] = side[GY - 8 :]
        wide_ref[base + 8 + GY : base + 16 + GY, :] = side[:8]
    strips = [wide_ref[pl.ds(8 + yl, COLS, stride=BY), :] for yl in range(BY)]
    below = wide_ref[pl.ds(7, COLS, stride=BY), :]
    above = wide_ref[pl.ds(16, COLS, stride=BY), :]
    x = lax.broadcasted_iota(jnp.int32, (COLS, 128), 1) % BX
    sides = jnp.zeros((COLS, 128), jnp.float32)
    for yl in range(BY):
        edge = wide_ref[pl.ds(GY + 16 + 8 + yl, COLS, stride=BY), :]
        sides = jnp.where(x == yl, pltpu.roll(edge, yl, 1) if yl else edge, sides)
        sides = jnp.where(x == BY + yl, pltpu.roll(edge, BY - 1 + yl, 1), sides)
    strips = strips + [below, above, sides, sides]
    for quad in range(3):
        for k, value in enumerate(swap_groups(strips[quad * 4 : quad * 4 + 4], 32)):
            out_ref[pl.ds(k * 3 + quad, COLS, stride=12), :] = value


def kick_kernel(owner_ref, stepped_ref, modes_ref, table_ref, out_ref, phi_ref, kicked_ref):
    table = table_ref[...]
    parts = []
    for quad in range(3):
        block = modes_ref[pl.ds(quad, GZ, stride=3), :]
        parts.append(dot(block, table, ((0,), (0,))))
    for yl in range(BY):
        phi_ref[pl.ds(BY + yl, BX, stride=BY), :] = parts[yl // 4][(yl % 4) * 32 : (yl % 4) * 32 + 32]
    phi_ref[0:BY, :] = parts[2][64 : 64 + BY]
    phi_ref[BY + BX * BY :, :] = parts[2][64 + BY : 64 + 2 * BY]
    phi = phi_ref[...].reshape(BX + 2, BY, GZ)
    mid = phi[1 : 1 + BX]
    below = parts[2][0:32].reshape(BX, 1, GZ)
    above = parts[2][32:64].reshape(BX, 1, GZ)
    grad_x = 0.5 * (phi[2:] - phi[:BX])
    lower = jnp.concatenate([below, mid[:, : BY - 1]], axis=1)
    upper = jnp.concatenate([mid[:, 1:], above], axis=1)
    grad_y = 0.5 * (upper - lower)
    grad_z = 0.5 * (pltpu.roll(mid, GZ - 1, 2) - pltpu.roll(mid, 1, 2))
    grads = (grad_x, grad_y, grad_z)
    density = stepped_ref[0]
    momenta = [stepped_ref[1 + d] for d in range(3)]
    work = momenta[0] * grad_x + momenta[1] * grad_y + momenta[2] * grad_z
    cells = BX * BY
    kicked_ref[0:cells, :] = density.reshape(cells, GZ)
    for d in range(3):
        value = momenta[d] - time_step * density * grads[d]
        kicked_ref[(1 + d) * cells : (2 + d) * cells, :] = value.reshape(cells, GZ)
    kicked_ref[4 * cells :, :] = (stepped_ref[4] - time_step * work).reshape(cells, GZ)
    for q in range(5):
        for xl in range(2):
            for part in range(2):
                base = (q * BX + xl * PE + part * 8) * BY
                lines = [kicked_ref[pl.ds(base + b, 8, stride=BY), :] for b in range(BY)]
                rows = q * PE + part * 8
                for zl, value in enumerate(swap_groups(lines, PE)):
                    out_ref[owner_ref[xl * 8 + zl], rows : rows + 8, :] = value


def spread_kernel(place_ref, recv_ref, out_ref):
    shift = place_ref[0]
    live = lax.broadcasted_iota(jnp.int32, (CAP, 128), 0) < place_ref[1]
    field = pl.program_id(0) * PE
    for tile in range(2 * PE):
        a, half = tile // 2, tile % 2
        lines = recv_ref[pl.ds(field + (half * BRICK + a), CAP, stride=2 * BRICK), :]
        turned = pltpu.roll(lines, shift, 0)
        out_ref[:, tile * 128 : (tile + 1) * 128] = jnp.where(live, turned, 0.0)


def call(kernel, outs, ins, scratch=()):
    shapes = [jax.ShapeDtypeStruct(s, jnp.float32) for s in outs]
    many = len(outs) > 1
    return pl.pallas_call(
        kernel,
        out_shape=tuple(shapes) if many else shapes[0],
        in_specs=[SM if i in ins[1] else VM for i in range(ins[0])],
        out_specs=tuple([VM] * len(outs)) if many else VM,
        scratch_shapes=[pltpu.VMEM(s, jnp.float32) for s in scratch],
        compiler_params=PARAMS,
    )


def gather_counts(counts):
    copies = jnp.broadcast_to(counts.astype(jnp.float32).reshape(1, 1, 1), (COLS, 1, 128))
    return lax.all_to_all(copies, "col", split_axis=0, concat_axis=0, tiled=True)


def on_device(fields, counts):
    my_row = lax.axis_index("row")
    my_column = lax.axis_index("col")
    staged = call(stage_kernel, [(COLS * BRICK, 128)], (1, ()))(fields.transpose(1, 0, 2))
    spread_counts = gather_counts(counts)
    row_counts = spread_counts[:, 0, 0].astype(jnp.int32)
    column_ids = jnp.arange(COLS, dtype=jnp.int32)
    starts = jnp.sum(
        jnp.where(column_ids[None, :] < column_ids[:, None], row_counts[None, :], 0), axis=1
    )
    own_start = jnp.sum(jnp.where(column_ids < my_column, row_counts, 0))
    y_patch = my_column // 2
    wanted = jnp.arange(LINES, dtype=jnp.int32) * 16 + y_patch
    owners = jnp.sum((starts[None, :] <= wanted[:, None]).astype(jnp.int32), axis=1) - 1
    turn = own_start % CAP

    sent = call(turn_kernel, [(COLS * BRICK, 128)], (3, (0,)))(
        my_column.reshape(1), spread_counts, staged
    )
    arrived = lax.all_to_all(
        sent.reshape(COLS, BRICK, 128), "col", split_axis=0, concat_axis=0, tiled=True
    )
    own, xfirst, xlast, yfirst, ylast = call(
        unpack_kernel,
        [
            (5, BX, BY, GZ),
            (5, HALO, BY, GZ),
            (5, HALO, BY, GZ),
            (5, BX, HALO, GZ),
            (5, BX, HALO, GZ),
        ],
        (2, (0,)),
        [(5 * BX * BY, GZ)],
    )(owners, arrived)

    def ring(count, step):
        return [(i, (i + step) % count) for i in range(count)]

    xlow = lax.ppermute(xlast, "row", ring(ROWS, 1))
    xhigh = lax.ppermute(xfirst, "row", ring(ROWS, -1))
    ylow = lax.ppermute(ylast, "col", ring(COLS, 1))
    yhigh = lax.ppermute(yfirst, "col", ring(COLS, -1))
    up, down = call(corner_kernel, [(5, 2, BY, GZ)] * 2, (2, ()))(ylow, yhigh)
    clow = lax.ppermute(up, "row", ring(ROWS, 1))
    chigh = lax.ppermute(down, "row", ring(ROWS, -1))

    table_z = hartley(GZ)
    table_x = hartley(GX)
    wide = (5, BX + 2 * HALO, BY + 2 * HALO, GZ)
    first, modes = call(
        euler_kernel, [(5, BX + HALO, BY + 2 * HALO, GZ), (256, 128)], (8, ()), [wide, (BX * BY, GZ)]
    )(own, xlow, xhigh, ylow, yhigh, clow, chigh, jnp.asarray(table_z))
    planes = lax.all_to_all(
        modes.reshape(COLS, 8, 128), "col", split_axis=0, concat_axis=0, tiled=True
    )
    kappa = jnp.asarray(np.repeat(kappas(), 2, axis=0).astype(np.float32))
    kappa = lax.dynamic_slice_in_dim(kappa, my_column * 8, 8, axis=0)
    expand = jnp.asarray(lane_expand())
    square = (GY, 256)
    stepped = call(second_kernel, [(5, BX, BY, GZ)], (2, ()))(own, first)
    planes, stepped, kappa = lax.optimization_barrier((planes, stepped, kappa))
    raw, ends = call(ends_kernel, [square, (ROWS * 24, 128)], (5, ()), [(GY, 128)])(
        planes.reshape(256, 128), jnp.asarray(table_x), kappa, expand, jnp.asarray(lane_picks())
    )
    local, left, right = call(weigh_kernel, [square] * 3, (4, ()))(
        kappa, expand, jnp.asarray(lane_spans()[None, :]), raw
    )
    ends = lax.all_to_all(
        ends.reshape(ROWS, 24, 128), "row", split_axis=0, concat_axis=0, tiled=True
    )
    strips = call(join_kernel, [(COLS * 12, 128)], (8, (0,)), [(2 * (GY + 16), 128)])(
        jnp.stack([my_row, my_column]),
        ends.reshape(ROWS * 24, 128),
        local,
        left,
        right,
        kappa,
        expand,
        jnp.asarray(table_x),
    )
    strips = lax.all_to_all(
        strips.reshape(COLS, 1, 1536), "col", split_axis=0, concat_axis=0, tiled=True
    )
    returned = call(
        kick_kernel,
        [(COLS, BRICK, 128)],
        (4, (0,)),
        [((BX + 2) * BY, GZ), (5 * BX * BY, GZ)],
    )(owners, stepped, strips.reshape(COLS * 12, 128), jnp.asarray(table_z))
    came_back = lax.all_to_all(returned, "col", split_axis=0, concat_axis=0, tiled=True)
    home = jnp.stack([(CAP - turn) % CAP, counts[0, 0]])
    result = pl.pallas_call(
        spread_kernel,
        grid=(5,),
        out_shape=jax.ShapeDtypeStruct((5, CAP, PE * PE * PE), jnp.float32),
        in_specs=[SM, VM],
        out_specs=pl.BlockSpec((None, CAP, PE * PE * PE), lambda q: (q, 0, 0)),
        compiler_params=PARAMS,
    )(home, came_back.reshape(COLS * BRICK, 128))
    return result.transpose(1, 0, 2)


def solution(mesh):
    return jax.shard_map(
        on_device,
        mesh=mesh,
        in_specs=(P(("row", "col"), None, None), P("row", "col")),
        out_specs=P(("row", "col"), None, None),
        check_vma=False,
    )
```

```python
import math

import jax
import jax.numpy as jnp
import numpy as np
from jax import lax
from jax.experimental import pallas as pl
from jax.experimental.pallas import tpu as pltpu
from jax.sharding import PartitionSpec as P

PE = 16
GX = 256
GY = 256
GZ = 128
ROWS = 8
COLS = 32
BX = GX // ROWS
BY = GY // COLS
CAP = 16
LINES = 16
BRICK = 5 * PE
HALO = 4

time_step = 0.03
four_pi_g = 10.0

PARAMS = pltpu.CompilerParams(vmem_limit_bytes=16 * 2**20)
VM = pl.BlockSpec(memory_space=pltpu.VMEM)
SM = pl.BlockSpec(memory_space=pltpu.SMEM)


def hartley(length):
    index = np.arange(length)
    angle = 2.0 * np.pi / length * (index[:, None] * index[None, :] % length)
    return ((np.cos(angle) + np.sin(angle)) / math.sqrt(length)).astype(np.float32)


def kappas():
    wave_y = np.sin(np.pi * np.arange(GY) / GY) ** 2
    wave_z = np.sin(np.pi * np.arange(GZ) / GZ) ** 2
    return 2.0 * np.arcsinh(np.sqrt(wave_z[:, None] + wave_y[None, :]))


def lane_spans():
    inner = np.arange(128) % BX
    return np.concatenate([inner, np.where(inner == 0, -1, BX)]).astype(np.float32)


def lane_expand():
    lanes = np.arange(256) % 128 // BX
    return 0.5 * (np.arange(8)[:, None] // 2 == lanes[None, :]).astype(np.float32)


def lane_picks():
    picks = np.zeros((8, 256), np.float32)
    for k in range(4):
        picks[2 * k, k * BX + BX - 1] = 1.0
        picks[2 * k + 1, 128 + k * BX] = 1.0
    return picks


def dot(left, right, dims=((1,), (0,)), precision=lax.Precision.HIGHEST):
    return lax.dot_general(
        left,
        right,
        (dims, ((), ())),
        precision=precision,
        preferred_element_type=jnp.float32,
    )


def swap_groups(arrays, group):
    count = len(arrays)
    lane = lax.broadcasted_iota(jnp.int32, arrays[0].shape, 1) // group
    arrays = list(arrays)
    distance = count // 2
    while distance:
        upper = (lane & distance) != 0
        for i in range(count):
            if i & distance:
                continue
            low, high = arrays[i], arrays[i + distance]
            arrays[i] = jnp.where(upper, pltpu.roll(high, distance * group, 1), low)
            arrays[i + distance] = jnp.where(
                upper, high, pltpu.roll(low, 128 - distance * group, 1)
            )
        distance //= 2
    return arrays


def stage_kernel(fields_ref, out_ref):
    for q in range(5):
        for tile in range(2 * PE):
            a, half = tile // 2, tile % 2
            slots = fields_ref[q, :, tile * 128 : (tile + 1) * 128]
            out_ref[pl.ds(half * BRICK + q * PE + a, CAP, stride=2 * BRICK), :] = slots


def turn_kernel(column_ref, counts_ref, staged_ref, out_ref):
    counts = counts_ref[...].reshape(COLS, 128)
    before = lax.broadcasted_iota(jnp.int32, (COLS, 128), 0) < column_ref[0]
    start = (jnp.sum(jnp.where(before, counts, 0.0)) * (1.0 / 128.0)).astype(jnp.int32)
    size = 2 * BRICK
    for y in range(CAP):
        source = pl.multiple_of(((y - start) & (CAP - 1)) * size, 8)
        out_ref[y * size : (y + 1) * size, :] = staged_ref[pl.ds(source, size), :]


def unpack_kernel(owner_ref, recv_ref, own_ref, xfirst_ref, xlast_ref, yfirst_ref, ylast_ref):
    for q in range(5):
        for xl in range(2):
            for part in range(2):
                rows = q * PE + part * 8
                lines = [
                    recv_ref[owner_ref[xl * 8 + zl], rows : rows + 8, :] for zl in range(8)
                ]
                for b, value in enumerate(swap_groups(lines, PE)):
                    base = (q * BX + xl * PE + part * 8) * BY + b
                    own_ref[pl.ds(base, 8, stride=BY), :] = value
    block = own_ref[...].reshape(5, BX, BY, GZ)
    xfirst_ref[...] = block[:, :HALO]
    xlast_ref[...] = block[:, BX - HALO :]
    yfirst_ref[...] = block[:, :, :HALO]
    ylast_ref[...] = block[:, :, BY - HALO :]


def corner_kernel(ylow_ref, yhigh_ref, up_ref, down_ref):
    for ref, first in ((up_ref, BX - 2), (down_ref, 0)):
        ref[:, :, :HALO] = yhigh_ref[:, first : first + 2]
        ref[:, :, HALO:] = ylow_ref[:, first : first + 2]


def minmod(p, q):
    return jnp.maximum(jnp.minimum(p, q), 0.0) + jnp.minimum(jnp.maximum(p, q), 0.0)


def half_flux(states, direction, sign):
    if len(states) == 2:
        return [0.5 * states[1] + sign * 2.0 * states[0]]
    density, energy = states[0], states[4]
    inverse = 1.0 / density
    velocity = 0.5 * states[1 + direction] * inverse
    squares = states[1] * states[1] + states[2] * states[2] + states[3] * states[3]
    pressure = 0.4 * energy - (0.2 * squares) * inverse
    pieces = [0.5 * states[1 + direction]]
    for component in range(3):
        term = states[1 + component] * velocity
        if component == direction:
            term = term + 0.5 * pressure
        pieces.append(term)
    pieces.append((energy + pressure) * velocity)
    if sign > 0:
        return [piece + 2.0 * state for piece, state in zip(pieces, states)]
    return [piece - 2.0 * state for piece, state in zip(pieces, states)]


def edge_terms(states, slopes, direction):
    halves = [0.5 * slope for slope in slopes]
    upper = half_flux([u + h for u, h in zip(states, halves)], direction, 1)
    lower = half_flux([u - h for u, h in zip(states, halves)], direction, -1)
    return upper, lower


def line_change(states, direction, axis):
    size = states[0].shape[axis]
    gaps = [pltpu.roll(u, size - 1, axis) - u for u in states]
    slopes = [minmod(pltpu.roll(g, 1, axis), g) for g in gaps]
    upper, lower = edge_terms(states, slopes, direction)
    faces = [u + pltpu.roll(w, size - 1, axis) for u, w in zip(upper, lower)]
    return [f - pltpu.roll(f, 1, axis) for f in faces]


def all_fields(states, direction):
    return states


def mass_fields(states, direction):
    return [states[0], states[1 + direction]]


def euler_stage(load, store, first_row, count, keep, unroll, pick=all_fields):
    def slopes_of(low, mid, high):
        return [minmod(b - a, c - b) for a, b, c in zip(low, mid, high)]

    cut = lambda states: [u[:keep] for u in states]
    cut_x = lambda states: cut(pick(states, 0))
    r0, r1, r2, r3 = [cut_x(load(first_row + k)) for k in (-2, -1, 0, 1)]
    upper_prev, _ = edge_terms(r1, slopes_of(r0, r1, r2), 0)
    upper_now, lower_now = edge_terms(r2, slopes_of(r1, r2, r3), 0)
    face = [u + w for u, w in zip(upper_prev, lower_now)]

    def step(k, carry):
        face_low, upper_here = carry
        i = first_row + k
        here, above, far = load(i), cut_x(load(i + 1)), cut_x(load(i + 2))
        mine = cut(here)
        upper_next, lower_next = edge_terms(above, slopes_of(pick(mine, 0), above, far), 0)
        face_high = [u + w for u, w in zip(upper_here, lower_next)]
        change = [h - l for h, l in zip(face_high, face_low)]
        along_y = cut(line_change(pick(here, 1), 1, 0))
        along_z = line_change(pick(mine, 2), 2, 1)
        rate = [-(a + b + c) for a, b, c in zip(change, along_y, along_z)]
        store(i, mine, rate)
        return tuple(face_high), tuple(upper_next)

    lax.fori_loop(0, count, step, (tuple(face), tuple(upper_now)), unroll=unroll)


def euler_kernel(
    own_ref, xlow_ref, xhigh_ref, ylow_ref, yhigh_ref, clow_ref, chigh_ref, table_ref,
    first_ref, modes_ref, ext_ref, flat_ref,
):
    low, high = slice(BY + HALO, BY + 2 * HALO), slice(BY, BY + HALO)
    inner = slice(HALO, HALO + BX)
    ext_ref[:, inner, 0:BY] = own_ref[...]
    ext_ref[:, 0:HALO, 0:BY] = xlow_ref[...]
    ext_ref[:, HALO + BX :, 0:BY] = xhigh_ref[...]
    ext_ref[:, inner, high] = yhigh_ref[...]
    ext_ref[:, inner, low] = ylow_ref[...]
    for start, ref in ((0, clow_ref), (HALO + BX, chigh_ref)):
        ext_ref[:, start : start + 2, BY:] = ref[...]
        ext_ref[:, start + 2 : start + 4, BY:] = ref[...]

    def load_ext(i):
        return [ext_ref[q, i] for q in range(5)]

    def store_first(i, states, rates):
        for q in range(5):
            first_ref[q, i - 2] = states[q] + time_step * rates[q]

    euler_stage(load_ext, store_first, 2, BX + 4, BY + 2 * HALO, 6)

    def load_mass(i):
        return [first_ref[q, i - 2] for q in range(4)]

    def store_density(i, states, rates):
        second = states[0] + time_step * rates[0]
        row = pl.multiple_of((i - HALO) * BY, BY)
        flat_ref[pl.ds(row, BY), :] = 0.5 * ext_ref[0, i, 0:BY] + 0.5 * second

    euler_stage(load_mass, store_density, HALO, BX, BY, 32, mass_fields)
    density = jnp.concatenate(
        [flat_ref[pl.ds(b, BX, stride=BY), :] for b in range(BY)], axis=0
    )
    spread = dot(table_ref[...], density, ((1,), (1,)))
    modes_ref[pl.ds(0, GZ, stride=2), :] = spread[:, :128]
    modes_ref[pl.ds(1, GZ, stride=2), :] = spread[:, 128:]


def second_kernel(own_ref, first_ref, stepped_ref):
    def load_first(i):
        return [first_ref[q, i - 2] for q in range(5)]

    def store_stepped(i, states, rates):
        for q in range(5):
            second = states[q] + time_step * rates[q]
            stepped_ref[q, i - HALO] = 0.5 * own_ref[q, i - HALO] + 0.5 * second

    euler_stage(load_first, store_stepped, HALO, BX, BY, 8)


def ends_kernel(modes_ref, table_ref, kappa_ref, expand_ref, pick_ref, raw_ref, ends_ref, plane_ref):
    for tile in range(2):
        lines = [modes_ref[pl.ds(k * 2 + tile, COLS, stride=8), :] for k in range(4)]
        for g, value in enumerate(swap_groups(lines, 32)):
            plane_ref[pl.ds(tile * 4 + g, COLS, stride=BY), :] = value
    power = jnp.exp(-dot(kappa_ref[...], expand_ref[:, :128], ((0,), (0,))))
    source = dot(table_ref[...], plane_ref[...])
    x = lax.broadcasted_iota(jnp.int32, (GY, 128), 1) % BX
    rising, falling = source, source
    step = 1
    while step < BX:
        rising = rising + jnp.where(x >= step, power * pltpu.roll(rising, step, 1), 0.0)
        falling = falling + jnp.where(x < BX - step, power * pltpu.roll(falling, 128 - step, 1), 0.0)
        power = power * power
        step *= 2
    ends = dot(pick_ref[...], jnp.concatenate([rising, falling], axis=1), ((1,), (1,)))
    for r in range(ROWS):
        ends_ref[r * 24 : r * 24 + 8, :] = ends[:, :128]
        ends_ref[r * 24 + 8 : r * 24 + 16, :] = ends[:, 128:]
        ends_ref[r * 24 + 16 : r * 24 + 24, :] = source[0:8]
    raw_ref[:, :128] = rising + falling - source
    raw_ref[:, 128:] = jnp.where(x == 0, falling, pltpu.roll(rising, 128 - BX + 2, 1))


def weigh_kernel(kappa_ref, expand_ref, span_ref, raw_ref, local_ref, left_ref, right_ref):
    kappa = dot(kappa_ref[...], expand_ref[:, :128], ((0,), (0,)))
    flat = kappa <= 0.0
    decay = jnp.exp(-kappa)
    width = jnp.where(flat, 1.0, jnp.exp(kappa) - decay)
    scale = jnp.where(flat, 0.0, -four_pi_g / width)
    images = scale / jnp.where(flat, 1.0, 1.0 - jnp.exp(-GX * kappa))
    for half in range(2):
        lanes = slice(half * 128, half * 128 + 128)
        span = span_ref[:, lanes]
        local_ref[:, lanes] = (scale * decay if half else scale) * raw_ref[:, lanes]
        left_ref[:, lanes] = images * jnp.exp(-kappa * (span + 1.0))
        right_ref[:, lanes] = images * jnp.exp(-kappa * (BX - span))


def join_kernel(
    place_ref, ends_ref, local_ref, left_ref, right_ref, kappa_ref, expand_ref, table_ref,
    out_ref, wide_ref,
):
    row = place_ref[0]

    def slab(step):
        return pl.multiple_of(((row + step) & (ROWS - 1)) * 24, 8)

    rising = lax.broadcasted_iota(jnp.int32, (8, GY), 0) % 2 == 0
    block = jnp.exp(-BX * kappa_ref[...])
    total = None
    for d in range(ROWS, 0, -1):
        below, above = slab(ROWS - d), slab(d)
        both = []
        for part in (0, 8):
            both.append((ends_ref[pl.ds(below + part, 8), :], ends_ref[pl.ds(above + part, 8), :]))
        low = jnp.concatenate([both[0][0], both[1][0]], axis=1)
        high = jnp.concatenate([both[0][1], both[1][1]], axis=1)
        value = jnp.where(rising, low, high)
        total = value if total is None else value + block * total
    end = lax.broadcasted_iota(jnp.int32, (8, 256), 0) % 2
    side = lax.broadcasted_iota(jnp.int32, (8, 256), 1) // 128
    spread = jnp.where(end == side, 2.0 * expand_ref[...], 0.0)
    incoming = dot(total, spread, ((0,), (0,)))
    halves = []
    for lanes in (slice(0, 128), slice(128, 256)):
        moved = left_ref[:, lanes] * incoming[:, :128] + right_ref[:, lanes] * incoming[:, 128:]
        halves.append(local_ref[:, lanes] + moved)
    field = jnp.concatenate(halves, axis=1)
    lane = lax.broadcasted_iota(jnp.int32, (8, 128), 1)
    halves = []
    for half in range(2):
        line = jnp.zeros((8, 128), jnp.float32)
        for g in range(4):
            values = ends_ref[pl.ds(slab(ROWS - half * 4 - g) + 16, 8), :]
            values = jnp.where(lane < BX, values, 0.0)
            line = line + (pltpu.roll(values, g * BX, 1) if g else values)
        halves.append(line)
    line = jnp.concatenate(halves, axis=1)
    line = line - jnp.sum(line, axis=1, keepdims=True) * (1.0 / GX)
    source = lax.broadcasted_iota(jnp.int32, (GX, 128), 0)
    target = lax.broadcasted_iota(jnp.int32, (GX, 128), 1)
    target = jnp.where(target == BX + 1, -1, target)
    gap = jnp.abs(source // BX * BX + target - source % BX).astype(jnp.float32)
    shape = four_pi_g * (gap * (0.5 - gap * (0.5 / GX)) - (GX * GX - 1.0) / (12.0 * GX))
    mean = dot(line, shape)
    first = lax.broadcasted_iota(jnp.int32, (8, 128), 0) == 0
    mean = jnp.where(jnp.logical_and(first, place_ref[1] == 0), mean, 0.0)
    inner = jnp.where(lane < BX, mean, 0.0)
    low, high = pltpu.roll(mean, 128 - BX - 1, 1), pltpu.roll(mean, 128 - BX + 1, 1)
    outer = jnp.where(lane == 0, low, jnp.where(lane == 1, high, 0.0))
    mean = jnp.concatenate([inner, outer], axis=1)
    field = jnp.concatenate([field[0:8] + mean, field[8:]], axis=0)
    potential = dot(table_ref[...], field, precision=lax.Precision.HIGH)
    for part in range(2):
        base, side = part * (GY + 16), potential[:, part * 128 : part * 128 + 128]
        wide_ref[base + 8 : base + 8 + GY, :] = side
        wide_ref[base : base + 8, :] = side[GY - 8 :]
        wide_ref[base + 8 + GY : base + 16 + GY, :] = side[:8]
    strips = [wide_ref[pl.ds(8 + yl, COLS, stride=BY), :] for yl in range(BY)]
    below = wide_ref[pl.ds(7, COLS, stride=BY), :]
    above = wide_ref[pl.ds(16, COLS, stride=BY), :]
    x = lax.broadcasted_iota(jnp.int32, (COLS, 128), 1) % BX
    sides = jnp.zeros((COLS, 128), jnp.float32)
    for yl in range(BY):
        edge = wide_ref[pl.ds(GY + 16 + 8 + yl, COLS, stride=BY), :]
        sides = jnp.where(x == yl, pltpu.roll(edge, yl, 1) if yl else edge, sides)
        sides = jnp.where(x == BY + yl, pltpu.roll(edge, BY - 1 + yl, 1), sides)
    strips = strips + [below, above, sides, sides]
    for quad in range(3):
        for k, value in enumerate(swap_groups(strips[quad * 4 : quad * 4 + 4], 32)):
            out_ref[pl.ds(k * 3 + quad, COLS, stride=12), :] = value


def kick_kernel(owner_ref, stepped_ref, modes_ref, table_ref, out_ref, phi_ref, kicked_ref):
    table = table_ref[...]
    parts = []
    for quad in range(3):
        block = modes_ref[pl.ds(quad, GZ, stride=3), :]
        parts.append(dot(block, table, ((0,), (0,))))
    for yl in range(BY):
        phi_ref[pl.ds(BY + yl, BX, stride=BY), :] = parts[yl // 4][(yl % 4) * 32 : (yl % 4) * 32 + 32]
    phi_ref[0:BY, :] = parts[2][64 : 64 + BY]
    phi_ref[BY + BX * BY :, :] = parts[2][64 + BY : 64 + 2 * BY]
    phi = phi_ref[...].reshape(BX + 2, BY, GZ)
    mid = phi[1 : 1 + BX]
    below = parts[2][0:32].reshape(BX, 1, GZ)
    above = parts[2][32:64].reshape(BX, 1, GZ)
    grad_x = 0.5 * (phi[2:] - phi[:BX])
    lower = jnp.concatenate([below, mid[:, : BY - 1]], axis=1)
    upper = jnp.concatenate([mid[:, 1:], above], axis=1)
    grad_y = 0.5 * (upper - lower)
    grad_z = 0.5 * (pltpu.roll(mid, GZ - 1, 2) - pltpu.roll(mid, 1, 2))
    grads = (grad_x, grad_y, grad_z)
    density = stepped_ref[0]
    momenta = [stepped_ref[1 + d] for d in range(3)]
    work = momenta[0] * grad_x + momenta[1] * grad_y + momenta[2] * grad_z
    cells = BX * BY
    kicked_ref[0:cells, :] = density.reshape(cells, GZ)
    for d in range(3):
        value = momenta[d] - time_step * density * grads[d]
        kicked_ref[(1 + d) * cells : (2 + d) * cells, :] = value.reshape(cells, GZ)
    kicked_ref[4 * cells :, :] = (stepped_ref[4] - time_step * work).reshape(cells, GZ)
    for q in range(5):
        for xl in range(2):
            for part in range(2):
                base = (q * BX + xl * PE + part * 8) * BY
                lines = [kicked_ref[pl.ds(base + b, 8, stride=BY), :] for b in range(BY)]
                rows = q * PE + part * 8
                for zl, value in enumerate(swap_groups(lines, PE)):
                    out_ref[owner_ref[xl * 8 + zl], rows : rows + 8, :] = value


def spread_kernel(place_ref, recv_ref, out_ref):
    shift = place_ref[0]
    live = lax.broadcasted_iota(jnp.int32, (CAP, 128), 0) < place_ref[1]
    for q in range(5):
        for tile in range(2 * PE):
            a, half = tile // 2, tile % 2
            lines = recv_ref[pl.ds(half * BRICK + q * PE + a, CAP, stride=2 * BRICK), :]
            turned = pltpu.roll(lines, shift, 0)
            out_ref[q, :, tile * 128 : (tile + 1) * 128] = jnp.where(live, turned, 0.0)


def call(kernel, outs, ins, scratch=()):
    shapes = [jax.ShapeDtypeStruct(s, jnp.float32) for s in outs]
    many = len(outs) > 1
    return pl.pallas_call(
        kernel,
        out_shape=tuple(shapes) if many else shapes[0],
        in_specs=[SM if i in ins[1] else VM for i in range(ins[0])],
        out_specs=tuple([VM] * len(outs)) if many else VM,
        scratch_shapes=[pltpu.VMEM(s, jnp.float32) for s in scratch],
        compiler_params=PARAMS,
    )


def gather_counts(counts):
    copies = jnp.broadcast_to(counts.astype(jnp.float32).reshape(1, 1, 1), (COLS, 1, 128))
    return lax.all_to_all(copies, "col", split_axis=0, concat_axis=0, tiled=True)


def on_device(fields, counts):
    my_row = lax.axis_index("row")
    my_column = lax.axis_index("col")
    staged = call(stage_kernel, [(COLS * BRICK, 128)], (1, ()))(fields.transpose(1, 0, 2))
    spread_counts = gather_counts(counts)
    row_counts = spread_counts[:, 0, 0].astype(jnp.int32)
    column_ids = jnp.arange(COLS, dtype=jnp.int32)
    starts = jnp.sum(
        jnp.where(column_ids[None, :] < column_ids[:, None], row_counts[None, :], 0), axis=1
    )
    own_start = jnp.sum(jnp.where(column_ids < my_column, row_counts, 0))
    y_patch = my_column // 2
    wanted = jnp.arange(LINES, dtype=jnp.int32) * 16 + y_patch
    owners = jnp.sum((starts[None, :] <= wanted[:, None]).astype(jnp.int32), axis=1) - 1
    turn = own_start % CAP

    sent = call(turn_kernel, [(COLS * BRICK, 128)], (3, (0,)))(
        my_column.reshape(1), spread_counts, staged
    )
    arrived = lax.all_to_all(
        sent.reshape(COLS, BRICK, 128), "col", split_axis=0, concat_axis=0, tiled=True
    )
    own, xfirst, xlast, yfirst, ylast = call(
        unpack_kernel,
        [
            (5 * BX * BY, GZ),
            (5, HALO, BY, GZ),
            (5, HALO, BY, GZ),
            (5, BX, HALO, GZ),
            (5, BX, HALO, GZ),
        ],
        (2, (0,)),
    )(owners, arrived)
    own = own.reshape(5, BX, BY, GZ)

    def ring(count, step):
        return [(i, (i + step) % count) for i in range(count)]

    xlow = lax.ppermute(xlast, "row", ring(ROWS, 1))
    xhigh = lax.ppermute(xfirst, "row", ring(ROWS, -1))
    ylow = lax.ppermute(ylast, "col", ring(COLS, 1))
    yhigh = lax.ppermute(yfirst, "col", ring(COLS, -1))
    up, down = call(corner_kernel, [(5, 2, BY, GZ)] * 2, (2, ()))(ylow, yhigh)
    clow = lax.ppermute(up, "row", ring(ROWS, 1))
    chigh = lax.ppermute(down, "row", ring(ROWS, -1))

    table_z = hartley(GZ)
    table_x = hartley(GX)
    wide = (5, BX + 2 * HALO, BY + 2 * HALO, GZ)
    first, modes = call(
        euler_kernel, [(5, BX + HALO, BY + 2 * HALO, GZ), (256, 128)], (8, ()), [wide, (BX * BY, GZ)]
    )(own, xlow, xhigh, ylow, yhigh, clow, chigh, jnp.asarray(table_z))
    planes = lax.all_to_all(
        modes.reshape(COLS, 8, 128), "col", split_axis=0, concat_axis=0, tiled=True
    )
    kappa = jnp.asarray(np.repeat(kappas(), 2, axis=0).astype(np.float32))
    kappa = lax.dynamic_slice_in_dim(kappa, my_column * 8, 8, axis=0)
    expand = jnp.asarray(lane_expand())
    square = (GY, 256)
    stepped = call(second_kernel, [(5, BX, BY, GZ)], (2, ()))(own, first)
    planes, stepped, kappa = lax.optimization_barrier((planes, stepped, kappa))
    raw, ends = call(ends_kernel, [square, (ROWS * 24, 128)], (5, ()), [(GY, 128)])(
        planes.reshape(256, 128), jnp.asarray(table_x), kappa, expand, jnp.asarray(lane_picks())
    )
    local, left, right = call(weigh_kernel, [square] * 3, (4, ()))(
        kappa, expand, jnp.asarray(lane_spans()[None, :]), raw
    )
    ends = lax.all_to_all(
        ends.reshape(ROWS, 24, 128), "row", split_axis=0, concat_axis=0, tiled=True
    )
    strips = call(join_kernel, [(COLS * 12, 128)], (8, (0,)), [(2 * (GY + 16), 128)])(
        jnp.stack([my_row, my_column]),
        ends.reshape(ROWS * 24, 128),
        local,
        left,
        right,
        kappa,
        expand,
        jnp.asarray(table_x),
    )
    strips = lax.all_to_all(
        strips.reshape(COLS, 1, 1536), "col", split_axis=0, concat_axis=0, tiled=True
    )
    returned = call(
        kick_kernel,
        [(COLS, BRICK, 128)],
        (4, (0,)),
        [((BX + 2) * BY, GZ), (5 * BX * BY, GZ)],
    )(owners, stepped, strips.reshape(COLS * 12, 128), jnp.asarray(table_z))
    came_back = lax.all_to_all(returned, "col", split_axis=0, concat_axis=0, tiled=True)
    home = jnp.stack([(CAP - turn) % CAP, counts[0, 0]])
    result = call(spread_kernel, [(5, CAP, PE * PE * PE)], (2, (0,)))(
        home, came_back.reshape(COLS * BRICK, 128)
    )
    return result.transpose(1, 0, 2)


def solution(mesh):
    return jax.shard_map(
        on_device,
        mesh=mesh,
        in_specs=(P(("row", "col"), None, None), P("row", "col")),
        out_specs=P(("row", "col"), None, None),
        check_vma=False,
    )
```

```python
import math

import jax
import jax.numpy as jnp
import numpy as np
from jax import lax
from jax.experimental import pallas as pl
from jax.experimental.pallas import tpu as pltpu
from jax.sharding import PartitionSpec as P

PE = 16
GX = 256
GY = 256
GZ = 128
ROWS = 8
COLS = 32
BX = GX // ROWS
BY = GY // COLS
CAP = 16
LINES = 16
BRICK = 5 * PE
EARLY = 8 + PE
LATE = 4 * PE
HALO = 4

time_step = 0.03
four_pi_g = 10.0

PARAMS = pltpu.CompilerParams(vmem_limit_bytes=16 * 2**20)
VM = pl.BlockSpec(memory_space=pltpu.VMEM)
SM = pl.BlockSpec(memory_space=pltpu.SMEM)


def hartley(length):
    index = np.arange(length)
    angle = 2.0 * np.pi / length * (index[:, None] * index[None, :] % length)
    return ((np.cos(angle) + np.sin(angle)) / math.sqrt(length)).astype(np.float32)


def kappas():
    wave_y = np.sin(np.pi * np.arange(GY) / GY) ** 2
    wave_z = np.sin(np.pi * np.arange(GZ) / GZ) ** 2
    return 2.0 * np.arcsinh(np.sqrt(wave_z[:, None] + wave_y[None, :]))


def lane_spans():
    inner = np.arange(128) % BX
    return np.concatenate([inner, np.where(inner == 0, -1, BX)]).astype(np.float32)


def lane_expand():
    lanes = np.arange(256) % 128 // BX
    return 0.5 * (np.arange(8)[:, None] // 2 == lanes[None, :]).astype(np.float32)


def lane_picks():
    picks = np.zeros((8, 256), np.float32)
    for k in range(4):
        picks[2 * k, k * BX + BX - 1] = 1.0
        picks[2 * k + 1, 128 + k * BX] = 1.0
    return picks


def dot(left, right, dims=((1,), (0,)), precision=lax.Precision.HIGHEST):
    return lax.dot_general(
        left,
        right,
        (dims, ((), ())),
        precision=precision,
        preferred_element_type=jnp.float32,
    )


def swap_groups(arrays, group):
    count = len(arrays)
    lane = lax.broadcasted_iota(jnp.int32, arrays[0].shape, 1) // group
    arrays = list(arrays)
    distance = count // 2
    while distance:
        upper = (lane & distance) != 0
        for i in range(count):
            if i & distance:
                continue
            low, high = arrays[i], arrays[i + distance]
            arrays[i] = jnp.where(upper, pltpu.roll(high, distance * group, 1), low)
            arrays[i + distance] = jnp.where(
                upper, high, pltpu.roll(low, 128 - distance * group, 1)
            )
        distance //= 2
    return arrays


def stage_kernel(fields_ref, out_ref):
    for q in range(5):
        for tile in range(2 * PE):
            a, half = tile // 2, tile % 2
            slots = fields_ref[q, :, tile * 128 : (tile + 1) * 128]
            out_ref[pl.ds(half * BRICK + q * PE + a, CAP, stride=2 * BRICK), :] = slots


def turn_kernel(column_ref, counts_ref, staged_ref, out_ref):
    counts = counts_ref[...].reshape(COLS, 128)
    before = lax.broadcasted_iota(jnp.int32, (COLS, 128), 0) < column_ref[0]
    start = (jnp.sum(jnp.where(before, counts, 0.0)) * (1.0 / 128.0)).astype(jnp.int32)
    size = 2 * BRICK
    for y in range(CAP):
        source = pl.multiple_of(((y - start) & (CAP - 1)) * size, 8)
        out_ref[y * size : (y + 1) * size, :] = staged_ref[pl.ds(source, size), :]


def unpack_kernel(owner_ref, recv_ref, own_ref, xfirst_ref, xlast_ref, yfirst_ref, ylast_ref):
    for q in range(5):
        for xl in range(2):
            for part in range(2):
                rows = q * PE + part * 8
                lines = [
                    recv_ref[owner_ref[xl * 8 + zl], rows : rows + 8, :] for zl in range(8)
                ]
                for b, value in enumerate(swap_groups(lines, PE)):
                    base = (q * BX + xl * PE + part * 8) * BY + b
                    own_ref[pl.ds(base, 8, stride=BY), :] = value
    block = own_ref[...].reshape(5, BX, BY, GZ)
    xfirst_ref[...] = block[:, :HALO]
    xlast_ref[...] = block[:, BX - HALO :]
    yfirst_ref[...] = block[:, :, :HALO]
    ylast_ref[...] = block[:, :, BY - HALO :]


def corner_kernel(ylow_ref, yhigh_ref, up_ref, down_ref):
    for ref, first in ((up_ref, BX - 2), (down_ref, 0)):
        ref[:, :, :HALO] = yhigh_ref[:, first : first + 2]
        ref[:, :, HALO:] = ylow_ref[:, first : first + 2]


def minmod(p, q):
    return jnp.maximum(jnp.minimum(p, q), 0.0) + jnp.minimum(jnp.maximum(p, q), 0.0)


def half_flux(states, direction, sign):
    if len(states) == 2:
        return [0.5 * states[1] + sign * 2.0 * states[0]]
    density, energy = states[0], states[4]
    inverse = 1.0 / density
    velocity = 0.5 * states[1 + direction] * inverse
    squares = states[1] * states[1] + states[2] * states[2] + states[3] * states[3]
    pressure = 0.4 * energy - (0.2 * squares) * inverse
    pieces = [0.5 * states[1 + direction]]
    for component in range(3):
        term = states[1 + component] * velocity
        if component == direction:
            term = term + 0.5 * pressure
        pieces.append(term)
    pieces.append((energy + pressure) * velocity)
    if sign > 0:
        return [piece + 2.0 * state for piece, state in zip(pieces, states)]
    return [piece - 2.0 * state for piece, state in zip(pieces, states)]


def edge_terms(states, slopes, direction):
    halves = [0.5 * slope for slope in slopes]
    upper = half_flux([u + h for u, h in zip(states, halves)], direction, 1)
    lower = half_flux([u - h for u, h in zip(states, halves)], direction, -1)
    return upper, lower


def line_change(states, direction, axis):
    size = states[0].shape[axis]
    gaps = [pltpu.roll(u, size - 1, axis) - u for u in states]
    slopes = [minmod(pltpu.roll(g, 1, axis), g) for g in gaps]
    upper, lower = edge_terms(states, slopes, direction)
    faces = [u + pltpu.roll(w, size - 1, axis) for u, w in zip(upper, lower)]
    return [f - pltpu.roll(f, 1, axis) for f in faces]


def all_fields(states, direction):
    return states


def mass_fields(states, direction):
    return [states[0], states[1 + direction]]


def euler_stage(load, store, first_row, count, keep, unroll, pick=all_fields):
    def slopes_of(low, mid, high):
        return [minmod(b - a, c - b) for a, b, c in zip(low, mid, high)]

    cut = lambda states: [u[:keep] for u in states]
    cut_x = lambda states: cut(pick(states, 0))
    r0, r1, r2, r3 = [cut_x(load(first_row + k)) for k in (-2, -1, 0, 1)]
    upper_prev, _ = edge_terms(r1, slopes_of(r0, r1, r2), 0)
    upper_now, lower_now = edge_terms(r2, slopes_of(r1, r2, r3), 0)
    face = [u + w for u, w in zip(upper_prev, lower_now)]

    def step(k, carry):
        face_low, upper_here = carry
        i = first_row + k
        here, above, far = load(i), cut_x(load(i + 1)), cut_x(load(i + 2))
        mine = cut(here)
        upper_next, lower_next = edge_terms(above, slopes_of(pick(mine, 0), above, far), 0)
        face_high = [u + w for u, w in zip(upper_here, lower_next)]
        change = [h - l for h, l in zip(face_high, face_low)]
        along_y = cut(line_change(pick(here, 1), 1, 0))
        along_z = line_change(pick(mine, 2), 2, 1)
        rate = [-(a + b + c) for a, b, c in zip(change, along_y, along_z)]
        store(i, mine, rate)
        return tuple(face_high), tuple(upper_next)

    lax.fori_loop(0, count, step, (tuple(face), tuple(upper_now)), unroll=unroll)


def euler_kernel(
    owner_ref, own_ref, xlow_ref, xhigh_ref, ylow_ref, yhigh_ref, clow_ref, chigh_ref, table_ref,
    own_first_ref, side_first_ref, modes_ref, ext_ref, first_ref, flat_ref,
):
    low, high = slice(BY + HALO, BY + 2 * HALO), slice(BY, BY + HALO)
    inner = slice(HALO, HALO + BX)
    ext_ref[:, inner, 0:BY] = own_ref[...]
    ext_ref[:, 0:HALO, 0:BY] = xlow_ref[...]
    ext_ref[:, HALO + BX :, 0:BY] = xhigh_ref[...]
    ext_ref[:, inner, high] = yhigh_ref[...]
    ext_ref[:, inner, low] = ylow_ref[...]
    for start, ref in ((0, clow_ref), (HALO + BX, chigh_ref)):
        ext_ref[:, start : start + 2, BY:] = ref[...]
        ext_ref[:, start + 2 : start + 4, BY:] = ref[...]

    def load_ext(i):
        return [ext_ref[q, i] for q in range(5)]

    def store_first(i, states, rates):
        for q in range(5):
            first_ref[q, i - 2] = states[q] + time_step * rates[q]

    euler_stage(load_ext, store_first, 2, BX + 4, BY + 2 * HALO, 6)

    def load_mass(i):
        return [first_ref[q, i - 2] for q in range(4)]

    def store_density(i, states, rates):
        second = states[0] + time_step * rates[0]
        row = pl.multiple_of((i - HALO) * BY, BY)
        flat_ref[pl.ds(row, BY), :] = 0.5 * ext_ref[0, i, 0:BY] + 0.5 * second

    euler_stage(load_mass, store_density, HALO, BX, BY, 32, mass_fields)
    own_first_ref[...] = first_ref[:, :, 0:BY]
    side_first_ref[:, :, 0:2] = first_ref[:, 2 : 2 + BX, BY : BY + 2]
    side_first_ref[:, :, 2:4] = first_ref[:, 2 : 2 + BX, BY + 6 : BY + 8]
    density = jnp.concatenate(
        [flat_ref[pl.ds(b, BX, stride=BY), :] for b in range(BY)], axis=0
    )
    spread = dot(table_ref[...], density, ((1,), (1,)))
    for k in range(4):
        for tile in range(2):
            piece = spread[k * COLS : (k + 1) * COLS, tile * 128 : tile * 128 + 128]
            modes_ref[pl.ds(k * 2 + tile, COLS, stride=EARLY), :] = piece
    for xl in range(2):
        for part in range(2):
            base = (xl * PE + part * 8) * BY
            lines = [flat_ref[pl.ds(base + b, 8, stride=BY), :] for b in range(BY)]
            for zl, value in enumerate(swap_groups(lines, PE)):
                row = owner_ref[xl * 8 + zl] * EARLY + 8 + part * 8
                modes_ref[pl.ds(pl.multiple_of(row, 8), 8), :] = value


def second_kernel(own_ref, own_first_ref, side_first_ref, stepped_ref, first_ref):
    first_ref[:, :, 0:BY] = own_first_ref[...]
    first_ref[:, :, BY:] = own_first_ref[...]
    first_ref[:, 2 : 2 + BX, BY : BY + 2] = side_first_ref[:, :, 0:2]
    first_ref[:, 2 : 2 + BX, BY + 6 : BY + 8] = side_first_ref[:, :, 2:4]

    def load_first(i):
        return [first_ref[q, i - 2] for q in range(5)]

    def store_stepped(i, states, rates):
        for q in range(5):
            second = states[q] + time_step * rates[q]
            stepped_ref[q, i - HALO] = 0.5 * own_ref[q, i - HALO] + 0.5 * second

    euler_stage(load_first, store_stepped, HALO, BX, BY, 8)


def ends_kernel(modes_ref, table_ref, kappa_ref, expand_ref, pick_ref, raw_ref, ends_ref, plane_ref):
    for tile in range(2):
        lines = [modes_ref[pl.ds(k * 2 + tile, COLS, stride=EARLY), :] for k in range(4)]
        for g, value in enumerate(swap_groups(lines, 32)):
            plane_ref[pl.ds(tile * 4 + g, COLS, stride=BY), :] = value
    power = jnp.exp(-dot(kappa_ref[...], expand_ref[:, :128], ((0,), (0,))))
    source = dot(table_ref[...], plane_ref[...])
    x = lax.broadcasted_iota(jnp.int32, (GY, 128), 1) % BX
    rising, falling = source, source
    step = 1
    while step < BX:
        rising = rising + jnp.where(x >= step, power * pltpu.roll(rising, step, 1), 0.0)
        falling = falling + jnp.where(x < BX - step, power * pltpu.roll(falling, 128 - step, 1), 0.0)
        power = power * power
        step *= 2
    ends = dot(pick_ref[...], jnp.concatenate([rising, falling], axis=1), ((1,), (1,)))
    for r in range(ROWS):
        ends_ref[r * 24 : r * 24 + 8, :] = ends[:, :128]
        ends_ref[r * 24 + 8 : r * 24 + 16, :] = ends[:, 128:]
        ends_ref[r * 24 + 16 : r * 24 + 24, :] = source[0:8]
    raw_ref[:, :128] = rising + falling - source
    raw_ref[:, 128:] = jnp.where(x == 0, falling, pltpu.roll(rising, 128 - BX + 2, 1))


def weigh_kernel(kappa_ref, expand_ref, span_ref, raw_ref, local_ref, left_ref, right_ref):
    kappa = dot(kappa_ref[...], expand_ref[:, :128], ((0,), (0,)))
    flat = kappa <= 0.0
    decay = jnp.exp(-kappa)
    width = jnp.where(flat, 1.0, jnp.exp(kappa) - decay)
    scale = jnp.where(flat, 0.0, -four_pi_g / width)
    images = scale / jnp.where(flat, 1.0, 1.0 - jnp.exp(-GX * kappa))
    for half in range(2):
        lanes = slice(half * 128, half * 128 + 128)
        span = span_ref[:, lanes]
        local_ref[:, lanes] = (scale * decay if half else scale) * raw_ref[:, lanes]
        left_ref[:, lanes] = images * jnp.exp(-kappa * (span + 1.0))
        right_ref[:, lanes] = images * jnp.exp(-kappa * (BX - span))


def join_kernel(
    place_ref, ends_ref, local_ref, left_ref, right_ref, kappa_ref, expand_ref, table_ref,
    out_ref, wide_ref,
):
    row = place_ref[0]

    def slab(step):
        return pl.multiple_of(((row + step) & (ROWS - 1)) * 24, 8)

    rising = lax.broadcasted_iota(jnp.int32, (8, GY), 0) % 2 == 0
    block = jnp.exp(-BX * kappa_ref[...])
    total = None
    for d in range(ROWS, 0, -1):
        below, above = slab(ROWS - d), slab(d)
        both = []
        for part in (0, 8):
            both.append((ends_ref[pl.ds(below + part, 8), :], ends_ref[pl.ds(above + part, 8), :]))
        low = jnp.concatenate([both[0][0], both[1][0]], axis=1)
        high = jnp.concatenate([both[0][1], both[1][1]], axis=1)
        value = jnp.where(rising, low, high)
        total = value if total is None else value + block * total
    end = lax.broadcasted_iota(jnp.int32, (8, 256), 0) % 2
    side = lax.broadcasted_iota(jnp.int32, (8, 256), 1) // 128
    spread = jnp.where(end == side, 2.0 * expand_ref[...], 0.0)
    incoming = dot(total, spread, ((0,), (0,)))
    halves = []
    for lanes in (slice(0, 128), slice(128, 256)):
        moved = left_ref[:, lanes] * incoming[:, :128] + right_ref[:, lanes] * incoming[:, 128:]
        halves.append(local_ref[:, lanes] + moved)
    field = jnp.concatenate(halves, axis=1)
    lane = lax.broadcasted_iota(jnp.int32, (8, 128), 1)
    halves = []
    for half in range(2):
        line = jnp.zeros((8, 128), jnp.float32)
        for g in range(4):
            values = ends_ref[pl.ds(slab(ROWS - half * 4 - g) + 16, 8), :]
            values = jnp.where(lane < BX, values, 0.0)
            line = line + (pltpu.roll(values, g * BX, 1) if g else values)
        halves.append(line)
    line = jnp.concatenate(halves, axis=1)
    line = line - jnp.sum(line, axis=1, keepdims=True) * (1.0 / GX)
    source = lax.broadcasted_iota(jnp.int32, (GX, 128), 0)
    target = lax.broadcasted_iota(jnp.int32, (GX, 128), 1)
    target = jnp.where(target == BX + 1, -1, target)
    gap = jnp.abs(source // BX * BX + target - source % BX).astype(jnp.float32)
    shape = four_pi_g * (gap * (0.5 - gap * (0.5 / GX)) - (GX * GX - 1.0) / (12.0 * GX))
    mean = dot(line, shape)
    first = lax.broadcasted_iota(jnp.int32, (8, 128), 0) == 0
    mean = jnp.where(jnp.logical_and(first, place_ref[1] == 0), mean, 0.0)
    inner = jnp.where(lane < BX, mean, 0.0)
    low, high = pltpu.roll(mean, 128 - BX - 1, 1), pltpu.roll(mean, 128 - BX + 1, 1)
    outer = jnp.where(lane == 0, low, jnp.where(lane == 1, high, 0.0))
    mean = jnp.concatenate([inner, outer], axis=1)
    field = jnp.concatenate([field[0:8] + mean, field[8:]], axis=0)
    potential = dot(table_ref[...], field, precision=lax.Precision.HIGH)
    for part in range(2):
        base, side = part * (GY + 16), potential[:, part * 128 : part * 128 + 128]
        wide_ref[base + 8 : base + 8 + GY, :] = side
        wide_ref[base : base + 8, :] = side[GY - 8 :]
        wide_ref[base + 8 + GY : base + 16 + GY, :] = side[:8]
    strips = [wide_ref[pl.ds(8 + yl, COLS, stride=BY), :] for yl in range(BY)]
    below = wide_ref[pl.ds(7, COLS, stride=BY), :]
    above = wide_ref[pl.ds(16, COLS, stride=BY), :]
    x = lax.broadcasted_iota(jnp.int32, (COLS, 128), 1) % BX
    sides = jnp.zeros((COLS, 128), jnp.float32)
    for yl in range(BY):
        edge = wide_ref[pl.ds(GY + 16 + 8 + yl, COLS, stride=BY), :]
        sides = jnp.where(x == yl, pltpu.roll(edge, yl, 1) if yl else edge, sides)
        sides = jnp.where(x == BY + yl, pltpu.roll(edge, BY - 1 + yl, 1), sides)
    strips = strips + [below, above, sides, sides]
    for quad in range(3):
        for k, value in enumerate(swap_groups(strips[quad * 4 : quad * 4 + 4], 32)):
            out_ref[pl.ds(k * 3 + quad, COLS, stride=12), :] = value


def kick_kernel(owner_ref, stepped_ref, modes_ref, table_ref, out_ref, phi_ref, kicked_ref):
    table = table_ref[...]
    parts = []
    for quad in range(3):
        block = modes_ref[pl.ds(quad, GZ, stride=3), :]
        parts.append(dot(block, table, ((0,), (0,))))
    for yl in range(BY):
        phi_ref[pl.ds(BY + yl, BX, stride=BY), :] = parts[yl // 4][(yl % 4) * 32 : (yl % 4) * 32 + 32]
    phi_ref[0:BY, :] = parts[2][64 : 64 + BY]
    phi_ref[BY + BX * BY :, :] = parts[2][64 + BY : 64 + 2 * BY]
    phi = phi_ref[...].reshape(BX + 2, BY, GZ)
    mid = phi[1 : 1 + BX]
    below = parts[2][0:32].reshape(BX, 1, GZ)
    above = parts[2][32:64].reshape(BX, 1, GZ)
    grad_x = 0.5 * (phi[2:] - phi[:BX])
    lower = jnp.concatenate([below, mid[:, : BY - 1]], axis=1)
    upper = jnp.concatenate([mid[:, 1:], above], axis=1)
    grad_y = 0.5 * (upper - lower)
    grad_z = 0.5 * (pltpu.roll(mid, GZ - 1, 2) - pltpu.roll(mid, 1, 2))
    grads = (grad_x, grad_y, grad_z)
    density = stepped_ref[0]
    momenta = [stepped_ref[1 + d] for d in range(3)]
    work = momenta[0] * grad_x + momenta[1] * grad_y + momenta[2] * grad_z
    cells = BX * BY
    for d in range(3):
        value = momenta[d] - time_step * density * grads[d]
        kicked_ref[d * cells : (1 + d) * cells, :] = value.reshape(cells, GZ)
    kicked_ref[3 * cells :, :] = (stepped_ref[4] - time_step * work).reshape(cells, GZ)
    for q in range(4):
        for xl in range(2):
            for part in range(2):
                base = (q * BX + xl * PE + part * 8) * BY
                lines = [kicked_ref[pl.ds(base + b, 8, stride=BY), :] for b in range(BY)]
                rows = q * PE + part * 8
                for zl, value in enumerate(swap_groups(lines, PE)):
                    out_ref[owner_ref[xl * 8 + zl], rows : rows + 8, :] = value


def spread_kernel(place_ref, early_ref, late_ref, out_ref):
    shift = place_ref[0]
    live = lax.broadcasted_iota(jnp.int32, (CAP, 128), 0) < place_ref[1]
    for q in range(5):
        for tile in range(2 * PE):
            a, half = tile // 2, tile % 2
            if q:
                lines = late_ref[pl.ds(half * LATE + (q - 1) * PE + a, CAP, stride=2 * LATE), :]
            else:
                lines = early_ref[pl.ds(half * EARLY + 8 + a, CAP, stride=2 * EARLY), :]
            turned = pltpu.roll(lines, shift, 0)
            out_ref[q, :, tile * 128 : (tile + 1) * 128] = jnp.where(live, turned, 0.0)


def call(kernel, outs, ins, scratch=()):
    shapes = [jax.ShapeDtypeStruct(s, jnp.float32) for s in outs]
    many = len(outs) > 1
    return pl.pallas_call(
        kernel,
        out_shape=tuple(shapes) if many else shapes[0],
        in_specs=[SM if i in ins[1] else VM for i in range(ins[0])],
        out_specs=tuple([VM] * len(outs)) if many else VM,
        scratch_shapes=[pltpu.VMEM(s, jnp.float32) for s in scratch],
        compiler_params=PARAMS,
    )


def gather_counts(counts):
    copies = jnp.broadcast_to(counts.astype(jnp.float32).reshape(1, 1, 1), (COLS, 1, 128))
    return lax.all_to_all(copies, "col", split_axis=0, concat_axis=0, tiled=True)


def on_device(fields, counts):
    my_row = lax.axis_index("row")
    my_column = lax.axis_index("col")
    staged = call(stage_kernel, [(COLS * BRICK, 128)], (1, ()))(fields.transpose(1, 0, 2))
    spread_counts = gather_counts(counts)
    row_counts = spread_counts[:, 0, 0].astype(jnp.int32)
    column_ids = jnp.arange(COLS, dtype=jnp.int32)
    starts = jnp.sum(
        jnp.where(column_ids[None, :] < column_ids[:, None], row_counts[None, :], 0), axis=1
    )
    own_start = jnp.sum(jnp.where(column_ids < my_column, row_counts, 0))
    y_patch = my_column // 2
    wanted = jnp.arange(LINES, dtype=jnp.int32) * 16 + y_patch
    owners = jnp.sum((starts[None, :] <= wanted[:, None]).astype(jnp.int32), axis=1) - 1
    turn = own_start % CAP

    sent = call(turn_kernel, [(COLS * BRICK, 128)], (3, (0,)))(
        my_column.reshape(1), spread_counts, staged
    )
    arrived = lax.all_to_all(
        sent.reshape(COLS, BRICK, 128), "col", split_axis=0, concat_axis=0, tiled=True
    )
    own, xfirst, xlast, yfirst, ylast = call(
        unpack_kernel,
        [
            (5 * BX * BY, GZ),
            (5, HALO, BY, GZ),
            (5, HALO, BY, GZ),
            (5, BX, HALO, GZ),
            (5, BX, HALO, GZ),
        ],
        (2, (0,)),
    )(owners, arrived)
    own = own.reshape(5, BX, BY, GZ)

    def ring(count, step):
        return [(i, (i + step) % count) for i in range(count)]

    xlow = lax.ppermute(xlast, "row", ring(ROWS, 1))
    xhigh = lax.ppermute(xfirst, "row", ring(ROWS, -1))
    ylow = lax.ppermute(ylast, "col", ring(COLS, 1))
    yhigh = lax.ppermute(yfirst, "col", ring(COLS, -1))
    up, down = call(corner_kernel, [(5, 2, BY, GZ)] * 2, (2, ()))(ylow, yhigh)
    clow = lax.ppermute(up, "row", ring(ROWS, 1))
    chigh = lax.ppermute(down, "row", ring(ROWS, -1))

    table_z = hartley(GZ)
    order_z = np.arange(GZ).reshape(COLS, 4).T.reshape(GZ)
    table_x = hartley(GX)
    wide = (5, BX + 2 * HALO, BY + 2 * HALO, GZ)
    ring_shape = (5, BX + HALO, BY + 2 * HALO, GZ)
    own_first, side_first, modes = call(
        euler_kernel,
        [(5, BX + HALO, BY, GZ), (5, BX, HALO, GZ), (COLS * EARLY, 128)],
        (9, (0,)),
        [wide, ring_shape, (BX * BY, GZ)],
    )(owners, own, xlow, xhigh, ylow, yhigh, clow, chigh, jnp.asarray(table_z[order_z]))
    planes = lax.all_to_all(
        modes.reshape(COLS, EARLY, 128), "col", split_axis=0, concat_axis=0, tiled=True
    )
    kappa = jnp.asarray(np.repeat(kappas(), 2, axis=0).astype(np.float32))
    kappa = lax.dynamic_slice_in_dim(kappa, my_column * 8, 8, axis=0)
    expand = jnp.asarray(lane_expand())
    square = (GY, 256)
    stepped = call(second_kernel, [(5, BX, BY, GZ)], (3, ()), [ring_shape])(
        own, own_first, side_first
    )
    planes, stepped, kappa = lax.optimization_barrier((planes, stepped, kappa))
    raw, ends = call(ends_kernel, [square, (ROWS * 24, 128)], (5, ()), [(GY, 128)])(
        planes.reshape(COLS * EARLY, 128), jnp.asarray(table_x), kappa, expand, jnp.asarray(lane_picks())
    )
    local, left, right = call(weigh_kernel, [square] * 3, (4, ()))(
        kappa, expand, jnp.asarray(lane_spans()[None, :]), raw
    )
    ends = lax.all_to_all(
        ends.reshape(ROWS, 24, 128), "row", split_axis=0, concat_axis=0, tiled=True
    )
    strips = call(join_kernel, [(COLS * 12, 128)], (8, (0,)), [(2 * (GY + 16), 128)])(
        jnp.stack([my_row, my_column]),
        ends.reshape(ROWS * 24, 128),
        local,
        left,
        right,
        kappa,
        expand,
        jnp.asarray(table_x),
    )
    strips = lax.all_to_all(
        strips.reshape(COLS, 1, 1536), "col", split_axis=0, concat_axis=0, tiled=True
    )
    returned = call(
        kick_kernel,
        [(COLS, LATE, 128)],
        (4, (0,)),
        [((BX + 2) * BY, GZ), (4 * BX * BY, GZ)],
    )(owners, stepped, strips.reshape(COLS * 12, 128), jnp.asarray(table_z))
    came_back = lax.all_to_all(returned, "col", split_axis=0, concat_axis=0, tiled=True)
    home = jnp.stack([(CAP - turn) % CAP, counts[0, 0]])
    result = call(spread_kernel, [(5, CAP, PE * PE * PE)], (3, (0,)))(
        home, planes.reshape(COLS * EARLY, 128), came_back.reshape(COLS * LATE, 128)
    )
    return result.transpose(1, 0, 2)


def solution(mesh):
    return jax.shard_map(
        on_device,
        mesh=mesh,
        in_specs=(P(("row", "col"), None, None), P("row", "col")),
        out_specs=P(("row", "col"), None, None),
        check_vma=False,
    )
```

```python
import math

import jax
import jax.numpy as jnp
import numpy as np
from jax import lax
from jax.experimental import pallas as pl
from jax.experimental.pallas import tpu as pltpu
from jax.sharding import PartitionSpec as P

PE = 16
GX = 256
GY = 256
GZ = 128
ROWS = 8
COLS = 32
BX = GX // ROWS
BY = GY // COLS
CAP = 16
LINES = 16
BRICK = 5 * PE
HALO = 4

time_step = 0.03
four_pi_g = 10.0

PARAMS = pltpu.CompilerParams(vmem_limit_bytes=16 * 2**20)
VM = pl.BlockSpec(memory_space=pltpu.VMEM)
SM = pl.BlockSpec(memory_space=pltpu.SMEM)


def hartley(length):
    index = np.arange(length)
    angle = 2.0 * np.pi / length * (index[:, None] * index[None, :] % length)
    return ((np.cos(angle) + np.sin(angle)) / math.sqrt(length)).astype(np.float32)


def kappas():
    wave_y = np.sin(np.pi * np.arange(GY) / GY) ** 2
    wave_z = np.sin(np.pi * np.arange(GZ) / GZ) ** 2
    return 2.0 * np.arcsinh(np.sqrt(wave_z[:, None] + wave_y[None, :]))


def lane_spans():
    inner = np.arange(128) % BX
    return np.concatenate([inner, np.where(inner == 0, -1, BX)]).astype(np.float32)


def lane_expand():
    lanes = np.arange(256) % 128 // BX
    return 0.5 * (np.arange(8)[:, None] // 2 == lanes[None, :]).astype(np.float32)


def lane_picks():
    picks = np.zeros((8, 256), np.float32)
    for k in range(4):
        picks[2 * k, k * BX + BX - 1] = 1.0
        picks[2 * k + 1, 128 + k * BX] = 1.0
    return picks


def dot(left, right, dims=((1,), (0,)), precision=lax.Precision.HIGHEST):
    return lax.dot_general(
        left,
        right,
        (dims, ((), ())),
        precision=precision,
        preferred_element_type=jnp.float32,
    )


def swap_groups(arrays, group):
    count = len(arrays)
    lane = lax.broadcasted_iota(jnp.int32, arrays[0].shape, 1) // group
    arrays = list(arrays)
    distance = count // 2
    while distance:
        upper = (lane & distance) != 0
        for i in range(count):
            if i & distance:
                continue
            low, high = arrays[i], arrays[i + distance]
            arrays[i] = jnp.where(upper, pltpu.roll(high, distance * group, 1), low)
            arrays[i + distance] = jnp.where(
                upper, high, pltpu.roll(low, 128 - distance * group, 1)
            )
        distance //= 2
    return arrays


def stage_kernel(fields_ref, out_ref):
    for q in range(5):
        for tile in range(2 * PE):
            a, half = tile // 2, tile % 2
            slots = fields_ref[q, :, tile * 128 : (tile + 1) * 128]
            out_ref[pl.ds(half * BRICK + q * PE + a, CAP, stride=2 * BRICK), :] = slots


def turn_kernel(column_ref, counts_ref, staged_ref, out_ref):
    counts = counts_ref[...].reshape(COLS, 128)
    before = lax.broadcasted_iota(jnp.int32, (COLS, 128), 0) < column_ref[0]
    start = (jnp.sum(jnp.where(before, counts, 0.0)) * (1.0 / 128.0)).astype(jnp.int32)
    size = 2 * BRICK
    for y in range(CAP):
        source = pl.multiple_of(((y - start) & (CAP - 1)) * size, 8)
        out_ref[y * size : (y + 1) * size, :] = staged_ref[pl.ds(source, size), :]


def unpack_kernel(owner_ref, recv_ref, own_ref, xfirst_ref, xlast_ref, yfirst_ref, ylast_ref):
    for q in range(5):
        for xl in range(2):
            for part in range(2):
                rows = q * PE + part * 8
                lines = [
                    recv_ref[owner_ref[xl * 8 + zl], rows : rows + 8, :] for zl in range(8)
                ]
                for b, value in enumerate(swap_groups(lines, PE)):
                    base = (q * BX + xl * PE + part * 8) * BY + b
                    own_ref[pl.ds(base, 8, stride=BY), :] = value
    block = own_ref[...].reshape(5, BX, BY, GZ)
    xfirst_ref[...] = block[:, :HALO]
    xlast_ref[...] = block[:, BX - HALO :]
    yfirst_ref[...] = block[:, :, :HALO]
    ylast_ref[...] = block[:, :, BY - HALO :]


def corner_kernel(ylow_ref, yhigh_ref, up_ref, down_ref):
    for ref, first in ((up_ref, BX - 2), (down_ref, 0)):
        ref[:, :, :HALO] = yhigh_ref[:, first : first + 2]
        ref[:, :, HALO:] = ylow_ref[:, first : first + 2]


def minmod(p, q):
    return jnp.maximum(jnp.minimum(p, q), 0.0) + jnp.minimum(jnp.maximum(p, q), 0.0)


def half_flux(states, direction, sign):
    if len(states) == 2:
        return [0.5 * states[1] + sign * 2.0 * states[0]]
    density, energy = states[0], states[4]
    inverse = 1.0 / density
    velocity = 0.5 * states[1 + direction] * inverse
    squares = states[1] * states[1] + states[2] * states[2] + states[3] * states[3]
    pressure = 0.4 * energy - (0.2 * squares) * inverse
    pieces = [0.5 * states[1 + direction]]
    for component in range(3):
        term = states[1 + component] * velocity
        if component == direction:
            term = term + 0.5 * pressure
        pieces.append(term)
    pieces.append((energy + pressure) * velocity)
    if sign > 0:
        return [piece + 2.0 * state for piece, state in zip(pieces, states)]
    return [piece - 2.0 * state for piece, state in zip(pieces, states)]


def edge_terms(states, slopes, direction):
    halves = [0.5 * slope for slope in slopes]
    upper = half_flux([u + h for u, h in zip(states, halves)], direction, 1)
    lower = half_flux([u - h for u, h in zip(states, halves)], direction, -1)
    return upper, lower


def line_change(states, direction, axis):
    size = states[0].shape[axis]
    gaps = [pltpu.roll(u, size - 1, axis) - u for u in states]
    slopes = [minmod(pltpu.roll(g, 1, axis), g) for g in gaps]
    upper, lower = edge_terms(states, slopes, direction)
    faces = [u + pltpu.roll(w, size - 1, axis) for u, w in zip(upper, lower)]
    return [f - pltpu.roll(f, 1, axis) for f in faces]


def all_fields(states, direction):
    return states


def mass_fields(states, direction):
    return [states[0], states[1 + direction]]


def euler_stage(load, store, first_row, count, keep, unroll, pick=all_fields):
    def slopes_of(low, mid, high):
        return [minmod(b - a, c - b) for a, b, c in zip(low, mid, high)]

    cut = lambda states: [u[:keep] for u in states]
    cut_x = lambda states: cut(pick(states, 0))
    r0, r1, r2, r3 = [cut_x(load(first_row + k)) for k in (-2, -1, 0, 1)]
    upper_prev, _ = edge_terms(r1, slopes_of(r0, r1, r2), 0)
    upper_now, lower_now = edge_terms(r2, slopes_of(r1, r2, r3), 0)
    face = [u + w for u, w in zip(upper_prev, lower_now)]

    def step(k, carry):
        face_low, upper_here = carry
        i = first_row + k
        here, above, far = load(i), cut_x(load(i + 1)), cut_x(load(i + 2))
        mine = cut(here)
        upper_next, lower_next = edge_terms(above, slopes_of(pick(mine, 0), above, far), 0)
        face_high = [u + w for u, w in zip(upper_here, lower_next)]
        change = [h - l for h, l in zip(face_high, face_low)]
        along_y = cut(line_change(pick(here, 1), 1, 0))
        along_z = line_change(pick(mine, 2), 2, 1)
        rate = [-(a + b + c) for a, b, c in zip(change, along_y, along_z)]
        store(i, mine, rate)
        return tuple(face_high), tuple(upper_next)

    lax.fori_loop(0, count, step, (tuple(face), tuple(upper_now)), unroll=unroll)


def euler_kernel(
    own_ref, xlow_ref, xhigh_ref, ylow_ref, yhigh_ref, clow_ref, chigh_ref, table_ref,
    first_ref, modes_ref, ext_ref, flat_ref,
):
    low, high = slice(BY + HALO, BY + 2 * HALO), slice(BY, BY + HALO)
    inner = slice(HALO, HALO + BX)
    ext_ref[:, inner, 0:BY] = own_ref[...]
    ext_ref[:, 0:HALO, 0:BY] = xlow_ref[...]
    ext_ref[:, HALO + BX :, 0:BY] = xhigh_ref[...]
    ext_ref[:, inner, high] = yhigh_ref[...]
    ext_ref[:, inner, low] = ylow_ref[...]
    for start, ref in ((0, clow_ref), (HALO + BX, chigh_ref)):
        ext_ref[:, start : start + 2, BY:] = ref[...]
        ext_ref[:, start + 2 : start + 4, BY:] = ref[...]

    def load_ext(i):
        return [ext_ref[q, i] for q in range(5)]

    def store_first(i, states, rates):
        for q in range(5):
            first_ref[q, i - 2] = states[q] + time_step * rates[q]

    euler_stage(load_ext, store_first, 2, BX + 4, BY + 2 * HALO, 6)

    def load_mass(i):
        return [first_ref[q, i - 2] for q in range(4)]

    def store_density(i, states, rates):
        second = states[0] + time_step * rates[0]
        row = pl.multiple_of((i - HALO) * BY, BY)
        flat_ref[pl.ds(row, BY), :] = 0.5 * ext_ref[0, i, 0:BY] + 0.5 * second

    euler_stage(load_mass, store_density, HALO, BX, BY, 32, mass_fields)
    density = jnp.concatenate(
        [flat_ref[pl.ds(b, BX, stride=BY), :] for b in range(BY)], axis=0
    )
    spread = dot(table_ref[...], density, ((1,), (1,)))
    modes_ref[pl.ds(0, GZ, stride=2), :] = spread[:, :128]
    modes_ref[pl.ds(1, GZ, stride=2), :] = spread[:, 128:]


def second_kernel(own_ref, first_ref, stepped_ref):
    def load_first(i):
        return [first_ref[q, i - 2] for q in range(5)]

    def store_stepped(i, states, rates):
        for q in range(5):
            second = states[q] + time_step * rates[q]
            stepped_ref[q, i - HALO] = 0.5 * own_ref[q, i - HALO] + 0.5 * second

    euler_stage(load_first, store_stepped, HALO, BX, BY, 8)


def ends_kernel(modes_ref, table_ref, kappa_ref, expand_ref, pick_ref, raw_ref, ends_ref, plane_ref):
    for tile in range(2):
        lines = [modes_ref[pl.ds(k * 2 + tile, COLS, stride=8), :] for k in range(4)]
        for g, value in enumerate(swap_groups(lines, 32)):
            plane_ref[pl.ds(tile * 4 + g, COLS, stride=BY), :] = value
    power = jnp.exp(-dot(kappa_ref[...], expand_ref[:, :128], ((0,), (0,))))
    plane = plane_ref[...]
    mean = jnp.sum(plane, axis=0, keepdims=True) * (1.0 / GY)
    source = dot(table_ref[...], plane - mean, precision=lax.Precision.HIGH)
    head = lax.broadcasted_iota(jnp.int32, (8, 128), 0) == 0
    head = source[0:8] + jnp.where(head, math.sqrt(GY) * mean, 0.0)
    source = jnp.concatenate([head, source[8:]], axis=0)
    x = lax.broadcasted_iota(jnp.int32, (GY, 128), 1) % BX
    rising, falling = source, source
    step = 1
    while step < BX:
        rising = rising + jnp.where(x >= step, power * pltpu.roll(rising, step, 1), 0.0)
        falling = falling + jnp.where(x < BX - step, power * pltpu.roll(falling, 128 - step, 1), 0.0)
        power = power * power
        step *= 2
    ends = dot(pick_ref[...], jnp.concatenate([rising, falling], axis=1), ((1,), (1,)))
    for r in range(ROWS):
        ends_ref[r * 24 : r * 24 + 8, :] = ends[:, :128]
        ends_ref[r * 24 + 8 : r * 24 + 16, :] = ends[:, 128:]
        ends_ref[r * 24 + 16 : r * 24 + 24, :] = source[0:8]
    raw_ref[:, :128] = rising + falling - source
    raw_ref[:, 128:] = jnp.where(x == 0, falling, pltpu.roll(rising, 128 - BX + 2, 1))


def weigh_kernel(kappa_ref, expand_ref, span_ref, raw_ref, local_ref, left_ref, right_ref):
    kappa = dot(kappa_ref[...], expand_ref[:, :128], ((0,), (0,)))
    flat = kappa <= 0.0
    decay = jnp.exp(-kappa)
    width = jnp.where(flat, 1.0, jnp.exp(kappa) - decay)
    scale = jnp.where(flat, 0.0, -four_pi_g / width)
    images = scale / jnp.where(flat, 1.0, 1.0 - jnp.exp(-GX * kappa))
    for half in range(2):
        lanes = slice(half * 128, half * 128 + 128)
        span = span_ref[:, lanes]
        local_ref[:, lanes] = (scale * decay if half else scale) * raw_ref[:, lanes]
        left_ref[:, lanes] = images * jnp.exp(-kappa * (span + 1.0))
        right_ref[:, lanes] = images * jnp.exp(-kappa * (BX - span))


def join_kernel(
    place_ref, ends_ref, local_ref, left_ref, right_ref, kappa_ref, expand_ref, table_ref,
    out_ref, wide_ref,
):
    row = place_ref[0]

    def slab(step):
        return pl.multiple_of(((row + step) & (ROWS - 1)) * 24, 8)

    rising = lax.broadcasted_iota(jnp.int32, (8, GY), 0) % 2 == 0
    block = jnp.exp(-BX * kappa_ref[...])
    total = None
    for d in range(ROWS, 0, -1):
        below, above = slab(ROWS - d), slab(d)
        both = []
        for part in (0, 8):
            both.append((ends_ref[pl.ds(below + part, 8), :], ends_ref[pl.ds(above + part, 8), :]))
        low = jnp.concatenate([both[0][0], both[1][0]], axis=1)
        high = jnp.concatenate([both[0][1], both[1][1]], axis=1)
        value = jnp.where(rising, low, high)
        total = value if total is None else value + block * total
    end = lax.broadcasted_iota(jnp.int32, (8, 256), 0) % 2
    side = lax.broadcasted_iota(jnp.int32, (8, 256), 1) // 128
    spread = jnp.where(end == side, 2.0 * expand_ref[...], 0.0)
    incoming = dot(total, spread, ((0,), (0,)))
    halves = []
    for lanes in (slice(0, 128), slice(128, 256)):
        moved = left_ref[:, lanes] * incoming[:, :128] + right_ref[:, lanes] * incoming[:, 128:]
        halves.append(local_ref[:, lanes] + moved)
    field = jnp.concatenate(halves, axis=1)
    lane = lax.broadcasted_iota(jnp.int32, (8, 128), 1)
    halves = []
    for half in range(2):
        line = jnp.zeros((8, 128), jnp.float32)
        for g in range(4):
            values = ends_ref[pl.ds(slab(ROWS - half * 4 - g) + 16, 8), :]
            values = jnp.where(lane < BX, values, 0.0)
            line = line + (pltpu.roll(values, g * BX, 1) if g else values)
        halves.append(line)
    line = jnp.concatenate(halves, axis=1)
    line = line - jnp.sum(line, axis=1, keepdims=True) * (1.0 / GX)
    source = lax.broadcasted_iota(jnp.int32, (GX, 128), 0)
    target = lax.broadcasted_iota(jnp.int32, (GX, 128), 1)
    target = jnp.where(target == BX + 1, -1, target)
    gap = jnp.abs(source // BX * BX + target - source % BX).astype(jnp.float32)
    shape = four_pi_g * (gap * (0.5 - gap * (0.5 / GX)) - (GX * GX - 1.0) / (12.0 * GX))
    mean = dot(line, shape)
    first = lax.broadcasted_iota(jnp.int32, (8, 128), 0) == 0
    mean = jnp.where(jnp.logical_and(first, place_ref[1] == 0), mean, 0.0)
    inner = jnp.where(lane < BX, mean, 0.0)
    low, high = pltpu.roll(mean, 128 - BX - 1, 1), pltpu.roll(mean, 128 - BX + 1, 1)
    outer = jnp.where(lane == 0, low, jnp.where(lane == 1, high, 0.0))
    mean = jnp.concatenate([inner, outer], axis=1)
    field = jnp.concatenate([field[0:8] + mean, field[8:]], axis=0)
    potential = dot(table_ref[...], field, precision=lax.Precision.HIGH)
    for part in range(2):
        base, side = part * (GY + 16), potential[:, part * 128 : part * 128 + 128]
        wide_ref[base + 8 : base + 8 + GY, :] = side
        wide_ref[base : base + 8, :] = side[GY - 8 :]
        wide_ref[base + 8 + GY : base + 16 + GY, :] = side[:8]
    strips = [wide_ref[pl.ds(8 + yl, COLS, stride=BY), :] for yl in range(BY)]
    below = wide_ref[pl.ds(7, COLS, stride=BY), :]
    above = wide_ref[pl.ds(16, COLS, stride=BY), :]
    x = lax.broadcasted_iota(jnp.int32, (COLS, 128), 1) % BX
    sides = jnp.zeros((COLS, 128), jnp.float32)
    for yl in range(BY):
        edge = wide_ref[pl.ds(GY + 16 + 8 + yl, COLS, stride=BY), :]
        sides = jnp.where(x == yl, pltpu.roll(edge, yl, 1) if yl else edge, sides)
        sides = jnp.where(x == BY + yl, pltpu.roll(edge, BY - 1 + yl, 1), sides)
    strips = strips + [below, above, sides, sides]
    for quad in range(3):
        for k, value in enumerate(swap_groups(strips[quad * 4 : quad * 4 + 4], 32)):
            out_ref[pl.ds(k * 3 + quad, COLS, stride=12), :] = value


def kick_kernel(owner_ref, stepped_ref, modes_ref, table_ref, out_ref, phi_ref, kicked_ref):
    table = table_ref[...]
    parts = []
    for quad in range(3):
        block = modes_ref[pl.ds(quad, GZ, stride=3), :]
        parts.append(dot(block, table, ((0,), (0,))))
    for yl in range(BY):
        phi_ref[pl.ds(BY + yl, BX, stride=BY), :] = parts[yl // 4][(yl % 4) * 32 : (yl % 4) * 32 + 32]
    phi_ref[0:BY, :] = parts[2][64 : 64 + BY]
    phi_ref[BY + BX * BY :, :] = parts[2][64 + BY : 64 + 2 * BY]
    phi = phi_ref[...].reshape(BX + 2, BY, GZ)
    mid = phi[1 : 1 + BX]
    below = parts[2][0:32].reshape(BX, 1, GZ)
    above = parts[2][32:64].reshape(BX, 1, GZ)
    grad_x = 0.5 * (phi[2:] - phi[:BX])
    lower = jnp.concatenate([below, mid[:, : BY - 1]], axis=1)
    upper = jnp.concatenate([mid[:, 1:], above], axis=1)
    grad_y = 0.5 * (upper - lower)
    grad_z = 0.5 * (pltpu.roll(mid, GZ - 1, 2) - pltpu.roll(mid, 1, 2))
    grads = (grad_x, grad_y, grad_z)
    density = stepped_ref[0]
    momenta = [stepped_ref[1 + d] for d in range(3)]
    work = momenta[0] * grad_x + momenta[1] * grad_y + momenta[2] * grad_z
    cells = BX * BY
    kicked_ref[0:cells, :] = density.reshape(cells, GZ)
    for d in range(3):
        value = momenta[d] - time_step * density * grads[d]
        kicked_ref[(1 + d) * cells : (2 + d) * cells, :] = value.reshape(cells, GZ)
    kicked_ref[4 * cells :, :] = (stepped_ref[4] - time_step * work).reshape(cells, GZ)
    for q in range(5):
        for xl in range(2):
            for part in range(2):
                base = (q * BX + xl * PE + part * 8) * BY
                lines = [kicked_ref[pl.ds(base + b, 8, stride=BY), :] for b in range(BY)]
                rows = q * PE + part * 8
                for zl, value in enumerate(swap_groups(lines, PE)):
                    out_ref[owner_ref[xl * 8 + zl], rows : rows + 8, :] = value


def spread_kernel(place_ref, recv_ref, out_ref):
    shift = place_ref[0]
    live = lax.broadcasted_iota(jnp.int32, (CAP, 128), 0) < place_ref[1]
    for q in range(5):
        for tile in range(2 * PE):
            a, half = tile // 2, tile % 2
            lines = recv_ref[pl.ds(half * BRICK + q * PE + a, CAP, stride=2 * BRICK), :]
            turned = pltpu.roll(lines, shift, 0)
            out_ref[q, :, tile * 128 : (tile + 1) * 128] = jnp.where(live, turned, 0.0)


def call(kernel, outs, ins, scratch=()):
    shapes = [jax.ShapeDtypeStruct(s, jnp.float32) for s in outs]
    many = len(outs) > 1
    return pl.pallas_call(
        kernel,
        out_shape=tuple(shapes) if many else shapes[0],
        in_specs=[SM if i in ins[1] else VM for i in range(ins[0])],
        out_specs=tuple([VM] * len(outs)) if many else VM,
        scratch_shapes=[pltpu.VMEM(s, jnp.float32) for s in scratch],
        compiler_params=PARAMS,
    )


def gather_counts(counts):
    copies = jnp.broadcast_to(counts.astype(jnp.float32).reshape(1, 1, 1), (COLS, 1, 128))
    return lax.all_to_all(copies, "col", split_axis=0, concat_axis=0, tiled=True)


def on_device(fields, counts):
    my_row = lax.axis_index("row")
    my_column = lax.axis_index("col")
    staged = call(stage_kernel, [(COLS * BRICK, 128)], (1, ()))(fields.transpose(1, 0, 2))
    spread_counts = gather_counts(counts)
    row_counts = spread_counts[:, 0, 0].astype(jnp.int32)
    column_ids = jnp.arange(COLS, dtype=jnp.int32)
    starts = jnp.sum(
        jnp.where(column_ids[None, :] < column_ids[:, None], row_counts[None, :], 0), axis=1
    )
    own_start = jnp.sum(jnp.where(column_ids < my_column, row_counts, 0))
    y_patch = my_column // 2
    wanted = jnp.arange(LINES, dtype=jnp.int32) * 16 + y_patch
    owners = jnp.sum((starts[None, :] <= wanted[:, None]).astype(jnp.int32), axis=1) - 1
    turn = own_start % CAP

    sent = call(turn_kernel, [(COLS * BRICK, 128)], (3, (0,)))(
        my_column.reshape(1), spread_counts, staged
    )
    arrived = lax.all_to_all(
        sent.reshape(COLS, BRICK, 128), "col", split_axis=0, concat_axis=0, tiled=True
    )
    own, xfirst, xlast, yfirst, ylast = call(
        unpack_kernel,
        [
            (5 * BX * BY, GZ),
            (5, HALO, BY, GZ),
            (5, HALO, BY, GZ),
            (5, BX, HALO, GZ),
            (5, BX, HALO, GZ),
        ],
        (2, (0,)),
    )(owners, arrived)
    own = own.reshape(5, BX, BY, GZ)

    def ring(count, step):
        return [(i, (i + step) % count) for i in range(count)]

    xlow = lax.ppermute(xlast, "row", ring(ROWS, 1))
    xhigh = lax.ppermute(xfirst, "row", ring(ROWS, -1))
    ylow = lax.ppermute(ylast, "col", ring(COLS, 1))
    yhigh = lax.ppermute(yfirst, "col", ring(COLS, -1))
    up, down = call(corner_kernel, [(5, 2, BY, GZ)] * 2, (2, ()))(ylow, yhigh)
    clow = lax.ppermute(up, "row", ring(ROWS, 1))
    chigh = lax.ppermute(down, "row", ring(ROWS, -1))

    table_z = hartley(GZ)
    table_x = hartley(GX)
    wide = (5, BX + 2 * HALO, BY + 2 * HALO, GZ)
    first, modes = call(
        euler_kernel, [(5, BX + HALO, BY + 2 * HALO, GZ), (256, 128)], (8, ()), [wide, (BX * BY, GZ)]
    )(own, xlow, xhigh, ylow, yhigh, clow, chigh, jnp.asarray(table_z))
    planes = lax.all_to_all(
        modes.reshape(COLS, 8, 128), "col", split_axis=0, concat_axis=0, tiled=True
    )
    kappa = jnp.asarray(np.repeat(kappas(), 2, axis=0).astype(np.float32))
    kappa = lax.dynamic_slice_in_dim(kappa, my_column * 8, 8, axis=0)
    expand = jnp.asarray(lane_expand())
    square = (GY, 256)
    stepped = call(second_kernel, [(5, BX, BY, GZ)], (2, ()))(own, first)
    planes, stepped, kappa = lax.optimization_barrier((planes, stepped, kappa))
    raw, ends = call(ends_kernel, [square, (ROWS * 24, 128)], (5, ()), [(GY, 128)])(
        planes.reshape(256, 128), jnp.asarray(table_x), kappa, expand, jnp.asarray(lane_picks())
    )
    local, left, right = call(weigh_kernel, [square] * 3, (4, ()))(
        kappa, expand, jnp.asarray(lane_spans()[None, :]), raw
    )
    ends = lax.all_to_all(
        ends.reshape(ROWS, 24, 128), "row", split_axis=0, concat_axis=0, tiled=True
    )
    strips = call(join_kernel, [(COLS * 12, 128)], (8, (0,)), [(2 * (GY + 16), 128)])(
        jnp.stack([my_row, my_column]),
        ends.reshape(ROWS * 24, 128),
        local,
        left,
        right,
        kappa,
        expand,
        jnp.asarray(table_x),
    )
    strips = lax.all_to_all(
        strips.reshape(COLS, 1, 1536), "col", split_axis=0, concat_axis=0, tiled=True
    )
    returned = call(
        kick_kernel,
        [(COLS, BRICK, 128)],
        (4, (0,)),
        [((BX + 2) * BY, GZ), (5 * BX * BY, GZ)],
    )(owners, stepped, strips.reshape(COLS * 12, 128), jnp.asarray(table_z))
    came_back = lax.all_to_all(returned, "col", split_axis=0, concat_axis=0, tiled=True)
    home = jnp.stack([(CAP - turn) % CAP, counts[0, 0]])
    result = call(spread_kernel, [(5, CAP, PE * PE * PE)], (2, (0,)))(
        home, came_back.reshape(COLS * BRICK, 128)
    )
    return result.transpose(1, 0, 2)


def solution(mesh):
    return jax.shard_map(
        on_device,
        mesh=mesh,
        in_specs=(P(("row", "col"), None, None), P("row", "col")),
        out_specs=P(("row", "col"), None, None),
        check_vma=False,
    )
```
